32 devices in a mesh: wide: 8 (over z, y), narrow: 4 (over x, core).
Axes of the slice: x: 2, y: 2, z: 4, core: 2. Of those that a mesh axis runs over, the one named last changes fastest.
Arguments:
- tokens: bfloat16 [8, 1024, 2048], P('wide', 'narrow'), may hold values from -6 to 6
- cotangent: bfloat16 [8, 1024, 2048], P('wide', 'narrow'), may hold values from -6 to 6
- lengths: int32 [8], P('wide'), may hold values from 256 to 1024, as said below
- norm_gains: float32 [4352], replicated, may hold values from 0.6 to 1.6
- gains_first: float32 [4352], replicated
- gains_second: float32 [4352], replicated, as said below
- query_weight: float32 [2048, 2048], P('wide', 'narrow'), may hold values from -0.125 to 0.125
- query_first: float32 [2048, 2048], P('wide', 'narrow')
- query_second: float32 [2048, 2048], P('wide', 'narrow'), as said below
- keyval_weight: float32 [2, 2048, 1024], P(None, 'wide', 'narrow'), may hold values from -0.125 to 0.125
- keyval_first: float32 [2, 2048, 1024], P(None, 'wide', 'narrow')
- keyval_second: float32 [2, 2048, 1024], P(None, 'wide', 'narrow'), as said below
- output_weight: float32 [2048, 2048], P('narrow', 'wide'), may hold values from -0.5 to 0.5
- output_first: float32 [2048, 2048], P('narrow', 'wide')
- output_second: float32 [2048, 2048], P('narrow', 'wide'), as said below
- gateup_weight: float32 [2, 2048, 6144], P(None, 'wide', 'narrow'), may hold values from -0.125 to 0.125
- gateup_first: float32 [2, 2048, 6144], P(None, 'wide', 'narrow')
- gateup_second: float32 [2, 2048, 6144], P(None, 'wide', 'narrow'), as said below
- down_weight: float32 [6144, 2048], P('narrow', 'wide'), may hold values from -0.078125 to 0.078125
- down_first: float32 [6144, 2048], P('narrow', 'wide')
- down_second: float32 [6144, 2048], P('narrow', 'wide'), as said below
Outputs:
- result: bfloat16 [8, 1024, 2048], P('wide', 'narrow')
- input_grad: bfloat16 [8, 1024, 2048], P('wide', 'narrow')
- rms_values: float32 [3, 8, 1024], P(None, 'wide', 'narrow')
- new_gains: float32 [4352], replicated
- new_gains_first: float32 [4352], replicated
- new_gains_second: float32 [4352], replicated
- new_query: float32 [2048, 2048], P('wide', 'narrow')
- new_query_first: float32 [2048, 2048], P('wide', 'narrow')
- new_query_second: float32 [2048, 2048], P('wide', 'narrow')
- new_keyval: float32 [2, 2048, 1024], P(None, 'wide', 'narrow')
- new_keyval_first: float32 [2, 2048, 1024], P(None, 'wide', 'narrow')
- new_keyval_second: float32 [2, 2048, 1024], P(None, 'wide', 'narrow')
- new_output: float32 [2048, 2048], P('narrow', 'wide')
- new_output_first: float32 [2048, 2048], P('narrow', 'wide')
- new_output_second: float32 [2048, 2048], P('narrow', 'wide')
- new_gateup: float32 [2, 2048, 6144], P(None, 'wide', 'narrow')
- new_gateup_first: float32 [2, 2048, 6144], P(None, 'wide', 'narrow')
- new_gateup_second: float32 [2, 2048, 6144], P(None, 'wide', 'narrow')
- new_down: float32 [6144, 2048], P('narrow', 'wide')
- new_down_first: float32 [6144, 2048], P('narrow', 'wide')
- new_down_second: float32 [6144, 2048], P('narrow', 'wide')
- lamb_stats: float32 [2, 11], replicated
- trust_ratios: float32 [11], replicated
The draws below stay inside these ranges and needn't reach their ends.
Inputs may be any that keep to these rules, and one draw needn't show every extreme that they name: `lengths`: some sequence has all 1024 positions valid and some exactly 256. `gains_second`: positive. `query_second`: positive. `keyval_second`: positive. `output_second`: positive. `gateup_second`: positive. `down_second`: positive.
All inputs are finite; a program needn't handle non-finite values.
Results may differ from the reference program's by a relative error of at most 0.024.
Values may be sent and summed in bfloat16 or wider, within the bound.
No kernel may reach another device: no remote copies, remote signals or barrier semaphores. Data moves between devices by JAX's collectives and lax.ppermute only.
A program may use at most 192 MiB of HBM per device.

```python
import math
import jax
import jax.numpy as jnp
from jax import lax

D = 2048
H = 16
KV = 8
HD = 128
FF = 6144
SEQ = 1024
STEP = 10
SEQS = 8


def token_root():
    return (0.625 * SEQS * SEQ) ** 0.5


def first_moment(key, scales):
    return 0.111 * scales * jax.random.normal(key, scales.shape, jnp.float32)


def second_moment(key, scales):
    factor = jnp.exp(jax.random.uniform(key, scales.shape, jnp.float32, math.log(0.5), math.log(8.0)))
    return 0.001 * scales * scales * factor


def gain_scales():
    return jnp.concatenate([jnp.full((2 * D,), token_root(), jnp.float32), jnp.full((2 * HD,), token_root() * H ** 0.5, jnp.float32)])


def draw_lengths(key, part):
    key_base, key_first, key_other = jax.random.split(key, 3)
    base = jax.random.randint(key_base, (SEQS,), SEQ // 4, SEQ + 1)
    first_index = jax.random.randint(key_first, (), 0, SEQS)
    other_index = (first_index + 1 + jax.random.randint(key_other, (), 0, SEQS - 1)) % SEQS
    return base.at[first_index].set(SEQ).at[other_index].set(SEQ // 4).astype(jnp.int32)


def draw_norm_gains(key, part):
    key_norm, key_head = jax.random.split(key)
    outer = jnp.clip(1.0 + 0.1 * jax.random.normal(key_norm, (2 * D,), jnp.float32), 0.6, 1.4)
    inner = jax.random.uniform(key_head, (2 * HD,), jnp.float32, 1.0, 1.6)
    return jnp.concatenate([outer, inner])


def draw_gains_first(key, part):
    return first_moment(key, gain_scales())


def draw_gains_second(key, part):
    return second_moment(key, gain_scales())


def draw_query_first(key, part):
    return first_moment(key, jnp.full((D, H * HD), token_root(), jnp.float32))


def draw_query_second(key, part):
    return second_moment(key, jnp.full((D, H * HD), token_root(), jnp.float32))


def draw_keyval_first(key, part):
    return first_moment(key, jnp.full((2, D, KV * HD), token_root(), jnp.float32))


def draw_keyval_second(key, part):
    return second_moment(key, jnp.full((2, D, KV * HD), token_root(), jnp.float32))


def draw_output_first(key, part):
    return first_moment(key, jnp.full((H * HD, D), 0.25 * token_root(), jnp.float32))


def draw_output_second(key, part):
    return second_moment(key, jnp.full((H * HD, D), 0.25 * token_root(), jnp.float32))


def draw_gateup_first(key, part):
    return first_moment(key, jnp.full((2, D, FF), 0.3 * token_root(), jnp.float32))


def draw_gateup_second(key, part):
    return second_moment(key, jnp.full((2, D, FF), 0.3 * token_root(), jnp.float32))


def draw_down_first(key, part):
    return first_moment(key, jnp.full((FF, D), 0.6 * token_root(), jnp.float32))


def draw_down_second(key, part):
    return second_moment(key, jnp.full((FF, D), 0.6 * token_root(), jnp.float32))


def shard_levels(own_key, dims, pieces, low, high):
    gain = 1.0
    for dim, shards_of in pieces:
        heights = jax.random.uniform(jax.random.fold_in(jax.random.fold_in(own_key, 6), dim), (shards_of,), jnp.float32, low / len(pieces), high / len(pieces))
        gain = gain * jnp.repeat(jnp.exp(heights), dims[dim] // shards_of).reshape((-1,) + (1,) * (len(dims) - 1 - dim))
    return gain


def bell_draw(own_key, shape, scale, most, cuts=(), kind=jnp.bfloat16):
    loudness = shard_levels(own_key, shape, cuts, -0.22, 0.18) if cuts else 1.0
    values = jax.random.normal(own_key, shape, jnp.float32) * scale * loudness
    return jnp.minimum(jnp.maximum(values, -most), most).astype(kind)


def setup_inputs(seed: int = 0) -> dict:
    key_of = jax.random.split(jax.random.key(seed), 22)
    return {
        "tokens": bell_draw(key_of[0], (SEQS, SEQ, D), 1.0, 6.0, ((0, 8), (1, 4))),
        "cotangent": bell_draw(key_of[1], (SEQS, SEQ, D), 1.0, 6.0, ((0, 8), (1, 4))),
        "lengths": draw_lengths(jax.random.fold_in(key_of[21], 71), 0),
        "norm_gains": draw_norm_gains(jax.random.fold_in(key_of[21], 71), 0),
        "gains_first": draw_gains_first(jax.random.fold_in(key_of[21], 71), 0),
        "gains_second": draw_gains_second(jax.random.fold_in(key_of[21], 71), 0),
        "query_weight": bell_draw(key_of[6], (D, H * HD), D ** -0.5, 0.125, ((0, 8), (1, 4)), jnp.float32),
        "query_first": draw_query_first(jax.random.fold_in(key_of[21], 71), 0),
        "query_second": draw_query_second(jax.random.fold_in(key_of[21], 71), 0),
        "keyval_weight": bell_draw(key_of[9], (2, D, KV * HD), D ** -0.5, 0.125, ((1, 8), (2, 4)), jnp.float32),
        "keyval_first": draw_keyval_first(jax.random.fold_in(key_of[21], 71), 0),
        "keyval_second": draw_keyval_second(jax.random.fold_in(key_of[21], 71), 0),
        "output_weight": bell_draw(key_of[12], (H * HD, D), (H * HD // 16) ** -0.5, 0.5, ((0, 4), (1, 8)), jnp.float32),
        "output_first": draw_output_first(jax.random.fold_in(key_of[21], 71), 0),
        "output_second": draw_output_second(jax.random.fold_in(key_of[21], 71), 0),
        "gateup_weight": bell_draw(key_of[15], (2, D, FF), D ** -0.5, 0.125, ((1, 8), (2, 4)), jnp.float32),
        "gateup_first": draw_gateup_first(jax.random.fold_in(key_of[21], 71), 0),
        "gateup_second": draw_gateup_second(jax.random.fold_in(key_of[21], 71), 0),
        "down_weight": bell_draw(key_of[18], (FF, D), FF ** -0.5, 0.078125, ((0, 4), (1, 8)), jnp.float32),
        "down_first": draw_down_first(jax.random.fold_in(key_of[21], 71), 0),
        "down_second": draw_down_second(jax.random.fold_in(key_of[21], 71), 0),
    }


EPS = 1e-06
THETA = 1000000.0
BETA_ONE = 0.9
BETA_TWO = 0.999
ADAM_EPS = 1e-06
DECAY = 0.01
LEARN = 0.5

@jax.custom_vjp
def low(v):
    return lax.optimization_barrier(v.astype(jnp.bfloat16)).astype(jnp.float32)

@jax.custom_vjp
def low_back(v):
    return v

def low_keep(v):
    return (low(v), None)

def low_pass(kept, grad):
    return (grad,)

def back_keep(v):
    return (v, None)

def back_low(kept, grad):
    return (low(grad),)
low.defvjp(low_keep, low_pass)
low_back.defvjp(back_keep, back_low)

def product(form, left, right):
    return jnp.einsum(form, left, right, precision=lax.Precision.HIGHEST)

def rope_tables():
    places = jnp.arange(SEQ, dtype=jnp.float32)
    frequency = THETA ** (-jnp.arange(HD // 2, dtype=jnp.float32) * 2.0 / HD)
    angles = places[:, None] * frequency[None, :]
    return (jnp.cos(angles)[:, None, :], jnp.sin(angles)[:, None, :])

def rotate(values, cos_table, sin_table):
    halfway = HD // 2
    former = values[..., :halfway]
    latter = values[..., halfway:]
    return jnp.concatenate([former * cos_table - latter * sin_table, latter * cos_table + former * sin_table], -1)

def head_scale(raw_values, gain_vector, head_count):
    shaped = raw_values.reshape(raw_values.shape[:-1] + (head_count, HD))
    inverse = lax.rsqrt(lax.optimization_barrier(jnp.mean(shaped * shaped, -1, keepdims=True)) + EPS)
    return shaped * inverse * gain_vector

def attend(queries, keys, values, limits):
    group_size = queries.shape[0]
    repeat = H // KV
    block_rows = min(512, SEQ)
    block_count = SEQ // block_rows
    score_scale = HD ** (-0.5)
    shaped = queries.reshape(group_size, block_count, block_rows, KV, repeat, HD).transpose(1, 0, 2, 3, 4, 5)
    starts = jnp.arange(block_count, dtype=jnp.int32) * block_rows
    key_places = jnp.arange(SEQ, dtype=jnp.int32)

    def one_block(slices):
        query_block, start = slices
        scores = low_back(product('gqkrd,gskd->gkrqs', query_block, keys) * score_scale)
        query_places = start + jnp.arange(block_rows, dtype=jnp.int32)
        allowed = (key_places[None, None, :] <= query_places[None, :, None]) & (key_places[None, None, :] < limits[:, None, None])
        scores = jnp.where(allowed[:, None, None, :, :], scores, -1e+30)
        row_max = lax.optimization_barrier(jnp.max(scores, -1, keepdims=True))
        weights = jnp.exp(scores - row_max)
        probability = weights / lax.optimization_barrier(jnp.sum(weights, -1, keepdims=True))
        context = product('gkrqs,gskd->gqkrd', low(probability), values)
        return context.reshape(group_size, block_rows, H * HD)
    blocks = lax.map(jax.checkpoint(one_block), (shaped, starts))
    return blocks.transpose(1, 0, 2, 3).reshape(group_size, SEQ, H * HD)

def layer(params, inputs, limits):
    gain_all, w_query, w_keyval, w_output, w_gateup, w_down = params
    group_size = inputs.shape[0]
    cos_table, sin_table = rope_tables()
    inv_one = lax.rsqrt(lax.optimization_barrier(jnp.mean(inputs * inputs, -1, keepdims=True)) + EPS)
    normed_one = low(inputs * inv_one * gain_all[:D])
    query_raw = low_back(product('gsd,dc->gsc', normed_one, low(w_query)))
    key_raw = low_back(product('gsd,dc->gsc', normed_one, low(w_keyval[0])))
    value_low = low(low_back(product('gsd,dc->gsc', normed_one, low(w_keyval[1]))))
    query_rot = low(rotate(head_scale(query_raw, gain_all[2 * D:2 * D + HD], H), cos_table, sin_table))
    key_rot = low(rotate(head_scale(key_raw, gain_all[2 * D + HD:], KV), cos_table, sin_table))
    values = value_low.reshape(group_size, SEQ, KV, HD)
    context = low(low_back(attend(query_rot, key_rot, values, limits)))
    attn = low_back(product('gsc,cd->gsd', context, low(w_output)))
    middle = inputs + attn
    inv_two = lax.rsqrt(lax.optimization_barrier(jnp.mean(middle * middle, -1, keepdims=True)) + EPS)
    normed_two = low(middle * inv_two * gain_all[D:2 * D])
    gate_val = low_back(product('gsd,df->gsf', normed_two, low(w_gateup[0])))
    up_val = low_back(product('gsd,df->gsf', normed_two, low(w_gateup[1])))
    hidden = low(jax.nn.silu(gate_val) * up_val)
    mlp = low_back(product('gsf,fd->gsd', hidden, low(w_down)))
    return (middle + mlp, (attn, mlp))

def adam_step(gradient, moment_one, moment_two, master):
    new_one = BETA_ONE * moment_one + (1.0 - BETA_ONE) * gradient
    new_two = BETA_TWO * moment_two + (1.0 - BETA_TWO) * gradient * gradient
    update = new_one / (1.0 - BETA_ONE ** STEP) / (jnp.sqrt(new_two / (1.0 - BETA_TWO ** STEP)) + ADAM_EPS) + DECAY * master
    return (new_one, new_two, update)

def norm_of(values):
    return jnp.sqrt(jnp.sum(values * values))

def root_mean(values):
    return jnp.sqrt(lax.optimization_barrier(jnp.mean(values * values, -1)))

def reference(tokens, cotangent, lengths, norm_gains, gains_first, gains_second, query_weight, query_first, query_second, keyval_weight, keyval_first, keyval_second, output_weight, output_first, output_second, gateup_weight, gateup_first, gateup_second, down_weight, down_first, down_second):
    params = (norm_gains, query_weight, keyval_weight, output_weight, gateup_weight, down_weight)
    group_size = math.gcd(SEQS, max(1, 4096 // SEQ))
    rounds = SEQS // group_size
    places = jnp.arange(SEQ, dtype=jnp.int32)
    valid = (places[None, :] < lengths[:, None]).astype(jnp.float32)
    inputs = tokens.astype(jnp.float32).reshape(rounds, group_size, SEQ, D)
    pulled = (cotangent.astype(jnp.float32) * valid[:, :, None]).reshape(rounds, group_size, SEQ, D)
    limits = lengths.reshape(rounds, group_size)
    zero_grads = jax.tree.map(jnp.zeros_like, params)

    def one_round(running, slices):
        input_part, grad_part, limit_part = slices

        def forward(weights, values):
            return layer(weights, values, limit_part)
        output, pullback, branches = jax.vjp(forward, params, input_part, has_aux=True)
        weight_grads, input_part_grad = pullback(grad_part)
        running = jax.tree.map(jnp.add, running, weight_grads)
        return (running, (output, input_part_grad, branches[0], branches[1]))
    total_grads, (outputs, input_grads, attn_all, mlp_all) = lax.scan(one_round, zero_grads, (inputs, pulled, limits))
    final = outputs.reshape(SEQS, SEQ, D)
    result = final.astype(jnp.bfloat16)
    input_grad = input_grads.reshape(SEQS, SEQ, D).astype(jnp.bfloat16)
    rms_values = jnp.stack([root_mean(attn_all.reshape(SEQS, SEQ, D)), root_mean(mlp_all.reshape(SEQS, SEQ, D)), root_mean(final)])
    gain_grad, query_grad, keyval_grad, output_grad, gateup_grad, down_grad = total_grads
    new_gains_first, new_gains_second, gains_update = adam_step(gain_grad, gains_first, gains_second, norm_gains)
    new_query_first, new_query_second, query_update = adam_step(query_grad, query_first, query_second, query_weight)
    new_keyval_first, new_keyval_second, keyval_update = adam_step(keyval_grad, keyval_first, keyval_second, keyval_weight)
    new_output_first, new_output_second, output_update = adam_step(output_grad, output_first, output_second, output_weight)
    new_gateup_first, new_gateup_second, gateup_update = adam_step(gateup_grad, gateup_first, gateup_second, gateup_weight)
    new_down_first, new_down_second, down_update = adam_step(down_grad, down_first, down_second, down_weight)
    pairs = [(norm_gains[:D], gains_update[:D]), (query_weight, query_update), (keyval_weight[0], keyval_update[0]), (keyval_weight[1], keyval_update[1]), (norm_gains[2 * D:2 * D + HD], gains_update[2 * D:2 * D + HD]), (norm_gains[2 * D + HD:], gains_update[2 * D + HD:]), (output_weight, output_update), (norm_gains[D:2 * D], gains_update[D:2 * D]), (gateup_weight[0], gateup_update[0]), (gateup_weight[1], gateup_update[1]), (down_weight, down_update)]
    weight_norms = jnp.stack([norm_of(pair[0]) for pair in pairs])
    update_norms = jnp.stack([norm_of(pair[1]) for pair in pairs])
    trust = weight_norms / update_norms
    gain_trust = jnp.concatenate([jnp.full((D,), 1.0, jnp.float32) * trust[0], jnp.full((D,), 1.0, jnp.float32) * trust[7], jnp.full((HD,), 1.0, jnp.float32) * trust[4], jnp.full((HD,), 1.0, jnp.float32) * trust[5]])
    new_gains = norm_gains - LEARN * gain_trust * gains_update
    new_query = query_weight - LEARN * trust[1] * query_update
    new_keyval = keyval_weight - LEARN * jnp.stack([trust[2], trust[3]])[:, None, None] * keyval_update
    new_output = output_weight - LEARN * trust[6] * output_update
    new_gateup = gateup_weight - LEARN * jnp.stack([trust[8], trust[9]])[:, None, None] * gateup_update
    new_down = down_weight - LEARN * trust[10] * down_update
    lamb_stats = jnp.stack([weight_norms, update_norms])
    return (result, input_grad, rms_values, new_gains, new_gains_first, new_gains_second, new_query, new_query_first, new_query_second, new_keyval, new_keyval_first, new_keyval_second, new_output, new_output_first, new_output_second, new_gateup, new_gateup_first, new_gateup_second, new_down, new_down_first, new_down_second, lamb_stats, trust)
```

```python
import functools

import jax
import jax.numpy as jnp
from jax import lax
from jax.experimental import pallas as pl
from jax.experimental.pallas import tpu as pltpu
from jax.sharding import PartitionSpec as P

D = 2048
H = 16
KV = 8
HD = 128
STEP = 10


EPS = 1e-06
THETA = 1000000.0
BETA_ONE = 0.9
BETA_TWO = 0.999
ADAM_EPS = 1e-06
DECAY = 0.01
LEARN = 0.5

SCALE = HD ** (-0.5)

CHIP = ("narrow", 2)
CORE = ("narrow", 1)
PAIR = ("inner", 1)


def swap(values, link):
    axis, bit = link
    return lax.ppermute(values, axis, [(i, i ^ bit) for i in range(lax.axis_size(axis))])


def gather_rows(own):
    half = own.shape[0] // 2
    chip = swap(own, CHIP)
    pair = swap(own, PAIR)
    cross = [swap(chip[:half], PAIR), swap(pair[half:], CHIP)]
    near = [own, chip, pair, *cross]
    return jnp.concatenate(near + [swap(block, CORE) for block in near], 0)


def scatter_rows(near, far_low):
    rows = near.shape[0] // 4
    half = rows // 2
    part = (near + swap(far_low, CORE).astype(jnp.float32)).astype(jnp.bfloat16)
    own, chip, pair, cross = (part[i * rows : (i + 1) * rows] for i in range(4))
    from_pair = swap(cross[:half], PAIR)
    from_chip = swap(cross[half:], CHIP)
    chip_late = swap(chip[half:], CHIP)
    pair_early = swap(pair[:half], PAIR)
    wide = jnp.float32
    chip_early = swap((chip[:half].astype(wide) + from_pair.astype(wide)).astype(jnp.bfloat16), CHIP)
    pair_late = swap((pair[half:].astype(wide) + from_chip.astype(wide)).astype(jnp.bfloat16), PAIR)
    return own.astype(wide) + jnp.concatenate(
        [
            chip_early.astype(wide) + pair_early.astype(wide),
            chip_late.astype(wide) + pair_late.astype(wide),
        ],
        0,
    )


def product_rows(form, left, right):
    rows = left.shape[0] // 2
    far = jnp.einsum(form, left[rows:], right, preferred_element_type=jnp.float32)
    near = jnp.einsum(form, left[:rows], right, preferred_element_type=jnp.float32)
    return scatter_rows(near, far.astype(jnp.bfloat16))


def halves(values, axis):
    place = lax.axis_index("inner")
    size = values.shape[axis] // 2
    mine = lax.dynamic_slice_in_dim(values, place * size, size, axis)
    theirs = lax.dynamic_slice_in_dim(values, (1 - place) * size, size, axis)
    return (mine, theirs)


def in_order(mine, theirs, axis):
    first = lax.axis_index("inner") == 0
    return jnp.concatenate([jnp.where(first, mine, theirs), jnp.where(first, theirs, mine)], axis)


def trade(values, cut, join):
    mine, theirs = halves(values, cut)
    return in_order(mine, swap(theirs, PAIR), join)


def rope_tables(length):
    places = jnp.arange(length, dtype=jnp.float32)
    frequency = THETA ** (-jnp.arange(HD // 2, dtype=jnp.float32) * 2.0 / HD)
    angles = places[:, None] * frequency[None, :]
    cos_table = jnp.cos(angles)
    sin_table = jnp.sin(angles)
    return (
        jnp.concatenate([cos_table, cos_table], 1),
        jnp.concatenate([-sin_table, sin_table], 1),
    )


def unit_of(raw):
    inverse = lax.rsqrt(jnp.mean(raw * raw, -1, keepdims=True) + EPS)
    return (raw * inverse, inverse)


def turn(values, cos_table, sin_table):
    return values * cos_table + pltpu.roll(values, HD // 2, 1) * sin_table


def place_of(meta, block):
    relative = jnp.bitwise_xor(meta[0], block)
    return (jnp.bitwise_and(relative, 1), lax.shift_right_logical(relative, 1))


def load_heads(meta, raw, gains, cos_ref, sin_ref, queries, keys, values, rows, blocks, heads):
    gain_query = gains[0:1, :]
    gain_key = gains[1:2, :]
    for block in range(blocks):
        core, chip = place_of(meta, block)
        span = slice(block * rows, (block + 1) * rows)
        tile = raw[core, chip]
        cos_table = cos_ref[span, :]
        sin_table = sin_ref[span, :]
        for head in range(heads):
            unit, _ = unit_of(tile[:, head * HD : (head + 1) * HD])
            queries[head, span, :] = turn(unit * gain_query, cos_table, sin_table).astype(jnp.bfloat16)
        unit, _ = unit_of(tile[:, heads * HD : (heads + 1) * HD])
        keys[span, :] = turn(unit * gain_key, cos_table, sin_table).astype(jnp.bfloat16)
        values[span, :] = tile[:, (heads + 1) * HD :].astype(jnp.bfloat16)


def weights_of(query, keys, start, valid_len):
    scores = lax.dot_general(query, keys, (((1,), (1,)), ((), ())), preferred_element_type=jnp.float32)
    row = start + lax.broadcasted_iota(jnp.int32, scores.shape, 0)
    column = lax.broadcasted_iota(jnp.int32, scores.shape, 1)
    allowed = (column <= row) & (column < valid_len)
    weights = jnp.where(allowed, jnp.exp(scores * SCALE), 0.0)
    return (weights, 1.0 / jnp.sum(weights, -1, keepdims=True))


def forward_kernel(rows, blocks, heads, meta, raw, gains, cos_ref, sin_ref, context, queries, keys, values):
    load_heads(meta, raw, gains, cos_ref, sin_ref, queries, keys, values, rows, blocks, heads)
    valid_len = meta[1 + pl.program_id(0)]
    for block in range(blocks):
        core, chip = place_of(meta, block)
        seen = (block + 1) * rows
        for head in range(heads):
            query = queries[head, block * rows : seen, :]
            weights, inverse = weights_of(query, keys[:seen, :], block * rows, valid_len)
            part = jnp.dot(
                weights.astype(jnp.bfloat16), values[:seen, :], preferred_element_type=jnp.float32
            )
            context[core, chip, :, head * HD : (head + 1) * HD] = (part * inverse).astype(jnp.bfloat16)


def backward_kernel(
    rows, blocks, heads, meta, raw, context_grad, gains, cos_ref, sin_ref,
    raw_grad, gain_grad, queries, keys, values, key_grad, value_grad, query_grad,
):
    load_heads(meta, raw, gains, cos_ref, sin_ref, queries, keys, values, rows, blocks, heads)
    valid_len = meta[1 + pl.program_id(0)]
    key_grad[...] = jnp.zeros_like(key_grad)
    value_grad[...] = jnp.zeros_like(value_grad)
    first = (((0,), (0,)), ((), ()))
    last = (((1,), (1,)), ((), ()))
    for block in range(blocks):
        core, chip = place_of(meta, block)
        seen = (block + 1) * rows
        for head in range(heads):
            query = queries[head, block * rows : seen, :]
            grad = context_grad[core, chip, :, head * HD : (head + 1) * HD]
            weights, inverse = weights_of(query, keys[:seen, :], block * rows, valid_len)
            probability = weights * inverse
            value_grad[:seen, :] += lax.dot_general(
                probability.astype(jnp.bfloat16), grad, first, preferred_element_type=jnp.float32
            )
            prob_grad = lax.dot_general(grad, values[:seen, :], last, preferred_element_type=jnp.float32)
            inner = jnp.sum(probability * prob_grad, -1, keepdims=True)
            score_grad = (probability * (prob_grad - inner)).astype(jnp.bfloat16)
            query_grad[head, block * rows : seen, :] = SCALE * jnp.dot(
                score_grad, keys[:seen, :], preferred_element_type=jnp.float32
            )
            key_grad[:seen, :] += SCALE * lax.dot_general(
                score_grad, query, first, preferred_element_type=jnp.float32
            )
    query_total = jnp.zeros((1, HD), jnp.float32)
    key_total = jnp.zeros((1, HD), jnp.float32)
    for block in range(blocks):
        core, chip = place_of(meta, block)
        span = slice(block * rows, (block + 1) * rows)
        cos_table = cos_ref[span, :]
        sin_table = sin_ref[span, :]

        def back(raw_values, turned, gain):
            unit, inverse = unit_of(raw_values)
            scaled = turn(turned, cos_table, -sin_table)
            total = jnp.sum(scaled * unit, 0, keepdims=True)
            scaled = scaled * gain
            result = inverse * (scaled - unit * jnp.mean(scaled * unit, -1, keepdims=True))
            return (result.astype(jnp.bfloat16), total)

        for head in range(heads):
            columns = slice(head * HD, (head + 1) * HD)
            result, total = back(raw[core, chip, :, columns], query_grad[head, span, :], gains[0:1, :])
            raw_grad[core, chip, :, columns] = result
            query_total += total
        columns = slice(heads * HD, (heads + 1) * HD)
        result, total = back(raw[core, chip, :, columns], key_grad[span, :], gains[1:2, :])
        raw_grad[core, chip, :, columns] = result
        key_total += total
        raw_grad[core, chip, :, (heads + 1) * HD :] = value_grad[span, :].astype(jnp.bfloat16)
    gain_grad[0:1, :] = query_total
    gain_grad[1:2, :] = key_total


def row_blocks(rows, columns):
    return pl.BlockSpec((2, None, 2, rows, columns), lambda s, meta: (0, s, 0, 0, 0))


def whole(shape):
    return pl.BlockSpec(shape, lambda s, meta: (0,) * len(shape))


def split_rows(values, rows):
    return values.reshape(2, 2, 2, rows, values.shape[-1])


def attend_forward(meta, raw, gains, cos_table, sin_table):
    length = cos_table.shape[0]
    rows = raw.shape[0] // 8
    blocks = length // rows
    heads = raw.shape[1] // HD - 2
    pairs = 2 * heads * length * length
    result = pl.pallas_call(
        functools.partial(forward_kernel, rows, blocks, heads),
        out_shape=jax.ShapeDtypeStruct((2, 2, 2, rows, heads * HD), jnp.bfloat16),
        grid_spec=pltpu.PrefetchScalarGridSpec(
            num_scalar_prefetch=1,
            grid=(2,),
            in_specs=[
                row_blocks(rows, raw.shape[1]),
                whole((2, HD)),
                whole((length, HD)),
                whole((length, HD)),
            ],
            out_specs=row_blocks(rows, heads * HD),
            scratch_shapes=[
                pltpu.VMEM((heads, length, HD), jnp.bfloat16),
                pltpu.VMEM((length, HD), jnp.bfloat16),
                pltpu.VMEM((length, HD), jnp.bfloat16),
            ],
        ),
        compiler_params=pltpu.CompilerParams(vmem_limit_bytes=40 << 20),
        cost_estimate=pl.CostEstimate(
            flops=4 * pairs * HD, transcendentals=pairs, bytes_accessed=raw.size * 6
        ),
        name="attend_forward",
    )(meta, split_rows(raw, rows), gains, cos_table, sin_table)
    return result.reshape(8 * rows, heads * HD)


def attend_backward(meta, raw, context_grad, gains, cos_table, sin_table):
    length = cos_table.shape[0]
    rows = raw.shape[0] // 8
    blocks = length // rows
    width = raw.shape[1]
    heads = width // HD - 2
    pairs = 2 * heads * length * length
    raw_grad, gain_grad = pl.pallas_call(
        functools.partial(backward_kernel, rows, blocks, heads),
        out_shape=(
            jax.ShapeDtypeStruct((2, 2, 2, rows, width), jnp.bfloat16),
            jax.ShapeDtypeStruct((2, 2, HD), jnp.float32),
        ),
        grid_spec=pltpu.PrefetchScalarGridSpec(
            num_scalar_prefetch=1,
            grid=(2,),
            in_specs=[
                row_blocks(rows, width),
                row_blocks(rows, heads * HD),
                whole((2, HD)),
                whole((length, HD)),
                whole((length, HD)),
            ],
            out_specs=(
                row_blocks(rows, width),
                pl.BlockSpec((None, 2, HD), lambda s, meta: (s, 0, 0)),
            ),
            scratch_shapes=[
                pltpu.VMEM((heads, length, HD), jnp.bfloat16),
                pltpu.VMEM((length, HD), jnp.bfloat16),
                pltpu.VMEM((length, HD), jnp.bfloat16),
                pltpu.VMEM((length, HD), jnp.float32),
                pltpu.VMEM((length, HD), jnp.float32),
                pltpu.VMEM((heads, length, HD), jnp.float32),
            ],
        ),
        compiler_params=pltpu.CompilerParams(vmem_limit_bytes=48 << 20),
        cost_estimate=pl.CostEstimate(
            flops=10 * pairs * HD, transcendentals=pairs, bytes_accessed=raw.size * 8
        ),
        name="attend_backward",
    )(meta, split_rows(raw, rows), split_rows(context_grad, rows), gains, cos_table, sin_table)
    return (raw_grad.reshape(8 * rows, width), jnp.sum(gain_grad, 0))


def norm_back(normed_grad, hat_values, inverse, gain_vector):
    gain_grad = jnp.sum(normed_grad * hat_values, axis=0)
    scaled = normed_grad * gain_vector
    return (
        inverse * (scaled - hat_values * jnp.mean(scaled * hat_values, -1, keepdims=True)),
        gain_grad,
    )


def adam_step(gradient, moment_one, moment_two, master):
    new_one = BETA_ONE * moment_one + (1.0 - BETA_ONE) * gradient
    new_two = BETA_TWO * moment_two + (1.0 - BETA_TWO) * gradient * gradient
    update = (
        new_one / (1.0 - BETA_ONE**STEP) / (jnp.sqrt(new_two / (1.0 - BETA_TWO**STEP)) + ADAM_EPS)
        + DECAY * master
    )
    return (new_one, new_two, update)


def square(values):
    return jnp.sum(values * values)


def root_mean(values):
    return jnp.sqrt(jnp.mean(values * values, -1))


def gather_outer(values):
    return lax.all_gather(values, "outer", axis=0, tiled=True)


def scatter_outer(values):
    return lax.psum_scatter(values, "outer", scatter_dimension=0, tiled=True)


def shards(
    tokens,
    cotangent,
    lengths,
    norm_gains,
    gains_first,
    gains_second,
    query_weight,
    query_first,
    query_second,
    keyval_weight,
    keyval_first,
    keyval_second,
    output_weight,
    output_first,
    output_second,
    gateup_weight,
    gateup_first,
    gateup_second,
    down_weight,
    down_first,
    down_second,
):
    low = jnp.bfloat16
    shard_len = tokens.shape[1]
    narrow_size = lax.axis_size("narrow")
    outer_size = lax.axis_size("outer")
    seq_len = shard_len * narrow_size
    gain_one = norm_gains[:D]
    gain_two = norm_gains[D : 2 * D]
    head_gains = norm_gains[2 * D :].reshape(2, HD)
    cos_table, sin_table = rope_tables(seq_len)

    attn_pair = jnp.concatenate(
        [
            trade(part.astype(low), 1, 0)
            for part in (query_weight, keyval_weight[0], keyval_weight[1])
        ],
        1,
    )
    output_pair = trade(output_weight.astype(low), 0, 1)
    gateup_pair = jnp.concatenate(
        [trade(gateup_weight[0].astype(low), 1, 0), trade(gateup_weight[1].astype(low), 1, 0)], 1
    )
    down_pair = trade(down_weight.astype(low), 0, 1)
    full_attn = gather_outer(attn_pair)
    full_output = gather_outer(output_pair[None])
    full_gateup = gather_outer(gateup_pair)
    full_down = gather_outer(down_pair[None])
    piece = output_pair.shape[1]
    hidden_size = down_pair.shape[0]

    residual = tokens[0].astype(jnp.float32)
    inv_one = lax.rsqrt(jnp.mean(residual * residual, -1, keepdims=True) + EPS)
    hat_one = residual * inv_one
    whole_one = gather_rows((hat_one * gain_one).astype(low))
    raw = jnp.einsum("rd,dc->rc", whole_one, full_attn, preferred_element_type=jnp.float32)
    meta = jnp.concatenate(
        [lax.axis_index("narrow").astype(jnp.int32)[None], lengths, swap(lengths, PAIR)]
    )
    context = attend_forward(meta, raw, head_gains, cos_table, sin_table)

    def out_product(left, right):
        rows = left.shape[0]
        result = jnp.einsum("rc,zcd->rzd", left, right, preferred_element_type=jnp.float32)
        return result.reshape(rows, D)

    def rows_out(left, right):
        rows = left.shape[0] // 2
        far = out_product(left[rows:], right).astype(low)
        return scatter_rows(out_product(left[:rows], right), far)

    attn_part = rows_out(context, full_output)
    middle = residual + attn_part
    inv_two = lax.rsqrt(jnp.mean(middle * middle, -1, keepdims=True) + EPS)
    hat_two = middle * inv_two
    whole_two = gather_rows((hat_two * gain_two).astype(low))
    gateup = jnp.einsum("rd,df->rf", whole_two, full_gateup, preferred_element_type=jnp.float32)
    gate_val = gateup[:, :hidden_size]
    up_val = gateup[:, hidden_size:]
    sigmoid = jax.nn.sigmoid(gate_val)
    swish = gate_val * sigmoid
    hidden = (swish * up_val).astype(low)

    places = lax.axis_index("narrow") * shard_len + jnp.arange(shard_len, dtype=jnp.int32)
    valid = (places < lengths[0]).astype(jnp.float32)
    grad_out = cotangent[0].astype(jnp.float32) * valid[:, None]
    whole_grad = gather_rows(grad_out.astype(low))
    pieces_grad = whole_grad.reshape(whole_grad.shape[0], outer_size, piece)
    down_grad = jnp.einsum("rf,rzd->zfd", hidden, pieces_grad, preferred_element_type=jnp.float32)
    hidden_grad = jnp.einsum("rzd,zfd->rf", pieces_grad, full_down, preferred_element_type=jnp.float32)
    slope = sigmoid * (1.0 + gate_val * (1.0 - sigmoid))
    pair_grad = jnp.concatenate([hidden_grad * up_val * slope, hidden_grad * swish], 1).astype(low)
    gateup_grad = jnp.einsum("rd,rf->df", whole_two, pair_grad, preferred_element_type=jnp.float32)
    normed_two = product_rows("rf,df->rd", pair_grad, full_gateup)
    middle_norm, gain_two_grad = norm_back(normed_two, hat_two, inv_two, gain_two)
    middle_grad = grad_out + middle_norm
    whole_mid = gather_rows(middle_grad.astype(low))
    pieces_mid = whole_mid.reshape(whole_mid.shape[0], outer_size, piece)
    output_grad = jnp.einsum("rc,rzd->zcd", context, pieces_mid, preferred_element_type=jnp.float32)
    context_grad = jnp.einsum(
        "rzd,zcd->rc", pieces_mid, full_output, preferred_element_type=jnp.float32
    ).astype(low)
    attn_low, head_gain_grad = attend_backward(meta, raw, context_grad, head_gains, cos_table, sin_table)
    attn_grad = jnp.einsum("rd,rc->dc", whole_one, attn_low, preferred_element_type=jnp.float32)
    normed_one = product_rows("rc,dc->rd", attn_low, full_attn)
    input_norm, gain_one_grad = norm_back(normed_one, hat_one, inv_one, gain_one)
    input_grad = (middle_grad + input_norm).astype(low)

    mlp_part = rows_out(hidden, full_down)
    final = middle + mlp_part
    result = final.astype(low)
    rms_values = jnp.stack([root_mean(attn_part), root_mean(mlp_part), root_mean(final)])[:, None, :]

    down_sum = trade(scatter_outer(down_grad.astype(low))[0], 1, 0).astype(jnp.float32)
    gateup_own = scatter_outer(gateup_grad.astype(low))
    gateup_sum = jnp.stack(
        [trade(gateup_own[:, :hidden_size], 0, 1), trade(gateup_own[:, hidden_size:], 0, 1)]
    ).astype(jnp.float32)
    output_sum = trade(scatter_outer(output_grad.astype(low))[0], 1, 0).astype(jnp.float32)
    attn_own = scatter_outer(attn_grad.astype(low))
    query_half = query_weight.shape[1] // 2
    key_half = keyval_weight.shape[2] // 2
    query_sum = trade(attn_own[:, :query_half], 0, 1).astype(jnp.float32)
    keyval_sum = jnp.stack(
        [
            trade(attn_own[:, query_half : query_half + key_half], 0, 1),
            trade(attn_own[:, query_half + key_half :], 0, 1),
        ]
    ).astype(jnp.float32)

    gain_part = jnp.concatenate([gain_one_grad, gain_two_grad, head_gain_grad.reshape(-1)])
    new_query_first, new_query_second, query_update = adam_step(
        query_sum, query_first, query_second, query_weight
    )
    new_keyval_first, new_keyval_second, keyval_update = adam_step(
        keyval_sum, keyval_first, keyval_second, keyval_weight
    )
    new_output_first, new_output_second, output_update = adam_step(
        output_sum, output_first, output_second, output_weight
    )
    new_gateup_first, new_gateup_second, gateup_update = adam_step(
        gateup_sum, gateup_first, gateup_second, gateup_weight
    )
    new_down_first, new_down_second, down_update = adam_step(
        down_sum, down_first, down_second, down_weight
    )
    squares = jnp.stack(
        [
            square(query_weight),
            square(keyval_weight[0]),
            square(keyval_weight[1]),
            square(output_weight),
            square(gateup_weight[0]),
            square(gateup_weight[1]),
            square(down_weight),
            square(query_update),
            square(keyval_update[0]),
            square(keyval_update[1]),
            square(output_update),
            square(gateup_update[0]),
            square(gateup_update[1]),
            square(down_update),
        ]
    )
    gain_total, square_total = lax.psum((gain_part, squares), ("outer", "inner", "narrow"))
    matrix_norms = jnp.sqrt(square_total)
    matrix_weight = matrix_norms[:7]
    matrix_update = matrix_norms[7:]
    new_gains_first, new_gains_second, gains_update = adam_step(
        gain_total, gains_first, gains_second, norm_gains
    )
    segments = ((0, D), (2 * D, 2 * D + HD), (2 * D + HD, 2 * D + 2 * HD), (D, 2 * D))
    gain_weight = [jnp.sqrt(square(norm_gains[lower:upper])) for lower, upper in segments]
    gain_update = [jnp.sqrt(square(gains_update[lower:upper])) for lower, upper in segments]

    def ordered(gain, matrix):
        return jnp.stack(
            [gain[0], matrix[0], matrix[1], matrix[2], gain[1], gain[2], matrix[3], gain[3]]
            + [matrix[4], matrix[5], matrix[6]]
        )

    weight_norms = ordered(gain_weight, matrix_weight)
    update_norms = ordered(gain_update, matrix_update)
    trust = weight_norms / update_norms
    gain_trust = jnp.concatenate(
        [
            jnp.full((D,), 1.0, jnp.float32) * trust[0],
            jnp.full((D,), 1.0, jnp.float32) * trust[7],
            jnp.full((HD,), 1.0, jnp.float32) * trust[4],
            jnp.full((HD,), 1.0, jnp.float32) * trust[5],
        ]
    )
    new_gains = norm_gains - LEARN * gain_trust * gains_update
    new_query = query_weight - LEARN * trust[1] * query_update
    new_keyval = (
        keyval_weight - LEARN * jnp.stack([trust[2], trust[3]])[:, None, None] * keyval_update
    )
    new_output = output_weight - LEARN * trust[6] * output_update
    new_gateup = (
        gateup_weight - LEARN * jnp.stack([trust[8], trust[9]])[:, None, None] * gateup_update
    )
    new_down = down_weight - LEARN * trust[10] * down_update
    lamb_stats = jnp.stack([weight_norms, update_norms])
    return (
        result[None],
        input_grad[None],
        rms_values,
        new_gains,
        new_gains_first,
        new_gains_second,
        new_query,
        new_query_first,
        new_query_second,
        new_keyval,
        new_keyval_first,
        new_keyval_second,
        new_output,
        new_output_first,
        new_output_second,
        new_gateup,
        new_gateup_first,
        new_gateup_second,
        new_down,
        new_down_first,
        new_down_second,
        lamb_stats,
        trust,
    )


def solution(mesh):
    wide_size, narrow_size = mesh.devices.shape
    cube = jax.sharding.Mesh(
        mesh.devices.reshape(wide_size // 2, 2, narrow_size), ("outer", "inner", "narrow")
    )
    wide = ("outer", "inner")
    rows = P(wide, "narrow", None)
    matrix = P(wide, "narrow")
    stacked = P(None, wide, "narrow")
    turned = P("narrow", wide)
    in_specs = (rows, rows, P(wide), P(), P(), P())
    in_specs += (matrix,) * 3 + (stacked,) * 3 + (turned,) * 3 + (stacked,) * 3 + (turned,) * 3
    out_specs = (rows, rows, stacked, P(), P(), P())
    out_specs += (matrix,) * 3 + (stacked,) * 3 + (turned,) * 3 + (stacked,) * 3 + (turned,) * 3
    out_specs += (P(), P())
    return jax.shard_map(shards, mesh=cube, in_specs=in_specs, out_specs=out_specs, check_vma=False)
```

```python
import functools

import jax
import jax.numpy as jnp
from jax import lax
from jax.experimental import pallas as pl
from jax.experimental.pallas import tpu as pltpu
from jax.sharding import PartitionSpec as P

D = 2048
H = 16
KV = 8
HD = 128
STEP = 10


EPS = 1e-06
THETA = 1000000.0
BETA_ONE = 0.9
BETA_TWO = 0.999
ADAM_EPS = 1e-06
DECAY = 0.01
LEARN = 0.5

SCALE = HD ** (-0.5)
LIGHT = pl.CostEstimate(flops=1024, transcendentals=0, bytes_accessed=1024)

CHIP = ("narrow", 2)
CORE = ("narrow", 1)
PAIR = ("inner", 1)


def named(name, function, *operands):
    with jax.named_scope(name):
        return function(*operands)


def swap(values, link):
    axis, bit = link
    return lax.ppermute(values, axis, [(i, i ^ bit) for i in range(lax.axis_size(axis))])


def together(*values):
    return lax.optimization_barrier(values)


def gather_start(own):
    return together(swap(own, CHIP), swap(own, PAIR))


def gather_cross(chip, pair, split):
    if not split:
        return [swap(pair, CHIP)]
    half = pair.shape[0] // 2
    return [swap(chip[:half], PAIR), swap(pair[half:], CHIP)]


def gather_end(near):
    return list(near) + [swap(block, CORE) for block in near]


def partial_rows(left, right):
    rows = left.shape[0] // 8
    wide = jnp.float32
    low = jnp.bfloat16

    def part(first, last):
        return lax.dot_general(
            left[first * rows : last * rows],
            right,
            (((1,), (1,)), ((), ())),
            preferred_element_type=wide,
        )

    cross_far, left = together(part(7, 8).astype(low), left)
    cross_far, rest_far = together(swap(cross_far, CORE), part(4, 7).astype(low))
    rest_far = swap(rest_far, CORE)
    cross = (part(3, 4) + cross_far.astype(wide)).astype(low)
    return (cross, part(0, 3) + rest_far.astype(wide))


def scatter_cross(cross):
    half = cross.shape[0] // 2
    return together(swap(cross[:half], PAIR), swap(cross[half:], CHIP))


def scatter_near(rest, from_pair, from_chip):
    rows = rest.shape[0] // 3
    half = rows // 2
    wide = jnp.float32
    low = jnp.bfloat16
    zero = jnp.float32(0.0)
    low_half = ((0, half, 0), (0, 0, 0))
    high_half = ((half, 0, 0), (0, 0, 0))
    chip = (rest[rows : 2 * rows] + lax.pad(from_pair.astype(wide), zero, low_half)).astype(low)
    pair = (rest[2 * rows :] + lax.pad(from_chip.astype(wide), zero, high_half)).astype(low)
    return (rest[:rows].astype(low), swap(chip, CHIP), swap(pair, PAIR))


def three(own, chip, pair):
    return own.astype(jnp.float32) + chip.astype(jnp.float32) + pair.astype(jnp.float32)


def product_rows(left, right):
    cross, rest = partial_rows(left, right)
    return three(*scatter_near(rest, *scatter_cross(cross)))


def product_first(left, right):
    return lax.dot_general(
        left, right, (((0,), (0,)), ((), ())), preferred_element_type=jnp.float32
    ).astype(jnp.bfloat16)


def halves(values):
    place = lax.axis_index("inner")
    size = values.shape[1] // 2
    mine = lax.dynamic_slice_in_dim(values, place * size, size, 1)
    theirs = lax.dynamic_slice_in_dim(values, (1 - place) * size, size, 1)
    return (mine, theirs)


def in_order(mine, theirs, axis):
    first = lax.axis_index("inner") == 0
    return jnp.concatenate([jnp.where(first, mine, theirs), jnp.where(first, theirs, mine)], axis)


def pair_weights(parts):
    cut = [halves(part) for part in parts]
    mine = jnp.concatenate([mine for mine, _ in cut], 1)
    theirs = jnp.concatenate([theirs for _, theirs in cut], 1)
    return (mine, theirs)


def gather_weights(mine, theirs):
    return gather_outer(in_order(mine, theirs, 0))


def own_grads(values):
    rows = values.shape[0] // 2
    place = lax.axis_index("inner")
    mine = lax.dynamic_slice_in_dim(values, place * rows, rows, 0)
    return (mine, swap(lax.dynamic_slice_in_dim(values, (1 - place) * rows, rows, 0), PAIR))


def total(values):
    for axis in ("narrow", "inner", "outer"):
        bit = 1
        while bit < lax.axis_size(axis):
            values = values + swap(values, (axis, bit))
            bit *= 2
    return values


def places_of(blocks, count):
    half = blocks.shape[1] // 2
    places = []
    for side in (0, 4):
        places += [blocks.at[side], blocks.at[side + 1], blocks.at[side + 2]]
        if count == 8:
            places += [blocks.at[side + 3]]
        else:
            places += [blocks.at[side + 3, pl.ds(0, half)], blocks.at[side + 3, pl.ds(half, half)]]
    return places


def parts_of(block, count):
    first = block % 4 + (block // 4) * (count // 2)
    return range(first, first + (count // 2 - 3 if block % 4 == 3 else 1))


def join_kernel(*refs):
    count = len(refs) - 4
    pieces = refs[:count]
    joined, blocks, arrive, leave = refs[count:]
    places = places_of(blocks, count)
    arrivals = [pltpu.make_async_copy(pieces[i], places[i], arrive.at[i]) for i in range(count)]
    departures = [pltpu.make_async_copy(blocks.at[i], joined.at[i], leave.at[i]) for i in range(8)]
    for copy in arrivals:
        copy.start()
    for block in range(8):
        for index in parts_of(block, count):
            arrivals[index].wait()
        departures[block].start()
    for copy in departures:
        copy.wait()


def join(pieces):
    rows, depth = pieces[0].shape
    anywhere = pl.BlockSpec(memory_space=pltpu.HBM)
    return pl.pallas_call(
        join_kernel,
        out_shape=jax.ShapeDtypeStruct((8, rows, depth), jnp.bfloat16),
        in_specs=[anywhere] * len(pieces),
        out_specs=anywhere,
        scratch_shapes=[
            pltpu.VMEM((8, rows, depth), jnp.bfloat16),
            pltpu.SemaphoreType.DMA((len(pieces),)),
            pltpu.SemaphoreType.DMA((8,)),
        ],
        cost_estimate=LIGHT,
        name="join",
    )(*pieces).reshape(8 * rows, depth)


def rows_kernel(finish, count, extra, results, *refs):
    pieces = refs[:count]
    weights = refs[count : count + extra]
    outputs = refs[count + extra : count + extra + results]
    joined, *beside, blocks, arrive, leave = refs[count + extra + results :]
    step = pl.program_id(0)
    places = places_of(blocks, count)

    def arrival(index):
        return pltpu.make_async_copy(pieces[index], places[index], arrive.at[index])

    def departure(block):
        return pltpu.make_async_copy(blocks.at[block], joined.at[block], leave.at[block])

    def beside_copies():
        if not beside:
            return []
        width = weights[0].shape[1]
        return [
            pltpu.make_async_copy(weight, beside[0].at[:, pl.ds(i * width, width)], leave.at[8 + i])
            for i, weight in enumerate(weights)
        ]

    @pl.when(step == 0)
    def _():
        for index in range(count):
            arrival(index).start()
        for copy in beside_copies():
            copy.start()

    for block in range(8):

        @pl.when(step == block)
        def _(block=block):
            for index in parts_of(block, count):
                arrival(index).wait()
            departure(block).start()

    finish(blocks[step], weights, (), outputs)

    @pl.when(step == 7)
    def _():
        for block in range(8):
            departure(block).wait()
        for copy in beside_copies():
            copy.wait()


def rows_call(name, finish, pieces, weights, widths, kinds, columns=None, place=0):
    rows, depth = pieces[0].shape
    columns = columns or weights[0].shape[1]
    beside = (depth, len(weights) * columns)

    def block(width):
        return pl.BlockSpec((None, rows, width), lambda i: (i, 0, 0))

    anywhere = pl.BlockSpec(memory_space=pltpu.HBM)
    more = len(weights) > 1
    results = pl.pallas_call(
        functools.partial(rows_kernel, finish, len(pieces), len(weights), len(widths)),
        out_shape=tuple(
            jax.ShapeDtypeStruct((8, rows, width), kind) for width, kind in zip(widths, kinds)
        )
        + (jax.ShapeDtypeStruct((8, rows, depth), jnp.bfloat16),)
        + (jax.ShapeDtypeStruct(beside, jnp.bfloat16),) * more,
        grid=(8,),
        in_specs=[anywhere] * len(pieces)
        + [pl.BlockSpec((depth, columns), lambda i: (0, place), pipeline_mode=pl.Buffered(1))]
        * len(weights),
        out_specs=tuple(block(width) for width in widths) + (anywhere,) * (1 + more),
        scratch_shapes=[
            pltpu.VMEM((8, rows, depth), jnp.bfloat16),
            pltpu.SemaphoreType.DMA((len(pieces),)),
            pltpu.SemaphoreType.DMA((8 + len(weights),)),
        ],
        cost_estimate=LIGHT,
        name=name,
    )(*pieces, *weights)
    count = len(widths) + 1
    return [result.reshape(8 * rows, result.shape[-1]) for result in results[:count]] + list(results[count:])


def blocks_kernel(finish, left, weight, *refs):
    finish(left[...], (weight,), refs[:-1], refs[-1:])


def blocks_call(name, finish, left, weight, operands, width, rows):
    depth, columns = weight.shape
    count = left.shape[0] // rows

    def block(size):
        return pl.BlockSpec((rows, size), lambda i: (i, 0))

    return pl.pallas_call(
        functools.partial(blocks_kernel, finish),
        out_shape=jax.ShapeDtypeStruct((left.shape[0], width), jnp.bfloat16),
        grid=(count,),
        in_specs=[block(depth), pl.BlockSpec(weight.shape, lambda i: (0, 0), pipeline_mode=pl.Buffered(1))]
        + [block(operand.shape[1]) for operand in operands],
        out_specs=block(width),
        cost_estimate=LIGHT,
        name=name,
    )(left, weight, *operands)


def product(left, right):
    return jnp.dot(left, right, preferred_element_type=jnp.float32)


def plain_finish(left, weights, operands, outputs):
    outputs[0][...] = product(left, weights[0][...]).astype(outputs[0].dtype)


def tiles_of(size):
    return [slice(start, start + 256) for start in range(0, size, 256)]


def gate_finish(left, weights, operands, outputs):
    both, hidden = outputs
    size = hidden.shape[1]
    for tile in tiles_of(size):
        up_tile = slice(size + tile.start, size + tile.stop)
        gate_val = product(left, weights[0][:, tile])
        up_val = product(left, weights[1][:, tile])
        both[:, tile] = gate_val.astype(both.dtype)
        both[:, up_tile] = up_val.astype(both.dtype)
        hidden[:, tile] = (gate_val * jax.nn.sigmoid(gate_val) * up_val).astype(hidden.dtype)


def hidden_finish(left, weights, operands, outputs):
    (both,) = operands
    (grads,) = outputs
    size = both.shape[1] // 2
    for tile in tiles_of(size):
        up_tile = slice(size + tile.start, size + tile.stop)
        hidden_grad = product(left, weights[0][:, tile])
        gate_val = both[:, tile].astype(jnp.float32)
        up_val = both[:, up_tile].astype(jnp.float32)
        sigmoid = jax.nn.sigmoid(gate_val)
        slope = sigmoid * (1.0 + gate_val * (1.0 - sigmoid))
        grads[:, tile] = (hidden_grad * up_val * slope).astype(grads.dtype)
        grads[:, up_tile] = (hidden_grad * (gate_val * sigmoid)).astype(grads.dtype)


def rope_tables(length):
    places = jnp.arange(length, dtype=jnp.float32)
    frequency = THETA ** (-jnp.arange(HD // 2, dtype=jnp.float32) * 2.0 / HD)
    angles = places[:, None] * frequency[None, :]
    cos_table = jnp.cos(angles)
    sin_table = jnp.sin(angles)
    return (
        jnp.concatenate([cos_table, cos_table], 1),
        jnp.concatenate([-sin_table, sin_table], 1),
    )


def unit_of(raw):
    inverse = lax.rsqrt(jnp.mean(raw * raw, -1, keepdims=True) + EPS)
    return (raw * inverse, inverse)


def turn(values, cos_table, sin_table):
    return values * cos_table + pltpu.roll(values, HD // 2, 1) * sin_table


def place_of(meta, block):
    relative = jnp.bitwise_xor(meta[0], block)
    return (jnp.bitwise_and(relative, 1), lax.shift_right_logical(relative, 1))


def load_heads(meta, raw, gains, cos_ref, sin_ref, queries, keys, values, rows, blocks, heads):
    gain_query = gains[0:1, :]
    gain_key = gains[1:2, :]
    for block in range(blocks):
        core, chip = place_of(meta, block)
        span = slice(block * rows, (block + 1) * rows)
        tile = raw[core, chip]
        cos_table = cos_ref[span, :]
        sin_table = sin_ref[span, :]
        for head in range(heads):
            unit, _ = unit_of(tile[:, head * HD : (head + 1) * HD])
            queries[head, span, :] = turn(unit * gain_query, cos_table, sin_table).astype(jnp.bfloat16)
        unit, _ = unit_of(tile[:, heads * HD : (heads + 1) * HD])
        keys[span, :] = turn(unit * gain_key, cos_table, sin_table).astype(jnp.bfloat16)
        values[span, :] = tile[:, (heads + 1) * HD :].astype(jnp.bfloat16)


def weights_of(query, keys, start, valid_len):
    scores = lax.dot_general(query, keys, (((1,), (1,)), ((), ())), preferred_element_type=jnp.float32)
    row = start + lax.broadcasted_iota(jnp.int32, scores.shape, 0)
    column = lax.broadcasted_iota(jnp.int32, scores.shape, 1)
    allowed = (column <= row) & (column < valid_len)
    weights = jnp.where(allowed, jnp.exp(scores * SCALE), 0.0)
    return (weights, 1.0 / jnp.sum(weights, -1, keepdims=True))


def forward_kernel(rows, blocks, heads, meta, raw, gains, cos_ref, sin_ref, context, queries, keys, values):
    load_heads(meta, raw, gains, cos_ref, sin_ref, queries, keys, values, rows, blocks, heads)
    valid_len = meta[1 + pl.program_id(0)]
    for block in range(blocks):
        core, chip = place_of(meta, block)
        seen = (block + 1) * rows
        for head in range(heads):
            query = queries[head, block * rows : seen, :]
            weights, inverse = weights_of(query, keys[:seen, :], block * rows, valid_len)
            part = jnp.dot(
                weights.astype(jnp.bfloat16), values[:seen, :], preferred_element_type=jnp.float32
            )
            context[core, chip, :, head * HD : (head + 1) * HD] = (part * inverse).astype(jnp.bfloat16)


def backward_kernel(
    rows, blocks, heads, meta, raw, context_grad, gains, cos_ref, sin_ref,
    raw_grad, gain_grad, queries, keys, values, key_grad, value_grad, query_grad,
):
    load_heads(meta, raw, gains, cos_ref, sin_ref, queries, keys, values, rows, blocks, heads)
    valid_len = meta[1 + pl.program_id(0)]
    key_grad[...] = jnp.zeros_like(key_grad)
    value_grad[...] = jnp.zeros_like(value_grad)
    first = (((0,), (0,)), ((), ()))
    last = (((1,), (1,)), ((), ()))
    for block in range(blocks):
        core, chip = place_of(meta, block)
        seen = (block + 1) * rows
        for head in range(heads):
            query = queries[head, block * rows : seen, :]
            grad = context_grad[core, chip, :, head * HD : (head + 1) * HD]
            weights, inverse = weights_of(query, keys[:seen, :], block * rows, valid_len)
            probability = weights * inverse
            value_grad[:seen, :] += lax.dot_general(
                probability.astype(jnp.bfloat16), grad, first, preferred_element_type=jnp.float32
            )
            prob_grad = lax.dot_general(grad, values[:seen, :], last, preferred_element_type=jnp.float32)
            inner = jnp.sum(probability * prob_grad, -1, keepdims=True)
            score_grad = (probability * (prob_grad - inner)).astype(jnp.bfloat16)
            query_grad[head, block * rows : seen, :] = SCALE * jnp.dot(
                score_grad, keys[:seen, :], preferred_element_type=jnp.float32
            )
            key_grad[:seen, :] += SCALE * lax.dot_general(
                score_grad, query, first, preferred_element_type=jnp.float32
            )
    query_total = jnp.zeros((1, HD), jnp.float32)
    key_total = jnp.zeros((1, HD), jnp.float32)
    for block in range(blocks):
        core, chip = place_of(meta, block)
        span = slice(block * rows, (block + 1) * rows)
        cos_table = cos_ref[span, :]
        sin_table = sin_ref[span, :]

        def back(raw_values, turned, gain):
            unit, inverse = unit_of(raw_values)
            scaled = turn(turned, cos_table, -sin_table)
            total = jnp.sum(scaled * unit, 0, keepdims=True)
            scaled = scaled * gain
            result = inverse * (scaled - unit * jnp.mean(scaled * unit, -1, keepdims=True))
            return (result.astype(jnp.bfloat16), total)

        for head in range(heads):
            columns = slice(head * HD, (head + 1) * HD)
            result, total = back(raw[core, chip, :, columns], query_grad[head, span, :], gains[0:1, :])
            raw_grad[core, chip, :, columns] = result
            query_total += total
        columns = slice(heads * HD, (heads + 1) * HD)
        result, total = back(raw[core, chip, :, columns], key_grad[span, :], gains[1:2, :])
        raw_grad[core, chip, :, columns] = result
        key_total += total
        raw_grad[core, chip, :, (heads + 1) * HD :] = value_grad[span, :].astype(jnp.bfloat16)
    gain_grad[0:1, :] = query_total
    gain_grad[1:2, :] = key_total


def row_blocks(rows, columns):
    return pl.BlockSpec((2, None, 2, rows, columns), lambda s, meta: (0, s, 0, 0, 0))


def whole(shape):
    return pl.BlockSpec(shape, lambda s, meta: (0,) * len(shape))


def split_rows(values, rows):
    return values.reshape(2, 2, 2, rows, values.shape[-1])


def attend_forward(meta, raw, gains, cos_table, sin_table):
    length = cos_table.shape[0]
    rows = raw.shape[0] // 8
    blocks = length // rows
    heads = raw.shape[1] // HD - 2
    result = pl.pallas_call(
        functools.partial(forward_kernel, rows, blocks, heads),
        out_shape=jax.ShapeDtypeStruct((2, 2, 2, rows, heads * HD), jnp.bfloat16),
        grid_spec=pltpu.PrefetchScalarGridSpec(
            num_scalar_prefetch=1,
            grid=(2,),
            in_specs=[
                row_blocks(rows, raw.shape[1]),
                whole((2, HD)),
                whole((length, HD)),
                whole((length, HD)),
            ],
            out_specs=row_blocks(rows, heads * HD),
            scratch_shapes=[
                pltpu.VMEM((heads, length, HD), jnp.bfloat16),
                pltpu.VMEM((length, HD), jnp.bfloat16),
                pltpu.VMEM((length, HD), jnp.bfloat16),
            ],
        ),
        cost_estimate=LIGHT,
        name="attend_forward",
    )(meta, split_rows(raw, rows), gains, cos_table, sin_table)
    return result.reshape(8 * rows, heads * HD)


def attend_backward(meta, raw, context_grad, gains, cos_table, sin_table):
    length = cos_table.shape[0]
    rows = raw.shape[0] // 8
    blocks = length // rows
    width = raw.shape[1]
    heads = width // HD - 2
    raw_grad, gain_grad = pl.pallas_call(
        functools.partial(backward_kernel, rows, blocks, heads),
        out_shape=(
            jax.ShapeDtypeStruct((2, 2, 2, rows, width), jnp.bfloat16),
            jax.ShapeDtypeStruct((2, 2, HD), jnp.float32),
        ),
        grid_spec=pltpu.PrefetchScalarGridSpec(
            num_scalar_prefetch=1,
            grid=(2,),
            in_specs=[
                row_blocks(rows, width),
                row_blocks(rows, heads * HD),
                whole((2, HD)),
                whole((length, HD)),
                whole((length, HD)),
            ],
            out_specs=(
                row_blocks(rows, width),
                pl.BlockSpec((None, 2, HD), lambda s, meta: (s, 0, 0)),
            ),
            scratch_shapes=[
                pltpu.VMEM((heads, length, HD), jnp.bfloat16),
                pltpu.VMEM((length, HD), jnp.bfloat16),
                pltpu.VMEM((length, HD), jnp.bfloat16),
                pltpu.VMEM((length, HD), jnp.float32),
                pltpu.VMEM((length, HD), jnp.float32),
                pltpu.VMEM((heads, length, HD), jnp.float32),
            ],
        ),
        cost_estimate=LIGHT,
        name="attend_backward",
    )(meta, split_rows(raw, rows), split_rows(context_grad, rows), gains, cos_table, sin_table)
    return (raw_grad.reshape(8 * rows, width), jnp.sum(gain_grad, 0))


def norm_back(normed_grad, hat_values, inverse, gain_vector):
    gain_grad = jnp.sum(normed_grad * hat_values, axis=0)
    scaled = normed_grad * gain_vector
    return (
        inverse * (scaled - hat_values * jnp.mean(scaled * hat_values, -1, keepdims=True)),
        gain_grad,
    )


def moments(gradient, moment_one, moment_two):
    new_one = BETA_ONE * moment_one + (1.0 - BETA_ONE) * gradient
    new_two = BETA_TWO * moment_two + (1.0 - BETA_TWO) * gradient * gradient
    return (new_one, new_two)


def update_of(new_one, new_two, master):
    return (
        new_one / (1.0 - BETA_ONE**STEP) / (jnp.sqrt(new_two / (1.0 - BETA_TWO**STEP)) + ADAM_EPS)
        + DECAY * master
    )


def square(values):
    return jnp.sum(jnp.sum(values * values, 1, keepdims=True), 0, keepdims=True)


def step_part(gradient, span, arrays, results):
    one, two, master = (array[span].reshape(gradient.shape) for array in arrays)
    new_one, new_two = moments(gradient, one, two)
    results[0][span] = new_one.reshape(results[0][span].shape)
    results[1][span] = new_two.reshape(results[1][span].shape)
    return (square(master), square(update_of(new_one, new_two, master)))


def put_sums(sums, pairs, first):
    row = lax.broadcasted_iota(jnp.int32, sums.shape, 0)
    tile = jnp.zeros(sums.shape, jnp.float32)
    for index, value in enumerate(pairs):
        tile = jnp.where(row == index, value, tile)
    sums[...] = tile + jnp.where(first, 0.0, sums[...])


def add_pairs(left, right):
    return (left[0] + right[0], left[1] + right[1])


def stacked_step(meta, mine, other, one, two, master, new_one, new_two, sums):
    step = pl.program_id(0)
    size = one.shape[2]
    pairs = []
    for side in range(2):
        columns = slice(side * size, (side + 1) * size)
        own = step == meta[0]
        gradient = jnp.where(own, mine[:, columns], other[:, columns]).astype(jnp.float32)
        pairs += step_part(gradient, (side,), (one, two, master), (new_one, new_two))
    put_sums(sums, pairs, step == 0)


def turned_step(meta, mine, other, one, two, master, new_one, new_two, sums):
    step = pl.program_id(0)
    gradient = jnp.where(step == meta[0], mine[...], other[...]).astype(jnp.float32).T
    pair = step_part(gradient, (slice(None),), (one, two, master), (new_one, new_two))
    put_sums(sums, pair, step == 0)


def attn_step(
    meta, mine, other, query_one, query_two, query, keyval_one, keyval_two, keyval,
    output_one, output_two, output, new_query_one, new_query_two, new_keyval_one, new_keyval_two,
    new_output_one, new_output_two, sums,
):
    step = pl.program_id(0)
    own = step == meta[0]
    width = query.shape[1]
    key_width = keyval.shape[2]

    def part(first, size):
        columns = slice(first, first + size)
        return jnp.where(own, mine[:, columns], other[:, columns]).astype(jnp.float32)

    whole_span = (slice(None),)
    pairs = []
    pairs += step_part(part(0, width), whole_span, (query_one, query_two, query), (new_query_one, new_query_two))
    for side in range(2):
        pairs += step_part(
            part(width + side * key_width, key_width), (side,),
            (keyval_one, keyval_two, keyval), (new_keyval_one, new_keyval_two),
        )
    pairs += step_part(
        part(width + 2 * key_width, mine.shape[1] - width - 2 * key_width).T, whole_span,
        (output_one, output_two, output), (new_output_one, new_output_two),
    )
    put_sums(sums, pairs, step == 0)


def half_block(array, axis):
    shape = tuple(size // 2 if place == axis else size for place, size in enumerate(array.shape))
    return pl.BlockSpec(shape, lambda i, meta: tuple(i if place == axis else 0 for place in range(len(shape))))


def step_call(name, kernel, place, mine, other, arrays, axes):
    fixed = pl.BlockSpec(mine.shape, lambda i, meta: (0, 0))
    specs = [half_block(array, axis) for group, axis in zip(arrays, axes) for array in group]
    out_arrays = [(array, axis) for group, axis in zip(arrays, axes) for array in group[:2]]
    size = sum(array.size for group in arrays for array in group)
    return pl.pallas_call(
        kernel,
        out_shape=tuple(jax.ShapeDtypeStruct(array.shape, jnp.float32) for array, _ in out_arrays)
        + (jax.ShapeDtypeStruct((8, HD), jnp.float32),),
        grid_spec=pltpu.PrefetchScalarGridSpec(
            num_scalar_prefetch=1,
            grid=(2,),
            in_specs=[fixed, fixed] + specs,
            out_specs=tuple(half_block(array, axis) for array, axis in out_arrays)
            + (pl.BlockSpec((8, HD), lambda i, meta: (0, 0)),),
        ),
        cost_estimate=pl.CostEstimate(flops=8 * size, transcendentals=0, bytes_accessed=7 * size),
        name=name,
    )(place, mine, other, *[array for group in arrays for array in group])


def ratio_of(weight_square, update_square):
    return jnp.sqrt(weight_square) / jnp.sqrt(update_square)


def apply_kernel(parts, axes, *refs):
    sums = refs[0]
    index = 1
    count = len(parts)
    for place, rows in enumerate(parts):
        one, two, master = refs[1 + 3 * place : 4 + 3 * place]
        result = refs[1 + 3 * count + place]
        for side, row in enumerate(rows):
            span = (side,) if len(rows) > 1 else (slice(None),)
            trust = ratio_of(sums[row : row + 1, 0:1], sums[row + 1 : row + 2, 0:1])
            old = master[span]
            result[span] = old - LEARN * trust * update_of(one[span], two[span], old)


def apply_call(name, sums, arrays, parts, axes, steps):
    def block(array, axis):
        shape = tuple(size // steps if place == axis else size for place, size in enumerate(array.shape))
        return pl.BlockSpec(shape, lambda i: tuple(i if place == axis else 0 for place in range(len(shape))))

    size = sum(array.size for group in arrays for array in group)
    return pl.pallas_call(
        functools.partial(apply_kernel, parts, axes),
        out_shape=tuple(jax.ShapeDtypeStruct(group[2].shape, jnp.float32) for group in arrays),
        grid=(steps,),
        in_specs=[pl.BlockSpec(sums.shape, lambda i: (0, 0))]
        + [block(array, axis) for group, axis in zip(arrays, axes) for array in group],
        out_specs=tuple(block(group[2], axis) for group, axis in zip(arrays, axes)),
        cost_estimate=pl.CostEstimate(flops=8 * size, transcendentals=0, bytes_accessed=6 * size),
        name=name,
    )(sums, *[array for group in arrays for array in group])


def gains_kernel(rows, late, early, first, second, gains, new_first, new_second, new_gains, stats, trust):
    each = (rows - 2) // 2
    new_one, new_two = moments(late[:rows, :], first[:rows, :], second[:rows, :])
    for result, values in ((new_first, new_one), (new_second, new_two), (new_gains, new_one)):
        result[:rows, :] = values
        result[rows:, :] = jnp.zeros_like(result[rows:, :])
    lane = lax.broadcasted_iota(jnp.int32, (1, HD), 1)
    weight_row = jnp.zeros((1, HD), jnp.float32)
    update_row = jnp.zeros((1, HD), jnp.float32)

    def put(place, weight_square, update_square, weight_row, update_row):
        return (
            jnp.where(lane == place, jnp.sqrt(weight_square), weight_row),
            jnp.where(lane == place, jnp.sqrt(update_square), update_row),
        )

    for place, start, size in ((0, 0, each), (7, each, each), (4, 2 * each, 1), (5, 2 * each + 1, 1)):
        span = slice(start, start + size)
        old = gains[span, :]
        update = update_of(new_one[span, :], new_two[span, :], old)
        weight_square, update_square = (square(old), square(update))
        new_gains[span, :] = old - LEARN * ratio_of(weight_square, update_square) * update
        weight_row, update_row = put(place, weight_square, update_square, weight_row, update_row)
    for place, index in ((1, 0), (2, 2), (3, 4), (6, 6)):
        weight_row, update_row = put(
            place, late[rows + index : rows + index + 1, 0:1], late[rows + index + 1 : rows + index + 2, 0:1],
            weight_row, update_row,
        )
    for place, index in ((8, 0), (9, 2), (10, 8)):
        weight_row, update_row = put(
            place, early[index : index + 1, 0:1], early[index + 1 : index + 2, 0:1], weight_row, update_row
        )
    stats[0:1, :] = weight_row[:, :11]
    stats[1:2, :] = update_row[:, :11]
    trust[...] = (weight_row / jnp.where(lane < 11, update_row, 1.0))[:, :11]


def root_mean(values):
    return jnp.sqrt(jnp.mean(values * values, -1))


def gather_outer(values):
    return lax.all_gather(values, "outer", axis=0, tiled=True)


def scatter_outer(values):
    return lax.psum_scatter(values, "outer", scatter_dimension=0, tiled=True)


def shards(
    tokens,
    cotangent,
    lengths,
    norm_gains,
    gains_first,
    gains_second,
    query_weight,
    query_first,
    query_second,
    keyval_weight,
    keyval_first,
    keyval_second,
    output_weight,
    output_first,
    output_second,
    gateup_weight,
    gateup_first,
    gateup_second,
    down_weight,
    down_first,
    down_second,
):
    low = jnp.bfloat16
    shard_len = tokens.shape[1]
    narrow_size = lax.axis_size("narrow")
    outer_size = lax.axis_size("outer")
    seq_len = shard_len * narrow_size
    gain_one = norm_gains[:D]
    gain_two = norm_gains[D : 2 * D]
    head_gains = norm_gains[2 * D :].reshape(2, HD)
    cos_table, sin_table = rope_tables(seq_len)

    residual = tokens[0].astype(jnp.float32)
    inv_one = lax.rsqrt(jnp.mean(residual * residual, -1, keepdims=True) + EPS)
    hat_one = residual * inv_one
    normed = (hat_one * gain_one).astype(low)

    query_half = query_weight.shape[1] // 2
    key_half = keyval_weight.shape[2] // 2
    output_half = output_weight.shape[0] // 2
    hidden_size = down_weight.shape[0] // 2
    raw_width = query_half + 2 * key_half
    places = lax.axis_index("narrow") * shard_len + jnp.arange(shard_len, dtype=jnp.int32)
    valid = (places < lengths[0]).astype(jnp.float32)
    grad_out = cotangent[0].astype(jnp.float32) * valid[:, None]
    attn_low = [w.astype(low) for w in (query_weight, keyval_weight[0], keyval_weight[1])]
    mine, theirs = pair_weights(attn_low + [output_weight.astype(low).T])
    full_attn = gather_weights(mine, swap(theirs, PAIR))

    chip, pair = named("norm_one", gather_start, normed)
    gateup_mine, gateup_theirs = pair_weights([part.astype(low) for part in gateup_weight])
    chip, pair, gateup_theirs = together(chip, pair, gateup_theirs)
    (cross,) = named("norm_one", gather_cross, chip, pair, False)
    gateup_pair = in_order(gateup_mine, swap(gateup_theirs, PAIR), 0)
    full_attn, grad_low = together(full_attn, grad_out.astype(low))
    cross, gateup_pair = together(cross, gateup_pair)
    full_gate = gather_outer(gateup_pair[:, :hidden_size])
    full_up = gather_outer(gateup_pair[:, hidden_size:])
    grad_chip, grad_pair = named("output_grad", gather_start, grad_low)
    pieces_one = named("norm_one", gather_end, (normed, chip, pair, cross))
    raw, whole_one = rows_call(
        "query_key_value", plain_finish, pieces_one, [full_attn], [raw_width], [jnp.float32], raw_width
    )
    down_mine, down_theirs = pair_weights([down_weight.astype(low).T])
    raw, grad_chip, grad_pair, down_theirs = together(raw, grad_chip, grad_pair, down_theirs)
    down_pair = in_order(down_mine, swap(down_theirs, PAIR), 0)
    meta = jnp.concatenate(
        [lax.axis_index("narrow").astype(jnp.int32)[None], lengths, swap(lengths, PAIR)]
    )
    context = attend_forward(meta, raw, head_gains, cos_table, sin_table)
    context, down_pair = together(context, down_pair)
    full_down = gather_outer(down_pair)

    full_output = full_attn[:, raw_width:]
    cross, rest = named("attention_out", partial_rows, context, full_output)
    moved = named("attention_out", scatter_cross, cross)
    own, chip, pair = named("attention_out", scatter_near, rest, *moved)
    own, chip, pair, full_gate = together(own, chip, pair, full_gate)
    attn_part = three(own, chip, pair)
    middle = residual + attn_part
    inv_two = lax.rsqrt(jnp.mean(middle * middle, -1, keepdims=True) + EPS)
    hat_two = middle * inv_two
    normed = (hat_two * gain_two).astype(low)
    chip, pair = named("norm_two", gather_start, normed)
    cross = named("norm_two", gather_cross, chip, pair, True)
    *cross, grad_chip, grad_pair = together(*cross, grad_chip, grad_pair)
    pieces_two = named("norm_two", gather_end, (normed, chip, pair, *cross))
    grad_cross = named("output_grad", gather_cross, grad_chip, grad_pair, True)
    pieces_grad = named("output_grad", gather_end, (grad_low, grad_chip, grad_pair, *grad_cross))
    both, hidden, whole_two, full_gateup = rows_call(
        "gate_up", gate_finish, pieces_two, [full_gate, full_up], [2 * hidden_size, hidden_size], [low, low]
    )
    whole_grad = join(pieces_grad)
    down_grad = product_first(whole_grad, hidden)
    full_down, down_grad = together(full_down, down_grad)
    down_own = scatter_outer(down_grad)
    pair_grad = blocks_call(
        "hidden_grad", hidden_finish, whole_grad, full_down, [both], 2 * hidden_size, shard_len
    )
    normed_two = named("norm_two_grad", product_rows, pair_grad, full_gateup)
    gateup_grad = product_first(whole_two, pair_grad)
    normed_two, gateup_grad = together(normed_two, gateup_grad)
    gateup_grad, down_own = together(gateup_grad, down_own)
    gateup_own = scatter_outer(gateup_grad)
    middle_norm, gain_two_grad = norm_back(normed_two, hat_two, inv_two, gain_two)
    middle_grad = grad_out + middle_norm
    middle_low = middle_grad.astype(low)
    chip, pair = named("middle_grad", gather_start, middle_low)
    cross = named("middle_grad", gather_cross, chip, pair, True)
    hidden, full_down, middle_low = together(hidden, full_down, middle_low)
    mlp_cross, mlp_rest = named("mlp_out", partial_rows, hidden, full_down)
    *cross, mlp_cross, mlp_rest = together(*cross, mlp_cross, mlp_rest)
    pieces_mid = named("middle_grad", gather_end, (middle_low, chip, pair, *cross))
    context_grad, whole_mid = rows_call(
        "context_grad", plain_finish, pieces_mid, [full_attn], [output_half], [low],
        output_half, raw_width // output_half,
    )
    moved = named("mlp_out", scatter_cross, mlp_cross)
    context_grad, mlp_rest, *moved = together(context_grad, mlp_rest, *moved)
    mlp_parts = named("mlp_out", scatter_near, mlp_rest, *moved)
    raw_grad, head_gain_grad = attend_backward(meta, raw, context_grad, head_gains, cos_table, sin_table)
    attn_grad = jnp.concatenate(
        [product_first(whole_one, raw_grad), product_first(whole_mid, context)], 1
    )
    raw_grad, attn_grad, *mlp_parts = together(raw_grad, attn_grad, *mlp_parts)
    mlp_part = three(*mlp_parts)
    attn_grad, gateup_own = together(attn_grad, gateup_own)
    attn_own = scatter_outer(attn_grad)
    normed_one = named("norm_one_grad", product_rows, raw_grad, full_attn[:, :raw_width])
    input_norm, gain_one_grad = norm_back(normed_one, hat_one, inv_one, gain_one)
    input_grad = (middle_grad + input_norm).astype(low)

    final = middle + mlp_part
    result = final.astype(low)
    rms_values = jnp.stack([root_mean(attn_part), root_mean(mlp_part), root_mean(final)])[:, None, :]

    place = lax.axis_index("inner").astype(jnp.int32)[None]
    down = (down_first, down_second, down_weight)
    gateup = (gateup_first, gateup_second, gateup_weight)
    new_down_first, new_down_second, down_sums = step_call(
        "down_step", turned_step, place, *own_grads(down_own), [down], [0]
    )
    new_gateup_first, new_gateup_second, gateup_sums = step_call(
        "gateup_step", stacked_step, place, *own_grads(gateup_own), [gateup], [2]
    )
    early = named("early_sums", total, jnp.concatenate([gateup_sums, down_sums], 0))
    new_gateup, new_down = apply_call(
        "gateup_down",
        early,
        [
            (new_gateup_first, new_gateup_second, gateup_weight),
            (new_down_first, new_down_second, down_weight),
        ],
        ((0, 2), (8,)),
        (1, 0),
        4,
    )
    attn_own, new_gateup, new_down = together(attn_own, new_gateup, new_down)
    attn_arrays = [
        (query_first, query_second, query_weight),
        (keyval_first, keyval_second, keyval_weight),
        (output_first, output_second, output_weight),
    ]
    (
        new_query_first, new_query_second, new_keyval_first, new_keyval_second,
        new_output_first, new_output_second, attn_sums,
    ) = step_call("attention_step", attn_step, place, *own_grads(attn_own), attn_arrays, [1, 2, 0])
    late = jnp.concatenate(
        [gain_one_grad.reshape(-1, HD), gain_two_grad.reshape(-1, HD), head_gain_grad, attn_sums], 0
    )
    late = named("late_sums", total, late)
    gain_rows = norm_gains.size // HD
    new_query, new_keyval, new_output = apply_call(
        "attention",
        late[gain_rows:],
        [
            (new_query_first, new_query_second, query_weight),
            (new_keyval_first, new_keyval_second, keyval_weight),
            (new_output_first, new_output_second, output_weight),
        ],
        ((0,), (2, 4), (6,)),
        (0, 1, 0),
        2,
    )
    padded = -(-gain_rows // 8) * 8
    gain_shape = jax.ShapeDtypeStruct((padded, HD), jnp.float32)
    new_gains_first, new_gains_second, new_gains, lamb_stats, trust = pl.pallas_call(
        functools.partial(gains_kernel, gain_rows),
        out_shape=(gain_shape, gain_shape, gain_shape)
        + tuple(jax.ShapeDtypeStruct((rows, 11), jnp.float32) for rows in (2, 1)),
        name="gains",
    )(
        late,
        early,
        *[
            jnp.pad(values, (0, (padded - gain_rows) * HD)).reshape(padded, HD)
            for values in (gains_first, gains_second, norm_gains)
        ],
    )
    new_gains, new_gains_first, new_gains_second = (
        values.reshape(-1)[: norm_gains.size] for values in (new_gains, new_gains_first, new_gains_second)
    )
    trust = trust[0]
    return (
        result[None],
        input_grad[None],
        rms_values,
        new_gains,
        new_gains_first,
        new_gains_second,
        new_query,
        new_query_first,
        new_query_second,
        new_keyval,
        new_keyval_first,
        new_keyval_second,
        new_output,
        new_output_first,
        new_output_second,
        new_gateup,
        new_gateup_first,
        new_gateup_second,
        new_down,
        new_down_first,
        new_down_second,
        lamb_stats,
        trust,
    )


def solution(mesh):
    wide_size, narrow_size = mesh.devices.shape
    cube = jax.sharding.Mesh(
        mesh.devices.reshape(wide_size // 2, 2, narrow_size), ("outer", "inner", "narrow")
    )
    wide = ("outer", "inner")
    rows = P(wide, "narrow", None)
    matrix = P(wide, "narrow")
    stacked = P(None, wide, "narrow")
    turned = P("narrow", wide)
    in_specs = (rows, rows, P(wide), P(), P(), P())
    in_specs += (matrix,) * 3 + (stacked,) * 3 + (turned,) * 3 + (stacked,) * 3 + (turned,) * 3
    out_specs = (rows, rows, stacked, P(), P(), P())
    out_specs += (matrix,) * 3 + (stacked,) * 3 + (turned,) * 3 + (stacked,) * 3 + (turned,) * 3
    out_specs += (P(), P())
    return jax.shard_map(shards, mesh=cube, in_specs=in_specs, out_specs=out_specs, check_vma=False)
```

```python
import functools

import jax
import jax.numpy as jnp
from jax import lax
from jax.experimental import pallas as pl
from jax.experimental.pallas import tpu as pltpu
from jax.sharding import PartitionSpec as P

D = 2048
H = 16
KV = 8
HD = 128
STEP = 10


EPS = 1e-06
THETA = 1000000.0
BETA_ONE = 0.9
BETA_TWO = 0.999
ADAM_EPS = 1e-06
DECAY = 0.01
LEARN = 0.5

SCALE = HD ** (-0.5)
LIGHT = pl.CostEstimate(flops=1024, transcendentals=0, bytes_accessed=1024)

CHIP = ("narrow", 2)
CORE = ("narrow", 1)
PAIR = ("inner", 1)


def named(name, function, *operands):
    with jax.named_scope(name):
        return function(*operands)


def swap(values, link):
    axis, bit = link
    return lax.ppermute(values, axis, [(i, i ^ bit) for i in range(lax.axis_size(axis))])


def together(*values):
    return lax.optimization_barrier(values)


def gather_start(own):
    return together(swap(own, CHIP), swap(own, PAIR))


def gather_cross(chip, pair, split):
    if not split:
        return [swap(pair, CHIP)]
    half = pair.shape[0] // 2
    return [swap(chip[:half], PAIR), swap(pair[half:], CHIP)]


def gather_end(near):
    return list(near) + [swap(block, CORE) for block in near]


def cross_kernel(left, right, near, far):
    values = lax.dot_general(
        left[...], right[...], (((1,), (1,)), ((), ())), preferred_element_type=jnp.float32
    )

    @pl.when(pl.program_id(0) == 0)
    def _():
        far[...] = values.astype(far.dtype)

    @pl.when(pl.program_id(0) == 1)
    def _():
        near[...] = values


def cross_call(left, right, depth, place):
    rows = left.shape[0] // 8
    shape = (rows, right.shape[0])
    return pl.pallas_call(
        cross_kernel,
        out_shape=(jax.ShapeDtypeStruct(shape, jnp.float32), jax.ShapeDtypeStruct(shape, jnp.bfloat16)),
        grid=(2,),
        in_specs=[
            pl.BlockSpec((rows, depth), lambda i: (7 - 4 * i, 0)),
            pl.BlockSpec((right.shape[0], depth), lambda i: (0, place), pipeline_mode=pl.Buffered(1)),
        ],
        out_specs=(pl.BlockSpec(shape, lambda i: (0, 0)),) * 2,
        cost_estimate=LIGHT,
        name="cross",
    )(left, right)


def part_kernel(left, right, *outs):
    values = lax.dot_general(
        left[...], right[...], (((1,), (1,)), ((), ())), preferred_element_type=jnp.float32
    )
    for index, out in enumerate(outs):

        @pl.when(pl.program_id(0) == index)
        def _(out=out):
            out[...] = values.astype(out.dtype)


def near_kernel(left, right, out):
    out[...] = lax.dot_general(
        left[...], right[...], (((1,), (1,)), ((), ())), preferred_element_type=jnp.float32
    )


def near_call(left, right, depth, place):
    rows = left.shape[0] // 8
    columns = right.shape[0]
    return pl.pallas_call(
        near_kernel,
        out_shape=jax.ShapeDtypeStruct((3 * rows, columns), jnp.float32),
        grid=(3,),
        in_specs=[
            pl.BlockSpec((rows, depth), lambda i: (i, 0)),
            pl.BlockSpec((columns, depth), lambda i: (0, place), pipeline_mode=pl.Buffered(1)),
        ],
        out_specs=pl.BlockSpec((rows, columns), lambda i: (i, 0)),
        cost_estimate=LIGHT,
        name="near",
    )(left, right)


def part_call(left, right, depth, place, first, kind):
    rows = left.shape[0] // 8
    columns = right.shape[0]
    return pl.pallas_call(
        part_kernel,
        out_shape=(jax.ShapeDtypeStruct((rows, columns), kind),) * 3,
        grid=(3,),
        in_specs=[
            pl.BlockSpec((rows, depth), lambda i: (first + i, 0)),
            pl.BlockSpec((columns, depth), lambda i: (0, place), pipeline_mode=pl.Buffered(1)),
        ],
        out_specs=(pl.BlockSpec((rows, columns), lambda i: (0, 0)),) * 3,
        cost_estimate=LIGHT,
        name="part",
    )(left, right)


def partial_rows(left, right, depth, place=0):
    low = jnp.bfloat16
    near_cross, far_cross = cross_call(left, right, depth, place)
    far_cross, left = together(far_cross, left)
    rest_far = part_call(left, right, depth, place, 4, low)
    far_cross, *rest_far = together(swap(far_cross, CORE), *rest_far)
    cross = (near_cross + far_cross.astype(jnp.float32)).astype(low)
    near = near_call(left, right, depth, place)
    return (cross, near, [swap(block, CORE) for block in rest_far])


def scatter_cross(cross):
    half = cross.shape[0] // 2
    return (swap(cross[:half], PAIR), swap(cross[half:], CHIP))


def sums_kernel(near_chip, near_pair, far_chip, far_pair, from_pair, from_chip, chip, pair):
    wide = jnp.float32
    early = pl.program_id(0) < pl.num_programs(0) // 2
    left = near_chip[...] + far_chip[...].astype(wide)
    right = near_pair[...] + far_pair[...].astype(wide)
    chip[...] = jnp.where(early, left + from_pair[...].astype(wide), left).astype(chip.dtype)
    pair[...] = jnp.where(early, right, right + from_chip[...].astype(wide)).astype(pair.dtype)


def near_sums(near, far, from_pair, from_chip):
    rows, columns = far[1].shape
    steps = 4
    half = steps // 2
    block = (rows // steps, columns)
    straight = pl.BlockSpec(block, lambda i: (i, 0))
    return pl.pallas_call(
        sums_kernel,
        out_shape=(jax.ShapeDtypeStruct((rows, columns), jnp.bfloat16),) * 2,
        grid=(steps,),
        in_specs=[
            pl.BlockSpec(block, lambda i: (steps + i, 0)),
            pl.BlockSpec(block, lambda i: (2 * steps + i, 0)),
            straight,
            straight,
        ]
        + [
            pl.BlockSpec(block, lambda i: (jnp.minimum(i, half - 1), 0)),
            pl.BlockSpec(block, lambda i: (jnp.maximum(i - half, 0), 0)),
        ],
        out_specs=(straight, straight),
        cost_estimate=LIGHT,
        name="sums",
    )(near, near, far[1], far[2], from_pair, from_chip)


def scatter_near(chip, pair):
    return (swap(chip, CHIP), swap(pair, PAIR))


def all_sums(near, far, chip, pair):
    own = (near[: far[0].shape[0]] + far[0].astype(jnp.float32)).astype(jnp.bfloat16)
    return own.astype(jnp.float32) + chip.astype(jnp.float32) + pair.astype(jnp.float32)


def first_kernel(*refs):
    out = refs[-1]
    start = 0
    for left, right in zip(refs[:-1:2], refs[1:-1:2]):
        span = slice(start, start + right.shape[1])
        values = lax.dot_general(
            left[...], right[...], (((0,), (0,)), ((), ())), preferred_element_type=jnp.float32
        )
        out[:, span] = values.astype(out.dtype)
        start = span.stop


def product_first(name, *pairs, cost=LIGHT):
    rows, depth = pairs[0][0].shape
    columns = sum(right.shape[1] for _, right in pairs)
    tile = 512
    specs = []
    for _, right in pairs:
        specs.append(pl.BlockSpec((rows, tile), lambda i: (0, i)))
        specs.append(pl.BlockSpec(right.shape, lambda i: (0, 0), pipeline_mode=pl.Buffered(1)))
    return pl.pallas_call(
        first_kernel,
        out_shape=jax.ShapeDtypeStruct((depth, columns), jnp.bfloat16),
        grid=(depth // tile,),
        in_specs=specs,
        out_specs=pl.BlockSpec((tile, columns), lambda i: (i, 0)),
        cost_estimate=cost,
        name=name,
    )(*[array for pair in pairs for array in pair])


def halves(values):
    place = lax.axis_index("inner")
    size = values.shape[1] // 2
    mine = lax.dynamic_slice_in_dim(values, place * size, size, 1)
    theirs = lax.dynamic_slice_in_dim(values, (1 - place) * size, size, 1)
    return (mine, theirs)


def in_order(mine, theirs, axis):
    first = lax.axis_index("inner") == 0
    return jnp.concatenate([jnp.where(first, mine, theirs), jnp.where(first, theirs, mine)], axis)


def pair_weights(parts):
    cut = [halves(part) for part in parts]
    mine = jnp.concatenate([mine for mine, _ in cut], 1)
    theirs = jnp.concatenate([theirs for _, theirs in cut], 1)
    return (mine, theirs)


def gather_weights(mine, theirs):
    return gather_outer(in_order(mine, theirs, 0))


def own_grads(values):
    rows = values.shape[0] // 2
    place = lax.axis_index("inner")
    mine = lax.dynamic_slice_in_dim(values, place * rows, rows, 0)
    return (mine, swap(lax.dynamic_slice_in_dim(values, (1 - place) * rows, rows, 0), PAIR))


def total(values):
    for axis in ("narrow", "inner", "outer"):
        bit = 1
        while bit < lax.axis_size(axis):
            values = values + swap(values, (axis, bit))
            bit *= 2
    return values


def places_of(blocks, count):
    half = blocks.shape[1] // 2
    places = []
    for side in (0, 4):
        places += [blocks.at[side], blocks.at[side + 1], blocks.at[side + 2]]
        if count == 8:
            places += [blocks.at[side + 3]]
        else:
            places += [blocks.at[side + 3, pl.ds(0, half)], blocks.at[side + 3, pl.ds(half, half)]]
    return places


def parts_of(block, count):
    first = block % 4 + (block // 4) * (count // 2)
    return range(first, first + (count // 2 - 3 if block % 4 == 3 else 1))


def join_kernel(*refs):
    count = len(refs) - 4
    pieces = refs[:count]
    joined, blocks, arrive, leave = refs[count:]
    places = places_of(blocks, count)
    arrivals = [pltpu.make_async_copy(pieces[i], places[i], arrive.at[i]) for i in range(count)]
    departures = [pltpu.make_async_copy(blocks.at[i], joined.at[i], leave.at[i]) for i in range(8)]
    for copy in arrivals:
        copy.start()
    for block in range(8):
        for index in parts_of(block, count):
            arrivals[index].wait()
        departures[block].start()
    for copy in departures:
        copy.wait()


def join(pieces):
    rows, depth = pieces[0].shape
    anywhere = pl.BlockSpec(memory_space=pltpu.HBM)
    return pl.pallas_call(
        join_kernel,
        out_shape=jax.ShapeDtypeStruct((8, rows, depth), jnp.bfloat16),
        in_specs=[anywhere] * len(pieces),
        out_specs=anywhere,
        scratch_shapes=[
            pltpu.VMEM((8, rows, depth), jnp.bfloat16),
            pltpu.SemaphoreType.DMA((len(pieces),)),
            pltpu.SemaphoreType.DMA((8,)),
        ],
        cost_estimate=LIGHT,
        name="join",
    )(*pieces).reshape(8 * rows, depth)


def rows_kernel(finish, count, extra, results, *refs):
    pieces = refs[:count]
    weights = refs[count : count + extra]
    outputs = refs[count + extra : count + extra + results]
    joined, *beside, blocks, arrive, leave = refs[count + extra + results :]
    step = pl.program_id(0)
    places = places_of(blocks, count)

    def arrival(index):
        return pltpu.make_async_copy(pieces[index], places[index], arrive.at[index])

    def departure(block):
        return pltpu.make_async_copy(blocks.at[block], joined.at[block], leave.at[block])

    def beside_copies():
        if not beside:
            return []
        width = weights[0].shape[1]
        return [
            pltpu.make_async_copy(weight, beside[0].at[:, pl.ds(i * width, width)], leave.at[8 + i])
            for i, weight in enumerate(weights)
        ]

    @pl.when(step == 0)
    def _():
        for index in range(count):
            arrival(index).start()
        for copy in beside_copies():
            copy.start()

    for block in range(8):

        @pl.when(step == block)
        def _(block=block):
            for index in parts_of(block, count):
                arrival(index).wait()
            departure(block).start()

    finish(blocks[step], weights, (), outputs)

    @pl.when(step == 7)
    def _():
        for block in range(8):
            departure(block).wait()
        for copy in beside_copies():
            copy.wait()


def rows_call(name, finish, pieces, weights, widths, kinds, columns=None, place=0):
    rows, depth = pieces[0].shape
    columns = columns or weights[0].shape[1]
    beside = (depth, len(weights) * columns)

    def block(width):
        return pl.BlockSpec((None, rows, width), lambda i: (i, 0, 0))

    anywhere = pl.BlockSpec(memory_space=pltpu.HBM)
    more = len(weights) > 1
    results = pl.pallas_call(
        functools.partial(rows_kernel, finish, len(pieces), len(weights), len(widths)),
        out_shape=tuple(
            jax.ShapeDtypeStruct((8, rows, width), kind) for width, kind in zip(widths, kinds)
        )
        + (jax.ShapeDtypeStruct((8, rows, depth), jnp.bfloat16),)
        + (jax.ShapeDtypeStruct(beside, jnp.bfloat16),) * more,
        grid=(8,),
        in_specs=[anywhere] * len(pieces)
        + [pl.BlockSpec((depth, columns), lambda i: (0, place), pipeline_mode=pl.Buffered(1))]
        * len(weights),
        out_specs=tuple(block(width) for width in widths) + (anywhere,) * (1 + more),
        scratch_shapes=[
            pltpu.VMEM((8, rows, depth), jnp.bfloat16),
            pltpu.SemaphoreType.DMA((len(pieces),)),
            pltpu.SemaphoreType.DMA((8 + len(weights),)),
        ],
        cost_estimate=LIGHT,
        name=name,
    )(*pieces, *weights)
    count = len(widths) + 1
    return [result.reshape(8 * rows, result.shape[-1]) for result in results[:count]] + list(results[count:])


def blocks_kernel(finish, left, weight, *refs):
    finish(left[...], (weight,), refs[:-1], refs[-1:])


def blocks_call(name, finish, left, weight, operands, width, rows):
    depth, columns = weight.shape
    count = left.shape[0] // rows

    def block(size):
        return pl.BlockSpec((rows, size), lambda i: (i, 0))

    return pl.pallas_call(
        functools.partial(blocks_kernel, finish),
        out_shape=jax.ShapeDtypeStruct((left.shape[0], width), jnp.bfloat16),
        grid=(count,),
        in_specs=[block(depth), pl.BlockSpec(weight.shape, lambda i: (0, 0), pipeline_mode=pl.Buffered(1))]
        + [block(operand.shape[1]) for operand in operands],
        out_specs=block(width),
        cost_estimate=LIGHT,
        name=name,
    )(left, weight, *operands)


def product(left, right):
    return jnp.dot(left, right, preferred_element_type=jnp.float32)


def plain_finish(left, weights, operands, outputs):
    outputs[0][...] = product(left, weights[0][...]).astype(outputs[0].dtype)


def tiles_of(size):
    return [slice(start, start + 256) for start in range(0, size, 256)]


def gate_finish(left, weights, operands, outputs):
    both, hidden = outputs
    size = hidden.shape[1]
    for tile in tiles_of(size):
        up_tile = slice(size + tile.start, size + tile.stop)
        gate_val = product(left, weights[0][:, tile])
        up_val = product(left, weights[0][:, up_tile])
        both[:, tile] = gate_val.astype(both.dtype)
        both[:, up_tile] = up_val.astype(both.dtype)
        hidden[:, tile] = (gate_val * jax.nn.sigmoid(gate_val) * up_val).astype(hidden.dtype)


def hidden_finish(left, weights, operands, outputs):
    (both,) = operands
    (grads,) = outputs
    size = both.shape[1] // 2
    for tile in tiles_of(size):
        up_tile = slice(size + tile.start, size + tile.stop)
        hidden_grad = product(left, weights[0][:, tile])
        gate_val = both[:, tile].astype(jnp.float32)
        up_val = both[:, up_tile].astype(jnp.float32)
        sigmoid = jax.nn.sigmoid(gate_val)
        slope = sigmoid * (1.0 + gate_val * (1.0 - sigmoid))
        grads[:, tile] = (hidden_grad * up_val * slope).astype(grads.dtype)
        grads[:, up_tile] = (hidden_grad * (gate_val * sigmoid)).astype(grads.dtype)


def rope_tables(length):
    places = jnp.arange(length, dtype=jnp.float32)
    frequency = THETA ** (-jnp.arange(HD // 2, dtype=jnp.float32) * 2.0 / HD)
    angles = places[:, None] * frequency[None, :]
    cos_table = jnp.cos(angles)
    sin_table = jnp.sin(angles)
    return (
        jnp.concatenate([cos_table, cos_table], 1),
        jnp.concatenate([-sin_table, sin_table], 1),
    )


def unit_of(raw):
    inverse = lax.rsqrt(jnp.mean(raw * raw, -1, keepdims=True) + EPS)
    return (raw * inverse, inverse)


def turn(values, cos_table, sin_table):
    return values * cos_table + pltpu.roll(values, HD // 2, 1) * sin_table


def place_of(meta, block):
    relative = jnp.bitwise_xor(meta[0], block)
    return (jnp.bitwise_and(relative, 1), lax.shift_right_logical(relative, 1))


def load_heads(meta, raw, gains, cos_ref, sin_ref, queries, keys, values, rows, blocks, heads):
    gain_query = gains[0:1, :]
    gain_key = gains[1:2, :]
    for block in range(blocks):
        core, chip = place_of(meta, block)
        span = slice(block * rows, (block + 1) * rows)
        tile = raw[core, chip]
        cos_table = cos_ref[span, :]
        sin_table = sin_ref[span, :]
        for head in range(heads):
            unit, _ = unit_of(tile[:, head * HD : (head + 1) * HD])
            queries[head, span, :] = turn(unit * gain_query, cos_table, sin_table).astype(jnp.bfloat16)
        unit, _ = unit_of(tile[:, heads * HD : (heads + 1) * HD])
        keys[span, :] = turn(unit * gain_key, cos_table, sin_table).astype(jnp.bfloat16)
        values[span, :] = tile[:, (heads + 1) * HD :].astype(jnp.bfloat16)


def weights_of(left, right, start, valid_len, key_axis):
    scores = lax.dot_general(left, right, (((1,), (1,)), ((), ())), preferred_element_type=jnp.float32)
    query_place = start + lax.broadcasted_iota(jnp.int32, scores.shape, 1 - key_axis)
    key_place = lax.broadcasted_iota(jnp.int32, scores.shape, key_axis)
    allowed = (key_place <= query_place) & (key_place < valid_len)
    return jnp.where(allowed, jnp.exp(scores * SCALE), 0.0)


def forward_kernel(rows, blocks, heads, meta, raw, gains, cos_ref, sin_ref, context, queries, keys, values):
    load_heads(meta, raw, gains, cos_ref, sin_ref, queries, keys, values, rows, blocks, heads)
    valid_len = meta[1 + pl.program_id(0)]
    for block in range(blocks):
        core, chip = place_of(meta, block)
        seen = (block + 1) * rows
        for head in range(heads):
            query = queries[head, block * rows : seen, :]
            weights = weights_of(query, keys[:seen, :], block * rows, valid_len, 1)
            inverse = 1.0 / jnp.sum(weights, -1, keepdims=True)
            part = jnp.dot(
                weights.astype(jnp.bfloat16), values[:seen, :], preferred_element_type=jnp.float32
            )
            context[core, chip, :, head * HD : (head + 1) * HD] = (part * inverse).astype(jnp.bfloat16)


def backward_kernel(
    rows, blocks, heads, meta, raw, context_grad, gains, cos_ref, sin_ref,
    raw_grad, gain_grad, queries, keys, values, key_grad, value_grad, query_grad,
):
    load_heads(meta, raw, gains, cos_ref, sin_ref, queries, keys, values, rows, blocks, heads)
    valid_len = meta[1 + pl.program_id(0)]
    key_grad[...] = jnp.zeros_like(key_grad)
    value_grad[...] = jnp.zeros_like(value_grad)
    first = (((0,), (0,)), ((), ()))
    last = (((1,), (1,)), ((), ()))
    for block in range(blocks):
        core, chip = place_of(meta, block)
        seen = (block + 1) * rows
        for head in range(heads):
            query = queries[head, block * rows : seen, :]
            grad = context_grad[core, chip, :, head * HD : (head + 1) * HD]
            weights = weights_of(keys[:seen, :], query, block * rows, valid_len, 0)
            probability = weights * (1.0 / jnp.sum(weights, 0, keepdims=True))
            value_grad[:seen, :] += jnp.dot(
                probability.astype(jnp.bfloat16), grad, preferred_element_type=jnp.float32
            )
            prob_grad = lax.dot_general(values[:seen, :], grad, last, preferred_element_type=jnp.float32)
            inner = jnp.sum(probability * prob_grad, 0, keepdims=True)
            score_grad = (probability * (prob_grad - inner)).astype(jnp.bfloat16)
            query_grad[head, block * rows : seen, :] = SCALE * lax.dot_general(
                score_grad, keys[:seen, :], first, preferred_element_type=jnp.float32
            )
            key_grad[:seen, :] += SCALE * jnp.dot(score_grad, query, preferred_element_type=jnp.float32)
    query_total = jnp.zeros((1, HD), jnp.float32)
    key_total = jnp.zeros((1, HD), jnp.float32)
    for block in range(blocks):
        core, chip = place_of(meta, block)
        span = slice(block * rows, (block + 1) * rows)
        cos_table = cos_ref[span, :]
        sin_table = sin_ref[span, :]

        def back(raw_values, turned, gain):
            unit, inverse = unit_of(raw_values)
            scaled = turn(turned, cos_table, -sin_table)
            total = jnp.sum(scaled * unit, 0, keepdims=True)
            scaled = scaled * gain
            result = inverse * (scaled - unit * jnp.mean(scaled * unit, -1, keepdims=True))
            return (result.astype(jnp.bfloat16), total)

        for head in range(heads):
            columns = slice(head * HD, (head + 1) * HD)
            result, total = back(raw[core, chip, :, columns], query_grad[head, span, :], gains[0:1, :])
            raw_grad[core, chip, :, columns] = result
            query_total += total
        columns = slice(heads * HD, (heads + 1) * HD)
        result, total = back(raw[core, chip, :, columns], key_grad[span, :], gains[1:2, :])
        raw_grad[core, chip, :, columns] = result
        key_total += total
        raw_grad[core, chip, :, (heads + 1) * HD :] = value_grad[span, :].astype(jnp.bfloat16)
    gain_grad[0:1, :] = query_total
    gain_grad[1:2, :] = key_total


def row_blocks(rows, columns):
    return pl.BlockSpec((2, None, 2, rows, columns), lambda s, meta: (0, s, 0, 0, 0))


def whole(shape):
    return pl.BlockSpec(shape, lambda s, meta: (0,) * len(shape))


def split_rows(values, rows):
    return values.reshape(2, 2, 2, rows, values.shape[-1])


def attend_forward(meta, raw, gains, cos_table, sin_table):
    length = cos_table.shape[0]
    rows = raw.shape[0] // 8
    blocks = length // rows
    heads = raw.shape[1] // HD - 2
    result = pl.pallas_call(
        functools.partial(forward_kernel, rows, blocks, heads),
        out_shape=jax.ShapeDtypeStruct((2, 2, 2, rows, heads * HD), jnp.bfloat16),
        grid_spec=pltpu.PrefetchScalarGridSpec(
            num_scalar_prefetch=1,
            grid=(2,),
            in_specs=[
                row_blocks(rows, raw.shape[1]),
                whole((2, HD)),
                whole((length, HD)),
                whole((length, HD)),
            ],
            out_specs=row_blocks(rows, heads * HD),
            scratch_shapes=[
                pltpu.VMEM((heads, length, HD), jnp.bfloat16),
                pltpu.VMEM((length, HD), jnp.bfloat16),
                pltpu.VMEM((length, HD), jnp.bfloat16),
            ],
        ),
        cost_estimate=LIGHT,
        name="attend_forward",
    )(meta, split_rows(raw, rows), gains, cos_table, sin_table)
    return result.reshape(8 * rows, heads * HD)


def attend_backward(meta, raw, context_grad, gains, cos_table, sin_table):
    length = cos_table.shape[0]
    rows = raw.shape[0] // 8
    blocks = length // rows
    width = raw.shape[1]
    heads = width // HD - 2
    raw_grad, gain_grad = pl.pallas_call(
        functools.partial(backward_kernel, rows, blocks, heads),
        out_shape=(
            jax.ShapeDtypeStruct((2, 2, 2, rows, width), jnp.bfloat16),
            jax.ShapeDtypeStruct((2, 2, HD), jnp.float32),
        ),
        grid_spec=pltpu.PrefetchScalarGridSpec(
            num_scalar_prefetch=1,
            grid=(2,),
            in_specs=[
                row_blocks(rows, width),
                row_blocks(rows, heads * HD),
                whole((2, HD)),
                whole((length, HD)),
                whole((length, HD)),
            ],
            out_specs=(
                row_blocks(rows, width),
                pl.BlockSpec((None, 2, HD), lambda s, meta: (s, 0, 0)),
            ),
            scratch_shapes=[
                pltpu.VMEM((heads, length, HD), jnp.bfloat16),
                pltpu.VMEM((length, HD), jnp.bfloat16),
                pltpu.VMEM((length, HD), jnp.bfloat16),
                pltpu.VMEM((length, HD), jnp.float32),
                pltpu.VMEM((length, HD), jnp.float32),
                pltpu.VMEM((heads, length, HD), jnp.float32),
            ],
        ),
        cost_estimate=LIGHT,
        name="attend_backward",
    )(meta, split_rows(raw, rows), split_rows(context_grad, rows), gains, cos_table, sin_table)
    return (raw_grad.reshape(8 * rows, width), jnp.sum(gain_grad, 0))


def norm_back(normed_grad, hat_values, inverse, gain_vector):
    gain_grad = jnp.sum(normed_grad * hat_values, axis=0)
    scaled = normed_grad * gain_vector
    return (
        inverse * (scaled - hat_values * jnp.mean(scaled * hat_values, -1, keepdims=True)),
        gain_grad,
    )


def moments(gradient, moment_one, moment_two):
    new_one = BETA_ONE * moment_one + (1.0 - BETA_ONE) * gradient
    new_two = BETA_TWO * moment_two + (1.0 - BETA_TWO) * gradient * gradient
    return (new_one, new_two)


def update_of(new_one, new_two, master):
    return (
        new_one / (1.0 - BETA_ONE**STEP) / (jnp.sqrt(new_two / (1.0 - BETA_TWO**STEP)) + ADAM_EPS)
        + DECAY * master
    )


def square(values):
    return jnp.sum(jnp.sum(values * values, 1, keepdims=True), 0, keepdims=True)


def step_part(gradient, span, arrays, results):
    one, two, master = (array[span].reshape(gradient.shape) for array in arrays)
    new_one, new_two = moments(gradient, one, two)
    update = update_of(new_one, new_two, master)
    for result, values in zip(results, (new_one, new_two, update)):
        result[span] = values.reshape(result[span].shape)
    return (square(master), square(update))


def put_sums(sums, pairs, first):
    row = lax.broadcasted_iota(jnp.int32, sums.shape, 0)
    tile = jnp.zeros(sums.shape, jnp.float32)
    for index, value in enumerate(pairs):
        tile = jnp.where(row == index, value, tile)
    sums[...] = tile + jnp.where(first, 0.0, sums[...])


def add_pairs(left, right):
    return (left[0] + right[0], left[1] + right[1])


def stacked_step(meta, mine, other, one, two, master, new_one, new_two, update, sums):
    step = pl.program_id(0)
    size = one.shape[2]
    pairs = []
    for side in range(2):
        columns = slice(side * size, (side + 1) * size)
        own = step == meta[0]
        gradient = jnp.where(own, mine[:, columns], other[:, columns]).astype(jnp.float32)
        pairs += step_part(gradient, (side,), (one, two, master), (new_one, new_two, update))
    put_sums(sums, pairs, step == 0)


def turned_step(meta, mine, other, one, two, master, new_one, new_two, update, sums):
    step = pl.program_id(0)
    gradient = jnp.where(step == meta[0], mine[...], other[...]).astype(jnp.float32).T
    pair = step_part(gradient, (slice(None),), (one, two, master), (new_one, new_two, update))
    put_sums(sums, pair, step == 0)


def attn_step(
    meta, mine, other, query_one, query_two, query, keyval_one, keyval_two, keyval,
    output_one, output_two, output, new_query_one, new_query_two, query_update,
    new_keyval_one, new_keyval_two, keyval_update, new_output_one, new_output_two, output_update, sums,
):
    step = pl.program_id(0)
    own = step == meta[0]
    width = query.shape[1]
    key_width = keyval.shape[2]

    def part(first, size):
        columns = slice(first, first + size)
        return jnp.where(own, mine[:, columns], other[:, columns]).astype(jnp.float32)

    whole_span = (slice(None),)
    pairs = []
    pairs += step_part(part(0, width), whole_span, (query_one, query_two, query), (new_query_one, new_query_two, query_update))
    for side in range(2):
        pairs += step_part(
            part(width + side * key_width, key_width), (side,),
            (keyval_one, keyval_two, keyval), (new_keyval_one, new_keyval_two, keyval_update),
        )
    pairs += step_part(
        part(width + 2 * key_width, mine.shape[1] - width - 2 * key_width).T, whole_span,
        (output_one, output_two, output), (new_output_one, new_output_two, output_update),
    )
    put_sums(sums, pairs, step == 0)


def half_block(array, axis):
    shape = tuple(size // 2 if place == axis else size for place, size in enumerate(array.shape))
    return pl.BlockSpec(shape, lambda i, meta: tuple(i if place == axis else 0 for place in range(len(shape))))


def step_call(name, kernel, place, mine, other, arrays, axes):
    fixed = pl.BlockSpec(mine.shape, lambda i, meta: (0, 0))
    specs = [half_block(array, axis) for group, axis in zip(arrays, axes) for array in group]
    out_arrays = [(array, axis) for group, axis in zip(arrays, axes) for array in group]
    return pl.pallas_call(
        kernel,
        out_shape=tuple(jax.ShapeDtypeStruct(array.shape, jnp.float32) for array, _ in out_arrays)
        + (jax.ShapeDtypeStruct((8, HD), jnp.float32),),
        grid_spec=pltpu.PrefetchScalarGridSpec(
            num_scalar_prefetch=1,
            grid=(2,),
            in_specs=[fixed, fixed] + specs,
            out_specs=tuple(half_block(array, axis) for array, axis in out_arrays)
            + (pl.BlockSpec((8, HD), lambda i, meta: (0, 0)),),
        ),
        cost_estimate=LIGHT,
        name=name,
    )(place, mine, other, *[array for group in arrays for array in group])


def ratio_of(weight_square, update_square):
    return jnp.sqrt(weight_square) / jnp.sqrt(update_square)


def apply_kernel(parts, axes, *refs):
    sums = refs[0]
    count = len(parts)
    for place, rows in enumerate(parts):
        update, master = refs[1 + 2 * place : 3 + 2 * place]
        result = refs[1 + 2 * count + place]
        for side, row in enumerate(rows):
            span = (side,) if len(rows) > 1 else (slice(None),)
            trust = ratio_of(sums[row : row + 1, 0:1], sums[row + 1 : row + 2, 0:1])
            result[span] = master[span] - LEARN * trust * update[span]


def apply_call(name, sums, arrays, parts, axes, steps):
    def block(array, axis):
        shape = tuple(size // steps if place == axis else size for place, size in enumerate(array.shape))
        return pl.BlockSpec(shape, lambda i: tuple(i if place == axis else 0 for place in range(len(shape))))

    return pl.pallas_call(
        functools.partial(apply_kernel, parts, axes),
        out_shape=tuple(jax.ShapeDtypeStruct(group[1].shape, jnp.float32) for group in arrays),
        grid=(steps,),
        in_specs=[pl.BlockSpec(sums.shape, lambda i: (0, 0))]
        + [block(array, axis) for group, axis in zip(arrays, axes) for array in group],
        out_specs=tuple(block(group[1], axis) for group, axis in zip(arrays, axes)),
        cost_estimate=LIGHT,
        name=name,
    )(sums, *[array for group in arrays for array in group])


def gains_kernel(rows, sums, first, second, gains, new_first, new_second, new_gains, stats, trust):
    each = (rows - 2) // 2
    new_one, new_two = moments(sums[24 : 24 + rows, :], first[:rows, :], second[:rows, :])
    for result, values in ((new_first, new_one), (new_second, new_two), (new_gains, new_one)):
        result[:rows, :] = values
        result[rows:, :] = jnp.zeros_like(result[rows:, :])
    lane = lax.broadcasted_iota(jnp.int32, (1, HD), 1)
    weight_row = jnp.zeros((1, HD), jnp.float32)
    update_row = jnp.zeros((1, HD), jnp.float32)

    def put(place, weight_square, update_square, weight_row, update_row):
        return (
            jnp.where(lane == place, jnp.sqrt(weight_square), weight_row),
            jnp.where(lane == place, jnp.sqrt(update_square), update_row),
        )

    for place, start, size in ((0, 0, each), (7, each, each), (4, 2 * each, 1), (5, 2 * each + 1, 1)):
        span = slice(start, start + size)
        old = gains[span, :]
        update = update_of(new_one[span, :], new_two[span, :], old)
        weight_square, update_square = (square(old), square(update))
        new_gains[span, :] = old - LEARN * ratio_of(weight_square, update_square) * update
        weight_row, update_row = put(place, weight_square, update_square, weight_row, update_row)
    for place, index in ((1, 16), (2, 18), (3, 20), (6, 22), (8, 0), (9, 2), (10, 8)):
        weight_row, update_row = put(
            place, sums[index : index + 1, 0:1], sums[index + 1 : index + 2, 0:1], weight_row, update_row
        )
    stats[0:1, :] = weight_row[:, :11]
    stats[1:2, :] = update_row[:, :11]
    trust[...] = (weight_row / jnp.where(lane < 11, update_row, 1.0))[:, :11]


def root_mean(values):
    return jnp.sqrt(jnp.mean(values * values, -1))


def gather_outer(values):
    return lax.all_gather(values, "outer", axis=0, tiled=True)


def scatter_outer(values):
    return lax.psum_scatter(values, "outer", scatter_dimension=0, tiled=True)


def shards(
    tokens,
    cotangent,
    lengths,
    norm_gains,
    gains_first,
    gains_second,
    query_weight,
    query_first,
    query_second,
    keyval_weight,
    keyval_first,
    keyval_second,
    output_weight,
    output_first,
    output_second,
    gateup_weight,
    gateup_first,
    gateup_second,
    down_weight,
    down_first,
    down_second,
):
    low = jnp.bfloat16
    shard_len = tokens.shape[1]
    narrow_size = lax.axis_size("narrow")
    outer_size = lax.axis_size("outer")
    seq_len = shard_len * narrow_size
    gain_one = norm_gains[:D]
    gain_two = norm_gains[D : 2 * D]
    head_gains = norm_gains[2 * D :].reshape(2, HD)
    cos_table, sin_table = rope_tables(seq_len)

    residual = tokens[0].astype(jnp.float32)
    inv_one = lax.rsqrt(jnp.mean(residual * residual, -1, keepdims=True) + EPS)
    hat_one = residual * inv_one
    normed = (hat_one * gain_one).astype(low)

    query_half = query_weight.shape[1] // 2
    key_half = keyval_weight.shape[2] // 2
    output_half = output_weight.shape[0] // 2
    hidden_size = down_weight.shape[0] // 2
    raw_width = query_half + 2 * key_half
    places = lax.axis_index("narrow") * shard_len + jnp.arange(shard_len, dtype=jnp.int32)
    valid = (places < lengths[0]).astype(jnp.float32)
    grad_out = cotangent[0].astype(jnp.float32) * valid[:, None]
    attn_low = [w.astype(low) for w in (query_weight, keyval_weight[0], keyval_weight[1])]
    mine, theirs = pair_weights(attn_low + [output_weight.astype(low).T])
    full_attn = gather_weights(mine, swap(theirs, PAIR))

    chip, pair = named("norm_one", gather_start, normed)
    gateup_mine, gateup_theirs = pair_weights(
        [gateup_weight[0].astype(low), gateup_weight[1].astype(low), down_weight.astype(low).T]
    )
    meta = jnp.concatenate(
        [lax.axis_index("narrow").astype(jnp.int32)[None], lengths, swap(lengths, PAIR)]
    )
    chip, pair, gateup_theirs, cos_table, sin_table, meta, head_gains = together(
        chip, pair, gateup_theirs, cos_table, sin_table, meta, head_gains
    )
    (cross,) = named("norm_one", gather_cross, chip, pair, False)
    gateup_pair = in_order(gateup_mine, swap(gateup_theirs, PAIR), 0)
    full_attn, grad_low = together(full_attn, grad_out.astype(low))
    cross, gateup_pair = together(cross, gateup_pair)
    full_gateup = gather_outer(gateup_pair[:, : 2 * hidden_size])
    full_down = gather_outer(gateup_pair[:, 2 * hidden_size :])
    grad_chip, grad_pair = named("output_grad", gather_start, grad_low)
    pieces_one = named("norm_one", gather_end, (normed, chip, pair, cross))
    raw, whole_one = rows_call(
        "query_key_value", plain_finish, pieces_one, [full_attn], [raw_width], [jnp.float32], raw_width
    )
    context = attend_forward(meta, raw, head_gains, cos_table, sin_table)
    context, grad_chip, grad_pair = together(context, grad_chip, grad_pair)

    cross, near, far = named(
        "attention_out", partial_rows, context, full_attn, output_half, raw_width // output_half
    )
    moved = named("attention_out", scatter_cross, cross)
    near, far[0], from_pair, from_chip = together(near, far[0], *moved)
    chip, pair = named("attention_out", near_sums, near, far, from_pair, from_chip)
    chip, pair = named("attention_out", scatter_near, chip, pair)
    attn_part = all_sums(near, far, chip, pair)
    middle = residual + attn_part
    inv_two = lax.rsqrt(jnp.mean(middle * middle, -1, keepdims=True) + EPS)
    hat_two = middle * inv_two
    normed = (hat_two * gain_two).astype(low)
    chip, pair = named("norm_two", gather_start, normed)
    cross = named("norm_two", gather_cross, chip, pair, True)
    *cross, grad_chip, grad_pair = together(*cross, grad_chip, grad_pair)
    pieces_two = named("norm_two", gather_end, (normed, chip, pair, *cross))
    grad_cross = named("output_grad", gather_cross, grad_chip, grad_pair, True)
    both, hidden, whole_two = rows_call(
        "gate_up", gate_finish, pieces_two, [full_gateup], [2 * hidden_size, hidden_size], [low, low],
    )
    hidden, *grad_cross = together(hidden, *grad_cross)
    whole_grad = join(
        named("output_grad", gather_end, (grad_low, grad_chip, grad_pair, *grad_cross))
    )
    down_grad = product_first("down_weight_grad", (whole_grad, hidden))
    full_down, down_grad = together(full_down, down_grad)
    down_own = scatter_outer(down_grad)
    pair_grad = blocks_call(
        "hidden_grad", hidden_finish, whole_grad, full_down, [both], 2 * hidden_size, shard_len
    )
    cross, near, far = named("norm_two_grad", partial_rows, pair_grad, full_gateup, 2 * hidden_size)
    moved = named("norm_two_grad", scatter_cross, cross)
    near, far[0], from_pair, from_chip = together(near, far[0], *moved)
    chip, pair = named("norm_two_grad", near_sums, near, far, from_pair, from_chip)
    chip, pair, pair_grad = together(chip, pair, pair_grad)
    chip, pair = named("norm_two_grad", scatter_near, chip, pair)
    gateup_grad = product_first(
        "gateup_weight_grad",
        (whole_two, pair_grad),
        cost=pl.CostEstimate(
            flops=2 * whole_two.size * pair_grad.shape[1], transcendentals=0, bytes_accessed=2 * whole_two.size
        ),
    )
    chip, pair, down_own, gateup_grad = together(chip, pair, down_own, gateup_grad)
    gateup_own = scatter_outer(gateup_grad)
    normed_two = all_sums(near, far, chip, pair)
    middle_norm, gain_two_grad = norm_back(normed_two, hat_two, inv_two, gain_two)
    middle_grad = grad_out + middle_norm
    down_mine, down_other = own_grads(down_own)
    middle_low, down_other = together(middle_grad.astype(low), down_other)
    chip, pair = named("middle_grad", gather_start, middle_low)
    cross = named("middle_grad", gather_cross, chip, pair, True)
    hidden, middle_low = together(hidden, middle_low)
    mlp_cross, mlp_near, mlp_far = named("mlp_out", partial_rows, hidden, full_down, hidden_size)
    *cross, mlp_cross, mlp_near = together(*cross, mlp_cross, mlp_near)
    pieces_mid = named("middle_grad", gather_end, (middle_low, chip, pair, *cross))
    context_grad, whole_mid = rows_call(
        "context_grad", plain_finish, pieces_mid, [full_attn], [output_half], [low],
        output_half, raw_width // output_half,
    )
    moved = named("mlp_out", scatter_cross, mlp_cross)
    mlp_chip, mlp_pair = named("mlp_out", near_sums, mlp_near, mlp_far, *moved)
    context_grad, mlp_chip, mlp_pair = together(context_grad, mlp_chip, mlp_pair)
    mlp_chip, mlp_pair = named("mlp_out", scatter_near, mlp_chip, mlp_pair)
    raw_grad, head_gain_grad = attend_backward(meta, raw, context_grad, head_gains, cos_table, sin_table)
    raw_grad, mlp_chip, mlp_pair = together(raw_grad, mlp_chip, mlp_pair)
    mlp_part = all_sums(mlp_near, mlp_far, mlp_chip, mlp_pair)
    attn_grad = product_first("attention_weight_grad", (whole_one, raw_grad), (whole_mid, context))
    attn_own = scatter_outer(attn_grad)
    gateup_mine, gateup_other = own_grads(gateup_own)
    place = lax.axis_index("inner").astype(jnp.int32)[None]
    down = (down_first, down_second, down_weight)
    gateup = (gateup_first, gateup_second, gateup_weight)
    cross, near, far = named("norm_one_grad", partial_rows, raw_grad, full_attn, raw_width)
    cross, gateup_other = together(cross, gateup_other)
    moved = named("norm_one_grad", scatter_cross, cross)
    near, far[0], from_pair, from_chip = together(near, far[0], *moved)
    chip, pair = named("norm_one_grad", near_sums, near, far, from_pair, from_chip)
    chip, pair = named("norm_one_grad", scatter_near, chip, pair)
    new_down_first, new_down_second, down_update, down_sums = step_call(
        "down_step", turned_step, place, down_mine, down_other, [down], [0]
    )
    new_gateup_first, new_gateup_second, gateup_update, gateup_sums = step_call(
        "gateup_step", stacked_step, place, gateup_mine, gateup_other, [gateup], [2]
    )
    final = middle + mlp_part
    result = final.astype(low)
    rms_values = jnp.stack([root_mean(attn_part), root_mean(mlp_part), root_mean(final)])[:, None, :]
    attn_own, result, rms_values, gain_two_grad = together(attn_own, result, rms_values, gain_two_grad)
    attn_mine, attn_other = own_grads(attn_own)
    chip, pair, gateup_sums, down_sums, attn_other = together(
        chip, pair, gateup_sums, down_sums, attn_other
    )
    normed_one = all_sums(near, far, chip, pair)
    input_norm, gain_one_grad = norm_back(normed_one, hat_one, inv_one, gain_one)
    input_grad = (middle_grad + input_norm).astype(low)

    attn_arrays = [
        (query_first, query_second, query_weight),
        (keyval_first, keyval_second, keyval_weight),
        (output_first, output_second, output_weight),
    ]
    (
        new_query_first, new_query_second, query_update, new_keyval_first, new_keyval_second,
        keyval_update, new_output_first, new_output_second, output_update, attn_sums,
    ) = step_call("attention_step", attn_step, place, attn_mine, attn_other, attn_arrays, [1, 2, 0])
    sums = jnp.concatenate(
        [gateup_sums, down_sums, attn_sums]
        + [gain_one_grad.reshape(-1, HD), gain_two_grad.reshape(-1, HD), head_gain_grad],
        0,
    )
    sums = named("all_sums", total, sums)
    matrix_sums = sums[:24]
    gain_rows = norm_gains.size // HD
    new_query, new_keyval, new_output = apply_call(
        "attention",
        matrix_sums,
        [(query_update, query_weight), (keyval_update, keyval_weight), (output_update, output_weight)],
        ((16,), (18, 20), (22,)),
        (0, 1, 0),
        2,
    )
    new_gateup, new_down = apply_call(
        "gateup_down",
        matrix_sums,
        [(gateup_update, gateup_weight), (down_update, down_weight)],
        ((0, 2), (8,)),
        (1, 0),
        4,
    )
    padded = -(-gain_rows // 8) * 8
    gain_shape = jax.ShapeDtypeStruct((padded, HD), jnp.float32)
    new_gains_first, new_gains_second, new_gains, lamb_stats, trust = pl.pallas_call(
        functools.partial(gains_kernel, gain_rows),
        out_shape=(gain_shape, gain_shape, gain_shape)
        + tuple(jax.ShapeDtypeStruct((rows, 11), jnp.float32) for rows in (2, 1)),
        name="gains",
    )(
        sums,
        *[
            jnp.pad(values, (0, (padded - gain_rows) * HD)).reshape(padded, HD)
            for values in (gains_first, gains_second, norm_gains)
        ],
    )
    new_gains, new_gains_first, new_gains_second = (
        values.reshape(-1)[: norm_gains.size] for values in (new_gains, new_gains_first, new_gains_second)
    )
    trust = trust[0]
    return (
        result[None],
        input_grad[None],
        rms_values,
        new_gains,
        new_gains_first,
        new_gains_second,
        new_query,
        new_query_first,
        new_query_second,
        new_keyval,
        new_keyval_first,
        new_keyval_second,
        new_output,
        new_output_first,
        new_output_second,
        new_gateup,
        new_gateup_first,
        new_gateup_second,
        new_down,
        new_down_first,
        new_down_second,
        lamb_stats,
        trust,
    )


def solution(mesh):
    wide_size, narrow_size = mesh.devices.shape
    cube = jax.sharding.Mesh(
        mesh.devices.reshape(wide_size // 2, 2, narrow_size), ("outer", "inner", "narrow")
    )
    wide = ("outer", "inner")
    rows = P(wide, "narrow", None)
    matrix = P(wide, "narrow")
    stacked = P(None, wide, "narrow")
    turned = P("narrow", wide)
    in_specs = (rows, rows, P(wide), P(), P(), P())
    in_specs += (matrix,) * 3 + (stacked,) * 3 + (turned,) * 3 + (stacked,) * 3 + (turned,) * 3
    out_specs = (rows, rows, stacked, P(), P(), P())
    out_specs += (matrix,) * 3 + (stacked,) * 3 + (turned,) * 3 + (stacked,) * 3 + (turned,) * 3
    out_specs += (P(), P())
    return jax.shard_map(shards, mesh=cube, in_specs=in_specs, out_specs=out_specs, check_vma=False)
```

```python
import functools

import jax
import jax.numpy as jnp
from jax import lax
from jax.experimental import pallas as pl
from jax.experimental.pallas import tpu as pltpu
from jax.sharding import PartitionSpec as P

D = 2048
H = 16
KV = 8
HD = 128
STEP = 10


EPS = 1e-06
THETA = 1000000.0
BETA_ONE = 0.9
BETA_TWO = 0.999
ADAM_EPS = 1e-06
DECAY = 0.01
LEARN = 0.5

SCALE = HD ** (-0.5)
LIGHT = pl.CostEstimate(flops=1024, transcendentals=0, bytes_accessed=1024)

CHIP = ("narrow", 2)
CORE = ("narrow", 1)
PAIR = ("inner", 1)


def named(name, function, *operands):
    with jax.named_scope(name):
        return function(*operands)


def swap(values, link):
    axis, bit = link
    return lax.ppermute(values, axis, [(i, i ^ bit) for i in range(lax.axis_size(axis))])


def together(*values):
    return lax.optimization_barrier(values)


def gather_start(own):
    return together(swap(own, CHIP), swap(own, PAIR))


def gather_cross(chip, pair, split):
    if not split:
        return [swap(pair, CHIP)]
    half = pair.shape[0] // 2
    return [swap(chip[:half], PAIR), swap(pair[half:], CHIP)]


def gather_end(near):
    return list(near) + [swap(block, CORE) for block in near]


def cross_kernel(left, right, near, far):
    values = lax.dot_general(
        left[...], right[...], (((1,), (1,)), ((), ())), preferred_element_type=jnp.float32
    )

    @pl.when(pl.program_id(0) == 0)
    def _():
        far[...] = values.astype(far.dtype)

    @pl.when(pl.program_id(0) == 1)
    def _():
        near[...] = values


def cross_call(left, right, depth, place):
    rows = left.shape[0] // 8
    shape = (rows, right.shape[0])
    return pl.pallas_call(
        cross_kernel,
        out_shape=(jax.ShapeDtypeStruct(shape, jnp.float32), jax.ShapeDtypeStruct(shape, jnp.bfloat16)),
        grid=(2,),
        in_specs=[
            pl.BlockSpec((rows, depth), lambda i: (7 - 4 * i, 0)),
            pl.BlockSpec((right.shape[0], depth), lambda i: (0, place), pipeline_mode=pl.Buffered(1)),
        ],
        out_specs=(pl.BlockSpec(shape, lambda i: (0, 0)),) * 2,
        cost_estimate=LIGHT,
        name="cross",
    )(left, right)


def part_kernel(left, right, *outs):
    values = lax.dot_general(
        left[...], right[...], (((1,), (1,)), ((), ())), preferred_element_type=jnp.float32
    )
    for index, out in enumerate(outs):

        @pl.when(pl.program_id(0) == index)
        def _(out=out):
            out[...] = values.astype(out.dtype)


def near_kernel(left, right, out):
    out[...] = lax.dot_general(
        left[...], right[...], (((1,), (1,)), ((), ())), preferred_element_type=jnp.float32
    )


def near_call(left, right, depth, place):
    rows = left.shape[0] // 8
    columns = right.shape[0]
    return pl.pallas_call(
        near_kernel,
        out_shape=jax.ShapeDtypeStruct((3 * rows, columns), jnp.float32),
        grid=(3,),
        in_specs=[
            pl.BlockSpec((rows, depth), lambda i: (i, 0)),
            pl.BlockSpec((columns, depth), lambda i: (0, place), pipeline_mode=pl.Buffered(1)),
        ],
        out_specs=pl.BlockSpec((rows, columns), lambda i: (i, 0)),
        cost_estimate=LIGHT,
        name="near",
    )(left, right)


def part_call(left, right, depth, place, first, kind):
    rows = left.shape[0] // 8
    columns = right.shape[0]
    return pl.pallas_call(
        part_kernel,
        out_shape=(jax.ShapeDtypeStruct((rows, columns), kind),) * 3,
        grid=(3,),
        in_specs=[
            pl.BlockSpec((rows, depth), lambda i: (first + i, 0)),
            pl.BlockSpec((columns, depth), lambda i: (0, place), pipeline_mode=pl.Buffered(1)),
        ],
        out_specs=(pl.BlockSpec((rows, columns), lambda i: (0, 0)),) * 3,
        cost_estimate=LIGHT,
        name="part",
    )(left, right)


def partial_rows(left, right, depth, place=0, beside=()):
    low = jnp.bfloat16
    near_cross, far_cross = cross_call(left, right, depth, place)
    far_cross, left = together(far_cross, left)
    rest_far = part_call(left, right, depth, place, 4, low)
    far_cross, *rest = together(swap(far_cross, CORE), *rest_far, *beside, *[left] * bool(beside))
    rest_far = rest[:3]
    if beside:
        *beside, left = rest[3:]
    cross = (near_cross + far_cross.astype(jnp.float32)).astype(low)
    near = near_call(left, right, depth, place)
    return (cross, near, [swap(block, CORE) for block in rest_far], *beside)


def scatter_cross(cross):
    half = cross.shape[0] // 2
    return (swap(cross[:half], PAIR), swap(cross[half:], CHIP))


def sums_kernel(near_chip, near_pair, far_chip, far_pair, from_pair, from_chip, chip, pair):
    wide = jnp.float32
    early = pl.program_id(0) < pl.num_programs(0) // 2
    left = near_chip[...] + far_chip[...].astype(wide)
    right = near_pair[...] + far_pair[...].astype(wide)
    chip[...] = jnp.where(early, left + from_pair[...].astype(wide), left).astype(chip.dtype)
    pair[...] = jnp.where(early, right, right + from_chip[...].astype(wide)).astype(pair.dtype)


def near_sums(near, far, from_pair, from_chip):
    rows, columns = far[1].shape
    steps = 2
    half = steps // 2
    block = (rows // steps, columns)
    straight = pl.BlockSpec(block, lambda i: (i, 0))
    return pl.pallas_call(
        sums_kernel,
        out_shape=(jax.ShapeDtypeStruct((rows, columns), jnp.bfloat16),) * 2,
        grid=(steps,),
        in_specs=[
            pl.BlockSpec(block, lambda i: (steps + i, 0)),
            pl.BlockSpec(block, lambda i: (2 * steps + i, 0)),
            straight,
            straight,
        ]
        + [
            pl.BlockSpec(block, lambda i: (jnp.minimum(i, half - 1), 0)),
            pl.BlockSpec(block, lambda i: (jnp.maximum(i - half, 0), 0)),
        ],
        out_specs=(straight, straight),
        cost_estimate=LIGHT,
        name="sums",
    )(near, near, far[1], far[2], from_pair, from_chip)


def scatter_near(chip, pair):
    return (swap(chip, CHIP), swap(pair, PAIR))


def all_sums(near, far, chip, pair):
    own = (near[: far[0].shape[0]] + far[0].astype(jnp.float32)).astype(jnp.bfloat16)
    return own.astype(jnp.float32) + chip.astype(jnp.float32) + pair.astype(jnp.float32)


def first_kernel(*refs):
    out = refs[-1]
    start = 0
    for left, right in zip(refs[:-1:2], refs[1:-1:2]):
        span = slice(start, start + right.shape[1])
        values = lax.dot_general(
            left[...], right[...], (((0,), (0,)), ((), ())), preferred_element_type=jnp.float32
        )
        out[:, span] = values.astype(out.dtype)
        start = span.stop


def product_first(name, *pairs, cost=LIGHT):
    rows, depth = pairs[0][0].shape
    columns = sum(right.shape[1] for _, right in pairs)
    tile = 512
    specs = []
    for _, right in pairs:
        specs.append(pl.BlockSpec((rows, tile), lambda i: (0, i)))
        specs.append(pl.BlockSpec(right.shape, lambda i: (0, 0), pipeline_mode=pl.Buffered(1)))
    return pl.pallas_call(
        first_kernel,
        out_shape=jax.ShapeDtypeStruct((depth, columns), jnp.bfloat16),
        grid=(depth // tile,),
        in_specs=specs,
        out_specs=pl.BlockSpec((tile, columns), lambda i: (i, 0)),
        cost_estimate=cost,
        name=name,
    )(*[array for pair in pairs for array in pair])


def halves(values):
    place = lax.axis_index("inner")
    size = values.shape[1] // 2
    mine = lax.dynamic_slice_in_dim(values, place * size, size, 1)
    theirs = lax.dynamic_slice_in_dim(values, (1 - place) * size, size, 1)
    return (mine, theirs)


def in_order(mine, theirs, axis):
    first = lax.axis_index("inner") == 0
    return jnp.concatenate([jnp.where(first, mine, theirs), jnp.where(first, theirs, mine)], axis)


def pair_weights(parts):
    cut = [halves(part) for part in parts]
    mine = jnp.concatenate([mine for mine, _ in cut], 1)
    theirs = jnp.concatenate([theirs for _, theirs in cut], 1)
    return (mine, theirs)


def gather_weights(mine, theirs):
    return gather_outer(in_order(mine, theirs, 0))


def own_grads(values):
    rows = values.shape[0] // 2
    place = lax.axis_index("inner")
    mine = lax.dynamic_slice_in_dim(values, place * rows, rows, 0)
    return (mine, swap(lax.dynamic_slice_in_dim(values, (1 - place) * rows, rows, 0), PAIR))


def total(values):
    for axis in ("narrow", "inner", "outer"):
        bit = 1
        while bit < lax.axis_size(axis):
            values = values + swap(values, (axis, bit))
            bit *= 2
    return values


def places_of(blocks, count):
    half = blocks.shape[1] // 2
    places = []
    for side in (0, 4):
        places += [blocks.at[side], blocks.at[side + 1], blocks.at[side + 2]]
        if count == 8:
            places += [blocks.at[side + 3]]
        else:
            places += [blocks.at[side + 3, pl.ds(0, half)], blocks.at[side + 3, pl.ds(half, half)]]
    return places


def parts_of(block, count):
    first = block % 4 + (block // 4) * (count // 2)
    return range(first, first + (count // 2 - 3 if block % 4 == 3 else 1))


def join_kernel(*refs):
    count = len(refs) - 4
    pieces = refs[:count]
    joined, blocks, arrive, leave = refs[count:]
    places = places_of(blocks, count)
    arrivals = [pltpu.make_async_copy(pieces[i], places[i], arrive.at[i]) for i in range(count)]
    departures = [pltpu.make_async_copy(blocks.at[i], joined.at[i], leave.at[i]) for i in range(8)]
    for copy in arrivals:
        copy.start()
    for block in range(8):
        for index in parts_of(block, count):
            arrivals[index].wait()
        departures[block].start()
    for copy in departures:
        copy.wait()


def join(pieces):
    rows, depth = pieces[0].shape
    anywhere = pl.BlockSpec(memory_space=pltpu.HBM)
    return pl.pallas_call(
        join_kernel,
        out_shape=jax.ShapeDtypeStruct((8, rows, depth), jnp.bfloat16),
        in_specs=[anywhere] * len(pieces),
        out_specs=anywhere,
        scratch_shapes=[
            pltpu.VMEM((8, rows, depth), jnp.bfloat16),
            pltpu.SemaphoreType.DMA((len(pieces),)),
            pltpu.SemaphoreType.DMA((8,)),
        ],
        cost_estimate=LIGHT,
        name="join",
    )(*pieces).reshape(8 * rows, depth)


def rows_kernel(finish, count, extra, results, *refs):
    pieces = refs[:count]
    weights = refs[count : count + extra]
    outputs = refs[count + extra : count + extra + results]
    joined, *beside, blocks, arrive, leave = refs[count + extra + results :]
    step = pl.program_id(0)
    places = places_of(blocks, count)

    def arrival(index):
        return pltpu.make_async_copy(pieces[index], places[index], arrive.at[index])

    def departure(block):
        return pltpu.make_async_copy(blocks.at[block], joined.at[block], leave.at[block])

    def beside_copies():
        if not beside:
            return []
        width = weights[0].shape[1]
        return [
            pltpu.make_async_copy(weight, beside[0].at[:, pl.ds(i * width, width)], leave.at[8 + i])
            for i, weight in enumerate(weights)
        ]

    @pl.when(step == 0)
    def _():
        for index in range(count):
            arrival(index).start()
        for copy in beside_copies():
            copy.start()

    for block in range(8):

        @pl.when(step == block)
        def _(block=block):
            for index in parts_of(block, count):
                arrival(index).wait()
            departure(block).start()

    finish(blocks[step], weights, (), outputs)

    @pl.when(step == 7)
    def _():
        for block in range(8):
            departure(block).wait()
        for copy in beside_copies():
            copy.wait()


def rows_call(name, finish, pieces, weights, widths, kinds, columns=None, place=0):
    rows, depth = pieces[0].shape
    columns = columns or weights[0].shape[1]
    beside = (depth, len(weights) * columns)

    def block(width):
        return pl.BlockSpec((None, rows, width), lambda i: (i, 0, 0))

    anywhere = pl.BlockSpec(memory_space=pltpu.HBM)
    more = len(weights) > 1
    results = pl.pallas_call(
        functools.partial(rows_kernel, finish, len(pieces), len(weights), len(widths)),
        out_shape=tuple(
            jax.ShapeDtypeStruct((8, rows, width), kind) for width, kind in zip(widths, kinds)
        )
        + (jax.ShapeDtypeStruct((8, rows, depth), jnp.bfloat16),)
        + (jax.ShapeDtypeStruct(beside, jnp.bfloat16),) * more,
        grid=(8,),
        in_specs=[anywhere] * len(pieces)
        + [pl.BlockSpec((depth, columns), lambda i: (0, place), pipeline_mode=pl.Buffered(1))]
        * len(weights),
        out_specs=tuple(block(width) for width in widths) + (anywhere,) * (1 + more),
        scratch_shapes=[
            pltpu.VMEM((8, rows, depth), jnp.bfloat16),
            pltpu.SemaphoreType.DMA((len(pieces),)),
            pltpu.SemaphoreType.DMA((8 + len(weights),)),
        ],
        cost_estimate=LIGHT,
        name=name,
    )(*pieces, *weights)
    count = len(widths) + 1
    return [result.reshape(8 * rows, result.shape[-1]) for result in results[:count]] + list(results[count:])


def blocks_kernel(finish, left, weight, *refs):
    finish(left[...], (weight,), refs[:-1], refs[-1:])


def blocks_call(name, finish, left, weight, operands, width, rows):
    depth, columns = weight.shape
    count = left.shape[0] // rows

    def block(size):
        return pl.BlockSpec((rows, size), lambda i: (i, 0))

    return pl.pallas_call(
        functools.partial(blocks_kernel, finish),
        out_shape=jax.ShapeDtypeStruct((left.shape[0], width), jnp.bfloat16),
        grid=(count,),
        in_specs=[block(depth), pl.BlockSpec(weight.shape, lambda i: (0, 0), pipeline_mode=pl.Buffered(1))]
        + [block(operand.shape[1]) for operand in operands],
        out_specs=block(width),
        cost_estimate=LIGHT,
        name=name,
    )(left, weight, *operands)


def product(left, right):
    return jnp.dot(left, right, preferred_element_type=jnp.float32)


def plain_finish(left, weights, operands, outputs):
    outputs[0][...] = product(left, weights[0][...]).astype(outputs[0].dtype)


def tiles_of(size):
    return [slice(start, start + 256) for start in range(0, size, 256)]


def gate_finish(left, weights, operands, outputs):
    both, hidden = outputs
    size = hidden.shape[1]
    for tile in tiles_of(size):
        up_tile = slice(size + tile.start, size + tile.stop)
        gate_val = product(left, weights[0][:, tile])
        up_val = product(left, weights[0][:, up_tile])
        both[:, tile] = gate_val.astype(both.dtype)
        both[:, up_tile] = up_val.astype(both.dtype)
        hidden[:, tile] = (gate_val * jax.nn.sigmoid(gate_val) * up_val).astype(hidden.dtype)


def hidden_finish(left, weights, operands, outputs):
    (both,) = operands
    (grads,) = outputs
    size = both.shape[1] // 2
    for tile in tiles_of(size):
        up_tile = slice(size + tile.start, size + tile.stop)
        hidden_grad = product(left, weights[0][:, tile])
        gate_val = both[:, tile].astype(jnp.float32)
        up_val = both[:, up_tile].astype(jnp.float32)
        sigmoid = jax.nn.sigmoid(gate_val)
        slope = sigmoid * (1.0 + gate_val * (1.0 - sigmoid))
        grads[:, tile] = (hidden_grad * up_val * slope).astype(grads.dtype)
        grads[:, up_tile] = (hidden_grad * (gate_val * sigmoid)).astype(grads.dtype)


def rope_tables(length):
    places = jnp.arange(length, dtype=jnp.float32)
    frequency = THETA ** (-jnp.arange(HD // 2, dtype=jnp.float32) * 2.0 / HD)
    angles = places[:, None] * frequency[None, :]
    cos_table = jnp.cos(angles)
    sin_table = jnp.sin(angles)
    return (
        jnp.concatenate([cos_table, cos_table], 1),
        jnp.concatenate([-sin_table, sin_table], 1),
    )


def unit_of(raw):
    inverse = lax.rsqrt(jnp.mean(raw * raw, -1, keepdims=True) + EPS)
    return (raw * inverse, inverse)


def turn(values, cos_table, sin_table):
    return values * cos_table + pltpu.roll(values, HD // 2, 1) * sin_table


def place_of(meta, block):
    relative = jnp.bitwise_xor(meta[0], block)
    return (jnp.bitwise_and(relative, 1), lax.shift_right_logical(relative, 1))


def load_heads(meta, raw, gains, cos_ref, sin_ref, queries, keys, values, rows, blocks, heads):
    gain_query = gains[0:1, :]
    gain_key = gains[1:2, :]
    for block in range(blocks):
        core, chip = place_of(meta, block)
        span = slice(block * rows, (block + 1) * rows)
        tile = raw[core, chip]
        cos_table = cos_ref[span, :]
        sin_table = sin_ref[span, :]
        for head in range(heads):
            unit, _ = unit_of(tile[:, head * HD : (head + 1) * HD])
            queries[head, span, :] = turn(unit * gain_query, cos_table, sin_table).astype(jnp.bfloat16)
        unit, _ = unit_of(tile[:, heads * HD : (heads + 1) * HD])
        keys[span, :] = turn(unit * gain_key, cos_table, sin_table).astype(jnp.bfloat16)
        values[span, :] = tile[:, (heads + 1) * HD :].astype(jnp.bfloat16)


def weights_of(left, right, start, valid_len, key_axis):
    scores = lax.dot_general(left, right, (((1,), (1,)), ((), ())), preferred_element_type=jnp.float32)
    query_place = start + lax.broadcasted_iota(jnp.int32, scores.shape, 1 - key_axis)
    key_place = lax.broadcasted_iota(jnp.int32, scores.shape, key_axis)
    allowed = (key_place <= query_place) & (key_place < valid_len)
    return jnp.where(allowed, jnp.exp(scores * SCALE), 0.0)


def forward_kernel(rows, blocks, heads, meta, raw, gains, cos_ref, sin_ref, context, queries, keys, values):
    load_heads(meta, raw, gains, cos_ref, sin_ref, queries, keys, values, rows, blocks, heads)
    valid_len = meta[1 + pl.program_id(0)]
    for block in range(blocks):
        core, chip = place_of(meta, block)
        seen = (block + 1) * rows
        for head in range(heads):
            query = queries[head, block * rows : seen, :]
            weights = weights_of(query, keys[:seen, :], block * rows, valid_len, 1)
            inverse = 1.0 / jnp.sum(weights, -1, keepdims=True)
            part = jnp.dot(
                weights.astype(jnp.bfloat16), values[:seen, :], preferred_element_type=jnp.float32
            )
            context[core, chip, :, head * HD : (head + 1) * HD] = (part * inverse).astype(jnp.bfloat16)


def backward_kernel(
    rows, blocks, heads, meta, raw, context_grad, gains, cos_ref, sin_ref,
    raw_grad, gain_grad, queries, keys, values, key_grad, value_grad, query_grad,
):
    load_heads(meta, raw, gains, cos_ref, sin_ref, queries, keys, values, rows, blocks, heads)
    valid_len = meta[1 + pl.program_id(0)]
    key_grad[...] = jnp.zeros_like(key_grad)
    value_grad[...] = jnp.zeros_like(value_grad)
    first = (((0,), (0,)), ((), ()))
    last = (((1,), (1,)), ((), ()))
    for block in range(blocks):
        core, chip = place_of(meta, block)
        seen = (block + 1) * rows
        for head in range(heads):
            query = queries[head, block * rows : seen, :]
            grad = context_grad[core, chip, :, head * HD : (head + 1) * HD]
            weights = weights_of(keys[:seen, :], query, block * rows, valid_len, 0)
            probability = weights * (1.0 / jnp.sum(weights, 0, keepdims=True))
            value_grad[:seen, :] += jnp.dot(
                probability.astype(jnp.bfloat16), grad, preferred_element_type=jnp.float32
            )
            prob_grad = lax.dot_general(values[:seen, :], grad, last, preferred_element_type=jnp.float32)
            inner = jnp.sum(probability * prob_grad, 0, keepdims=True)
            score_grad = (probability * (prob_grad - inner)).astype(jnp.bfloat16)
            query_grad[head, block * rows : seen, :] = SCALE * lax.dot_general(
                score_grad, keys[:seen, :], first, preferred_element_type=jnp.float32
            )
            key_grad[:seen, :] += SCALE * jnp.dot(score_grad, query, preferred_element_type=jnp.float32)
    query_total = jnp.zeros((1, HD), jnp.float32)
    key_total = jnp.zeros((1, HD), jnp.float32)
    for block in range(blocks):
        core, chip = place_of(meta, block)
        span = slice(block * rows, (block + 1) * rows)
        cos_table = cos_ref[span, :]
        sin_table = sin_ref[span, :]

        def back(raw_values, turned, gain):
            unit, inverse = unit_of(raw_values)
            scaled = turn(turned, cos_table, -sin_table)
            total = jnp.sum(scaled * unit, 0, keepdims=True)
            scaled = scaled * gain
            result = inverse * (scaled - unit * jnp.mean(scaled * unit, -1, keepdims=True))
            return (result.astype(jnp.bfloat16), total)

        for head in range(heads):
            columns = slice(head * HD, (head + 1) * HD)
            result, total = back(raw[core, chip, :, columns], query_grad[head, span, :], gains[0:1, :])
            raw_grad[core, chip, :, columns] = result
            query_total += total
        columns = slice(heads * HD, (heads + 1) * HD)
        result, total = back(raw[core, chip, :, columns], key_grad[span, :], gains[1:2, :])
        raw_grad[core, chip, :, columns] = result
        key_total += total
        raw_grad[core, chip, :, (heads + 1) * HD :] = value_grad[span, :].astype(jnp.bfloat16)
    gain_grad[0:1, :] = query_total
    gain_grad[1:2, :] = key_total


def row_blocks(rows, columns):
    return pl.BlockSpec((2, None, 2, rows, columns), lambda s, meta: (0, s, 0, 0, 0))


def whole(shape):
    return pl.BlockSpec(shape, lambda s, meta: (0,) * len(shape))


def split_rows(values, rows):
    return values.reshape(2, 2, 2, rows, values.shape[-1])


def attend_forward(meta, raw, gains, cos_table, sin_table):
    length = cos_table.shape[0]
    rows = raw.shape[0] // 8
    blocks = length // rows
    heads = raw.shape[1] // HD - 2
    result = pl.pallas_call(
        functools.partial(forward_kernel, rows, blocks, heads),
        out_shape=jax.ShapeDtypeStruct((2, 2, 2, rows, heads * HD), jnp.bfloat16),
        grid_spec=pltpu.PrefetchScalarGridSpec(
            num_scalar_prefetch=1,
            grid=(2,),
            in_specs=[
                row_blocks(rows, raw.shape[1]),
                whole((2, HD)),
                whole((length, HD)),
                whole((length, HD)),
            ],
            out_specs=row_blocks(rows, heads * HD),
            scratch_shapes=[
                pltpu.VMEM((heads, length, HD), jnp.bfloat16),
                pltpu.VMEM((length, HD), jnp.bfloat16),
                pltpu.VMEM((length, HD), jnp.bfloat16),
            ],
        ),
        cost_estimate=LIGHT,
        name="attend_forward",
    )(meta, split_rows(raw, rows), gains, cos_table, sin_table)
    return result.reshape(8 * rows, heads * HD)


def attend_backward(meta, raw, context_grad, gains, cos_table, sin_table):
    length = cos_table.shape[0]
    rows = raw.shape[0] // 8
    blocks = length // rows
    width = raw.shape[1]
    heads = width // HD - 2
    raw_grad, gain_grad = pl.pallas_call(
        functools.partial(backward_kernel, rows, blocks, heads),
        out_shape=(
            jax.ShapeDtypeStruct((2, 2, 2, rows, width), jnp.bfloat16),
            jax.ShapeDtypeStruct((2, 2, HD), jnp.float32),
        ),
        grid_spec=pltpu.PrefetchScalarGridSpec(
            num_scalar_prefetch=1,
            grid=(2,),
            in_specs=[
                row_blocks(rows, width),
                row_blocks(rows, heads * HD),
                whole((2, HD)),
                whole((length, HD)),
                whole((length, HD)),
            ],
            out_specs=(
                row_blocks(rows, width),
                pl.BlockSpec((None, 2, HD), lambda s, meta: (s, 0, 0)),
            ),
            scratch_shapes=[
                pltpu.VMEM((heads, length, HD), jnp.bfloat16),
                pltpu.VMEM((length, HD), jnp.bfloat16),
                pltpu.VMEM((length, HD), jnp.bfloat16),
                pltpu.VMEM((length, HD), jnp.float32),
                pltpu.VMEM((length, HD), jnp.float32),
                pltpu.VMEM((heads, length, HD), jnp.float32),
            ],
        ),
        cost_estimate=LIGHT,
        name="attend_backward",
    )(meta, split_rows(raw, rows), split_rows(context_grad, rows), gains, cos_table, sin_table)
    return (raw_grad.reshape(8 * rows, width), jnp.sum(gain_grad, 0))


def norm_back(normed_grad, hat_values, inverse, gain_vector):
    gain_grad = jnp.sum(normed_grad * hat_values, axis=0)
    scaled = normed_grad * gain_vector
    return (
        inverse * (scaled - hat_values * jnp.mean(scaled * hat_values, -1, keepdims=True)),
        gain_grad,
    )


def moments(gradient, moment_one, moment_two):
    new_one = BETA_ONE * moment_one + (1.0 - BETA_ONE) * gradient
    new_two = BETA_TWO * moment_two + (1.0 - BETA_TWO) * gradient * gradient
    return (new_one, new_two)


def update_of(new_one, new_two, master):
    return (
        new_one / (1.0 - BETA_ONE**STEP) / (jnp.sqrt(new_two / (1.0 - BETA_TWO**STEP)) + ADAM_EPS)
        + DECAY * master
    )


def square(values):
    return jnp.sum(jnp.sum(values * values, 1, keepdims=True), 0, keepdims=True)


def step_part(gradient, span, arrays, results):
    one, two, master = (array[span].reshape(gradient.shape) for array in arrays)
    new_one, new_two = moments(gradient, one, two)
    update = update_of(new_one, new_two, master)
    for result, values in zip(results, (new_one, new_two, update)):
        result[span] = values.reshape(result[span].shape)
    return (square(master), square(update))


def put_sums(sums, pairs, first):
    row = lax.broadcasted_iota(jnp.int32, sums.shape, 0)
    tile = jnp.zeros(sums.shape, jnp.float32)
    for index, value in enumerate(pairs):
        tile = jnp.where(row == index, value, tile)
    sums[...] = tile + jnp.where(first, 0.0, sums[...])


def add_pairs(left, right):
    return (left[0] + right[0], left[1] + right[1])


def stacked_step(meta, mine, other, one, two, master, new_one, new_two, update, sums):
    step = pl.program_id(0)
    size = one.shape[2]
    pairs = []
    for side in range(2):
        columns = slice(side * size, (side + 1) * size)
        own = step == meta[0]
        gradient = jnp.where(own, mine[:, columns], other[:, columns]).astype(jnp.float32)
        pairs += step_part(gradient, (side,), (one, two, master), (new_one, new_two, update))
    put_sums(sums, pairs, step == 0)


def turned_step(meta, mine, other, one, two, master, new_one, new_two, update, sums):
    step = pl.program_id(0)
    gradient = jnp.where(step == meta[0], mine[...], other[...]).astype(jnp.float32).T
    pair = step_part(gradient, (slice(None),), (one, two, master), (new_one, new_two, update))
    put_sums(sums, pair, step == 0)


def attn_step(
    meta, mine, other, query_one, query_two, query, keyval_one, keyval_two, keyval,
    output_one, output_two, output, new_query_one, new_query_two, query_update,
    new_keyval_one, new_keyval_two, keyval_update, new_output_one, new_output_two, output_update, sums,
):
    step = pl.program_id(0)
    own = step == meta[0]
    width = query.shape[1]
    key_width = keyval.shape[2]

    def part(first, size):
        columns = slice(first, first + size)
        return jnp.where(own, mine[:, columns], other[:, columns]).astype(jnp.float32)

    whole_span = (slice(None),)
    pairs = []
    pairs += step_part(part(0, width), whole_span, (query_one, query_two, query), (new_query_one, new_query_two, query_update))
    for side in range(2):
        pairs += step_part(
            part(width + side * key_width, key_width), (side,),
            (keyval_one, keyval_two, keyval), (new_keyval_one, new_keyval_two, keyval_update),
        )
    pairs += step_part(
        part(width + 2 * key_width, mine.shape[1] - width - 2 * key_width).T, whole_span,
        (output_one, output_two, output), (new_output_one, new_output_two, output_update),
    )
    put_sums(sums, pairs, step == 0)


def half_block(array, axis):
    shape = tuple(size // 2 if place == axis else size for place, size in enumerate(array.shape))
    return pl.BlockSpec(shape, lambda i, meta: tuple(i if place == axis else 0 for place in range(len(shape))))


def step_call(name, kernel, place, mine, other, arrays, axes):
    fixed = pl.BlockSpec(mine.shape, lambda i, meta: (0, 0))
    specs = [half_block(array, axis) for group, axis in zip(arrays, axes) for array in group]
    out_arrays = [(array, axis) for group, axis in zip(arrays, axes) for array in group]
    return pl.pallas_call(
        kernel,
        out_shape=tuple(jax.ShapeDtypeStruct(array.shape, jnp.float32) for array, _ in out_arrays)
        + (jax.ShapeDtypeStruct((8, HD), jnp.float32),),
        grid_spec=pltpu.PrefetchScalarGridSpec(
            num_scalar_prefetch=1,
            grid=(2,),
            in_specs=[fixed, fixed] + specs,
            out_specs=tuple(half_block(array, axis) for array, axis in out_arrays)
            + (pl.BlockSpec((8, HD), lambda i, meta: (0, 0)),),
        ),
        cost_estimate=LIGHT,
        name=name,
    )(place, mine, other, *[array for group in arrays for array in group])


def ratio_of(weight_square, update_square):
    return jnp.sqrt(weight_square) / jnp.sqrt(update_square)


def apply_kernel(parts, axes, *refs):
    sums = refs[0]
    count = len(parts)
    for place, rows in enumerate(parts):
        update, master = refs[1 + 2 * place : 3 + 2 * place]
        result = refs[1 + 2 * count + place]
        for side, row in enumerate(rows):
            span = (side,) if len(rows) > 1 else (slice(None),)
            trust = ratio_of(sums[row : row + 1, 0:1], sums[row + 1 : row + 2, 0:1])
            result[span] = master[span] - LEARN * trust * update[span]


def apply_call(name, sums, arrays, parts, axes, steps):
    def block(array, axis):
        shape = tuple(size // steps if place == axis else size for place, size in enumerate(array.shape))
        return pl.BlockSpec(shape, lambda i: tuple(i if place == axis else 0 for place in range(len(shape))))

    return pl.pallas_call(
        functools.partial(apply_kernel, parts, axes),
        out_shape=tuple(jax.ShapeDtypeStruct(group[1].shape, jnp.float32) for group in arrays),
        grid=(steps,),
        in_specs=[pl.BlockSpec(sums.shape, lambda i: (0, 0))]
        + [block(array, axis) for group, axis in zip(arrays, axes) for array in group],
        out_specs=tuple(block(group[1], axis) for group, axis in zip(arrays, axes)),
        cost_estimate=LIGHT,
        name=name,
    )(sums, *[array for group in arrays for array in group])


def gains_kernel(rows, sums, first, second, gains, new_first, new_second, new_gains, stats, trust):
    each = (rows - 2) // 2
    new_one, new_two = moments(sums[24 : 24 + rows, :], first[:rows, :], second[:rows, :])
    for result, values in ((new_first, new_one), (new_second, new_two), (new_gains, new_one)):
        result[:rows, :] = values
        result[rows:, :] = jnp.zeros_like(result[rows:, :])
    lane = lax.broadcasted_iota(jnp.int32, (1, HD), 1)
    weight_row = jnp.zeros((1, HD), jnp.float32)
    update_row = jnp.zeros((1, HD), jnp.float32)

    def put(place, weight_square, update_square, weight_row, update_row):
        return (
            jnp.where(lane == place, jnp.sqrt(weight_square), weight_row),
            jnp.where(lane == place, jnp.sqrt(update_square), update_row),
        )

    for place, start, size in ((0, 0, each), (7, each, each), (4, 2 * each, 1), (5, 2 * each + 1, 1)):
        span = slice(start, start + size)
        old = gains[span, :]
        update = update_of(new_one[span, :], new_two[span, :], old)
        weight_square, update_square = (square(old), square(update))
        new_gains[span, :] = old - LEARN * ratio_of(weight_square, update_square) * update
        weight_row, update_row = put(place, weight_square, update_square, weight_row, update_row)
    for place, index in ((1, 16), (2, 18), (3, 20), (6, 22), (8, 0), (9, 2), (10, 8)):
        weight_row, update_row = put(
            place, sums[index : index + 1, 0:1], sums[index + 1 : index + 2, 0:1], weight_row, update_row
        )
    stats[0:1, :] = weight_row[:, :11]
    stats[1:2, :] = update_row[:, :11]
    trust[...] = (weight_row / jnp.where(lane < 11, update_row, 1.0))[:, :11]


def root_mean(values):
    return jnp.sqrt(jnp.mean(values * values, -1))


def gather_outer(values):
    return lax.all_gather(values, "outer", axis=0, tiled=True)


def scatter_outer(values):
    return lax.psum_scatter(values, "outer", scatter_dimension=0, tiled=True)


def shards(
    tokens,
    cotangent,
    lengths,
    norm_gains,
    gains_first,
    gains_second,
    query_weight,
    query_first,
    query_second,
    keyval_weight,
    keyval_first,
    keyval_second,
    output_weight,
    output_first,
    output_second,
    gateup_weight,
    gateup_first,
    gateup_second,
    down_weight,
    down_first,
    down_second,
):
    low = jnp.bfloat16
    shard_len = tokens.shape[1]
    narrow_size = lax.axis_size("narrow")
    outer_size = lax.axis_size("outer")
    seq_len = shard_len * narrow_size
    gain_one = norm_gains[:D]
    gain_two = norm_gains[D : 2 * D]
    head_gains = norm_gains[2 * D :].reshape(2, HD)
    cos_table, sin_table = rope_tables(seq_len)

    residual = tokens[0].astype(jnp.float32)
    inv_one = lax.rsqrt(jnp.mean(residual * residual, -1, keepdims=True) + EPS)
    hat_one = residual * inv_one
    normed = (hat_one * gain_one).astype(low)

    query_half = query_weight.shape[1] // 2
    key_half = keyval_weight.shape[2] // 2
    output_half = output_weight.shape[0] // 2
    hidden_size = down_weight.shape[0] // 2
    raw_width = query_half + 2 * key_half
    places = lax.axis_index("narrow") * shard_len + jnp.arange(shard_len, dtype=jnp.int32)
    valid = (places < lengths[0]).astype(jnp.float32)
    grad_out = cotangent[0].astype(jnp.float32) * valid[:, None]
    attn_low = [w.astype(low) for w in (query_weight, keyval_weight[0], keyval_weight[1])]
    mine, theirs = pair_weights(attn_low + [output_weight.astype(low).T])
    full_attn = gather_weights(mine, swap(theirs, PAIR))

    chip, pair = named("norm_one", gather_start, normed)
    gateup_mine, gateup_theirs = pair_weights(
        [gateup_weight[0].astype(low), gateup_weight[1].astype(low), down_weight.astype(low).T]
    )
    meta = jnp.concatenate(
        [lax.axis_index("narrow").astype(jnp.int32)[None], lengths, swap(lengths, PAIR)]
    )
    chip, pair, gateup_theirs, cos_table, sin_table, meta, head_gains = together(
        chip, pair, gateup_theirs, cos_table, sin_table, meta, head_gains
    )
    (cross,) = named("norm_one", gather_cross, chip, pair, False)
    gateup_pair = in_order(gateup_mine, swap(gateup_theirs, PAIR), 0)
    full_attn, grad_low = together(full_attn, grad_out.astype(low))
    cross, gateup_pair = together(cross, gateup_pair)
    full_gateup = gather_outer(gateup_pair[:, : 2 * hidden_size])
    full_down = gather_outer(gateup_pair[:, 2 * hidden_size :])
    grad_chip, grad_pair = named("output_grad", gather_start, grad_low)
    pieces_one = named("norm_one", gather_end, (normed, chip, pair, cross))
    raw, whole_one = rows_call(
        "query_key_value", plain_finish, pieces_one, [full_attn], [raw_width], [jnp.float32], raw_width
    )
    context = attend_forward(meta, raw, head_gains, cos_table, sin_table)
    context, grad_chip, grad_pair = together(context, grad_chip, grad_pair)

    cross, near, far = named(
        "attention_out", partial_rows, context, full_attn, output_half, raw_width // output_half
    )
    moved = named("attention_out", scatter_cross, cross)
    near, far[0], from_pair, from_chip = together(near, far[0], *moved)
    chip, pair = named("attention_out", near_sums, near, far, from_pair, from_chip)
    chip, pair = named("attention_out", scatter_near, chip, pair)
    attn_part = all_sums(near, far, chip, pair)
    middle = residual + attn_part
    inv_two = lax.rsqrt(jnp.mean(middle * middle, -1, keepdims=True) + EPS)
    hat_two = middle * inv_two
    normed = (hat_two * gain_two).astype(low)
    chip, pair = named("norm_two", gather_start, normed)
    cross = named("norm_two", gather_cross, chip, pair, True)
    *cross, grad_chip, grad_pair = together(*cross, grad_chip, grad_pair)
    pieces_two = named("norm_two", gather_end, (normed, chip, pair, *cross))
    grad_cross = named("output_grad", gather_cross, grad_chip, grad_pair, True)
    both, hidden, whole_two = rows_call(
        "gate_up", gate_finish, pieces_two, [full_gateup], [2 * hidden_size, hidden_size], [low, low],
    )
    hidden, *grad_cross = together(hidden, *grad_cross)
    whole_grad = join(
        named("output_grad", gather_end, (grad_low, grad_chip, grad_pair, *grad_cross))
    )
    down_grad = product_first("down_weight_grad", (whole_grad, hidden))
    full_down, down_grad = together(full_down, down_grad)
    down_own = scatter_outer(down_grad)
    pair_grad = blocks_call(
        "hidden_grad", hidden_finish, whole_grad, full_down, [both], 2 * hidden_size, shard_len
    )
    cross, near, far = named("norm_two_grad", partial_rows, pair_grad, full_gateup, 2 * hidden_size)
    moved = named("norm_two_grad", scatter_cross, cross)
    near, far[0], from_pair, from_chip = together(near, far[0], *moved)
    chip, pair = named("norm_two_grad", near_sums, near, far, from_pair, from_chip)
    chip, pair, pair_grad = together(chip, pair, pair_grad)
    chip, pair = named("norm_two_grad", scatter_near, chip, pair)
    gateup_grad = product_first(
        "gateup_weight_grad",
        (whole_two, pair_grad),
        cost=pl.CostEstimate(
            flops=2 * whole_two.size * pair_grad.shape[1], transcendentals=0, bytes_accessed=2 * whole_two.size
        ),
    )
    chip, pair, down_own, gateup_grad = together(chip, pair, down_own, gateup_grad)
    gateup_own = scatter_outer(gateup_grad)
    normed_two = all_sums(near, far, chip, pair)
    middle_norm, gain_two_grad = norm_back(normed_two, hat_two, inv_two, gain_two)
    middle_grad = grad_out + middle_norm
    down_mine, down_other = own_grads(down_own)
    middle_low, down_other = together(middle_grad.astype(low), down_other)
    chip, pair = named("middle_grad", gather_start, middle_low)
    cross = named("middle_grad", gather_cross, chip, pair, True)
    hidden, middle_low = together(hidden, middle_low)
    mlp_cross, mlp_near, mlp_far = named("mlp_out", partial_rows, hidden, full_down, hidden_size)
    *cross, mlp_cross, mlp_near = together(*cross, mlp_cross, mlp_near)
    pieces_mid = named("middle_grad", gather_end, (middle_low, chip, pair, *cross))
    context_grad, whole_mid = rows_call(
        "context_grad", plain_finish, pieces_mid, [full_attn], [output_half], [low],
        output_half, raw_width // output_half,
    )
    moved = named("mlp_out", scatter_cross, mlp_cross)
    context_grad, *moved = together(context_grad, *moved)
    mlp_chip, mlp_pair = named("mlp_out", near_sums, mlp_near, mlp_far, *moved)
    context_grad, mlp_chip, mlp_pair = together(context_grad, mlp_chip, mlp_pair)
    mlp_chip, mlp_pair = named("mlp_out", scatter_near, mlp_chip, mlp_pair)
    raw_grad, head_gain_grad = attend_backward(meta, raw, context_grad, head_gains, cos_table, sin_table)
    raw_grad, mlp_chip, mlp_pair = together(raw_grad, mlp_chip, mlp_pair)
    mlp_part = all_sums(mlp_near, mlp_far, mlp_chip, mlp_pair)
    attn_grad = product_first("attention_weight_grad", (whole_one, raw_grad), (whole_mid, context))
    attn_own = scatter_outer(attn_grad)
    gateup_mine, gateup_other = own_grads(gateup_own)
    place = lax.axis_index("inner").astype(jnp.int32)[None]
    down = (down_first, down_second, down_weight)
    gateup = (gateup_first, gateup_second, gateup_weight)
    cross, near, far, gateup_other = named(
        "norm_one_grad", partial_rows, raw_grad, full_attn, raw_width, 0, (gateup_other,)
    )
    final = middle + mlp_part
    result = final.astype(low)
    rms_values = jnp.stack([root_mean(attn_part), root_mean(mlp_part), root_mean(final)])[:, None, :]
    moved = named("norm_one_grad", scatter_cross, cross)
    near, far[0], from_pair, from_chip = together(near, far[0], *moved)
    chip, pair = named("norm_one_grad", near_sums, near, far, from_pair, from_chip)
    chip, pair = named("norm_one_grad", scatter_near, chip, pair)
    new_down_first, new_down_second, down_update, down_sums = step_call(
        "down_step", turned_step, place, down_mine, down_other, [down], [0]
    )
    new_gateup_first, new_gateup_second, gateup_update, gateup_sums = step_call(
        "gateup_step", stacked_step, place, gateup_mine, gateup_other, [gateup], [2]
    )
    attn_own, gain_two_grad = together(attn_own, gain_two_grad)
    attn_mine, attn_other = own_grads(attn_own)
    chip, pair, gateup_sums, down_sums, attn_other, result, rms_values = together(
        chip, pair, gateup_sums, down_sums, attn_other, result, rms_values
    )
    normed_one = all_sums(near, far, chip, pair)
    input_norm, gain_one_grad = norm_back(normed_one, hat_one, inv_one, gain_one)
    input_grad = (middle_grad + input_norm).astype(low)

    attn_arrays = [
        (query_first, query_second, query_weight),
        (keyval_first, keyval_second, keyval_weight),
        (output_first, output_second, output_weight),
    ]
    (
        new_query_first, new_query_second, query_update, new_keyval_first, new_keyval_second,
        keyval_update, new_output_first, new_output_second, output_update, attn_sums,
    ) = step_call("attention_step", attn_step, place, attn_mine, attn_other, attn_arrays, [1, 2, 0])
    sums = jnp.concatenate(
        [gateup_sums, down_sums, attn_sums]
        + [gain_one_grad.reshape(-1, HD), gain_two_grad.reshape(-1, HD), head_gain_grad],
        0,
    )
    sums = named("all_sums", total, sums)
    matrix_sums = sums[:24]
    gain_rows = norm_gains.size // HD
    new_query, new_keyval, new_output = apply_call(
        "attention",
        matrix_sums,
        [(query_update, query_weight), (keyval_update, keyval_weight), (output_update, output_weight)],
        ((16,), (18, 20), (22,)),
        (0, 1, 0),
        2,
    )
    new_gateup, new_down = apply_call(
        "gateup_down",
        matrix_sums,
        [(gateup_update, gateup_weight), (down_update, down_weight)],
        ((0, 2), (8,)),
        (1, 0),
        4,
    )
    padded = -(-gain_rows // 8) * 8
    gain_shape = jax.ShapeDtypeStruct((padded, HD), jnp.float32)
    new_gains_first, new_gains_second, new_gains, lamb_stats, trust = pl.pallas_call(
        functools.partial(gains_kernel, gain_rows),
        out_shape=(gain_shape, gain_shape, gain_shape)
        + tuple(jax.ShapeDtypeStruct((rows, 11), jnp.float32) for rows in (2, 1)),
        name="gains",
    )(
        sums,
        *[
            jnp.pad(values, (0, (padded - gain_rows) * HD)).reshape(padded, HD)
            for values in (gains_first, gains_second, norm_gains)
        ],
    )
    new_gains, new_gains_first, new_gains_second = (
        values.reshape(-1)[: norm_gains.size] for values in (new_gains, new_gains_first, new_gains_second)
    )
    trust = trust[0]
    return (
        result[None],
        input_grad[None],
        rms_values,
        new_gains,
        new_gains_first,
        new_gains_second,
        new_query,
        new_query_first,
        new_query_second,
        new_keyval,
        new_keyval_first,
        new_keyval_second,
        new_output,
        new_output_first,
        new_output_second,
        new_gateup,
        new_gateup_first,
        new_gateup_second,
        new_down,
        new_down_first,
        new_down_second,
        lamb_stats,
        trust,
    )


def solution(mesh):
    wide_size, narrow_size = mesh.devices.shape
    cube = jax.sharding.Mesh(
        mesh.devices.reshape(wide_size // 2, 2, narrow_size), ("outer", "inner", "narrow")
    )
    wide = ("outer", "inner")
    rows = P(wide, "narrow", None)
    matrix = P(wide, "narrow")
    stacked = P(None, wide, "narrow")
    turned = P("narrow", wide)
    in_specs = (rows, rows, P(wide), P(), P(), P())
    in_specs += (matrix,) * 3 + (stacked,) * 3 + (turned,) * 3 + (stacked,) * 3 + (turned,) * 3
    out_specs = (rows, rows, stacked, P(), P(), P())
    out_specs += (matrix,) * 3 + (stacked,) * 3 + (turned,) * 3 + (stacked,) * 3 + (turned,) * 3
    out_specs += (P(), P())
    return jax.shard_map(shards, mesh=cube, in_specs=in_specs, out_specs=out_specs, check_vma=False)
```

```python
import functools

import jax
import jax.numpy as jnp
from jax import lax
from jax.experimental import pallas as pl
from jax.experimental.pallas import tpu as pltpu
from jax.sharding import PartitionSpec as P

D = 2048
H = 16
KV = 8
HD = 128
STEP = 10


EPS = 1e-06
THETA = 1000000.0
BETA_ONE = 0.9
BETA_TWO = 0.999
ADAM_EPS = 1e-06
DECAY = 0.01
LEARN = 0.5

SCALE = HD ** (-0.5)
LIGHT = pl.CostEstimate(flops=1024, transcendentals=0, bytes_accessed=1024)

CHIP = ("narrow", 2)
CORE = ("narrow", 1)
PAIR = ("inner", 1)


def named(name, function, *operands):
    with jax.named_scope(name):
        return function(*operands)


def swap(values, link):
    axis, bit = link
    return lax.ppermute(values, axis, [(i, i ^ bit) for i in range(lax.axis_size(axis))])


def together(*values):
    return lax.optimization_barrier(values)


def gather_start(own):
    return together(swap(own, CHIP), swap(own, PAIR))


def gather_cross(chip, pair, split):
    if not split:
        return [swap(pair, CHIP)]
    half = pair.shape[0] // 2
    return [swap(chip[:half], PAIR), swap(pair[half:], CHIP)]


def gather_end(near):
    return list(near) + [swap(block, CORE) for block in near]


def cross_kernel(left, right, near, far):
    values = lax.dot_general(
        left[...], right[...], (((1,), (1,)), ((), ())), preferred_element_type=jnp.float32
    )

    @pl.when(pl.program_id(0) == 0)
    def _():
        far[...] = values.astype(far.dtype)

    @pl.when(pl.program_id(0) == 1)
    def _():
        near[...] = values


def cross_call(left, right, depth, place):
    rows = left.shape[0] // 8
    shape = (rows, right.shape[0])
    return pl.pallas_call(
        cross_kernel,
        out_shape=(jax.ShapeDtypeStruct(shape, jnp.float32), jax.ShapeDtypeStruct(shape, jnp.bfloat16)),
        grid=(2,),
        in_specs=[
            pl.BlockSpec((rows, depth), lambda i: (7 - 4 * i, 0)),
            pl.BlockSpec((right.shape[0], depth), lambda i: (0, place), pipeline_mode=pl.Buffered(1)),
        ],
        out_specs=(pl.BlockSpec(shape, lambda i: (0, 0)),) * 2,
        cost_estimate=LIGHT,
        name="cross",
    )(left, right)


def part_kernel(left, right, *outs):
    values = lax.dot_general(
        left[...], right[...], (((1,), (1,)), ((), ())), preferred_element_type=jnp.float32
    )
    for index, out in enumerate(outs):

        @pl.when(pl.program_id(0) == index)
        def _(out=out):
            out[...] = values.astype(out.dtype)


def near_kernel(left, right, out):
    out[...] = lax.dot_general(
        left[...], right[...], (((1,), (1,)), ((), ())), preferred_element_type=jnp.float32
    )


def near_call(left, right, depth, place):
    rows = left.shape[0] // 8
    columns = right.shape[0]
    return pl.pallas_call(
        near_kernel,
        out_shape=jax.ShapeDtypeStruct((3 * rows, columns), jnp.float32),
        grid=(3,),
        in_specs=[
            pl.BlockSpec((rows, depth), lambda i: (i, 0)),
            pl.BlockSpec((columns, depth), lambda i: (0, place), pipeline_mode=pl.Buffered(1)),
        ],
        out_specs=pl.BlockSpec((rows, columns), lambda i: (i, 0)),
        cost_estimate=LIGHT,
        name="near",
    )(left, right)


def part_call(left, right, depth, place, first, kind):
    rows = left.shape[0] // 8
    columns = right.shape[0]
    return pl.pallas_call(
        part_kernel,
        out_shape=(jax.ShapeDtypeStruct((rows, columns), kind),) * 3,
        grid=(3,),
        in_specs=[
            pl.BlockSpec((rows, depth), lambda i: (first + i, 0)),
            pl.BlockSpec((columns, depth), lambda i: (0, place), pipeline_mode=pl.Buffered(1)),
        ],
        out_specs=(pl.BlockSpec((rows, columns), lambda i: (0, 0)),) * 3,
        cost_estimate=LIGHT,
        name="part",
    )(left, right)


def partial_rows(left, right, depth, place=0, beside=()):
    low = jnp.bfloat16
    near_cross, far_cross = cross_call(left, right, depth, place)
    far_cross, left = together(far_cross, left)
    rest_far = part_call(left, right, depth, place, 4, low)
    far_cross, *rest = together(swap(far_cross, CORE), *rest_far, *beside, *[left] * bool(beside))
    rest_far = rest[:3]
    if beside:
        *beside, left = rest[3:]
    cross = (near_cross + far_cross.astype(jnp.float32)).astype(low)
    near = near_call(left, right, depth, place)
    return (cross, near, [swap(block, CORE) for block in rest_far], *beside)


def scatter_cross(cross):
    half = cross.shape[0] // 2
    return (swap(cross[:half], PAIR), swap(cross[half:], CHIP))


def sums_kernel(near_chip, near_pair, far_chip, far_pair, from_pair, from_chip, chip, pair):
    wide = jnp.float32
    early = pl.program_id(0) < pl.num_programs(0) // 2
    left = near_chip[...] + far_chip[...].astype(wide)
    right = near_pair[...] + far_pair[...].astype(wide)
    chip[...] = jnp.where(early, left + from_pair[...].astype(wide), left).astype(chip.dtype)
    pair[...] = jnp.where(early, right, right + from_chip[...].astype(wide)).astype(pair.dtype)


def near_sums(near, far, from_pair, from_chip):
    rows, columns = far[1].shape
    steps = 2
    half = steps // 2
    block = (rows // steps, columns)
    straight = pl.BlockSpec(block, lambda i: (i, 0))
    return pl.pallas_call(
        sums_kernel,
        out_shape=(jax.ShapeDtypeStruct((rows, columns), jnp.bfloat16),) * 2,
        grid=(steps,),
        in_specs=[
            pl.BlockSpec(block, lambda i: (steps + i, 0)),
            pl.BlockSpec(block, lambda i: (2 * steps + i, 0)),
            straight,
            straight,
        ]
        + [
            pl.BlockSpec(block, lambda i: (jnp.minimum(i, half - 1), 0)),
            pl.BlockSpec(block, lambda i: (jnp.maximum(i - half, 0), 0)),
        ],
        out_specs=(straight, straight),
        cost_estimate=LIGHT,
        name="sums",
    )(near, near, far[1], far[2], from_pair, from_chip)


def scatter_near(chip, pair):
    return (swap(chip, CHIP), swap(pair, PAIR))


def all_sums(near, far, chip, pair):
    own = (near[: far[0].shape[0]] + far[0].astype(jnp.float32)).astype(jnp.bfloat16)
    return own.astype(jnp.float32) + chip.astype(jnp.float32) + pair.astype(jnp.float32)


def first_kernel(*refs):
    out = refs[-1]
    start = 0
    for left, right in zip(refs[:-1:2], refs[1:-1:2]):
        span = slice(start, start + right.shape[1])
        values = lax.dot_general(
            left[...], right[...], (((0,), (0,)), ((), ())), preferred_element_type=jnp.float32
        )
        out[:, span] = values.astype(out.dtype)
        start = span.stop


def product_first(name, *pairs, cost=LIGHT):
    rows, depth = pairs[0][0].shape
    columns = sum(right.shape[1] for _, right in pairs)
    tile = 512
    specs = []
    for _, right in pairs:
        specs.append(pl.BlockSpec((rows, tile), lambda i: (0, i)))
        specs.append(pl.BlockSpec(right.shape, lambda i: (0, 0), pipeline_mode=pl.Buffered(1)))
    return pl.pallas_call(
        first_kernel,
        out_shape=jax.ShapeDtypeStruct((depth, columns), jnp.bfloat16),
        grid=(depth // tile,),
        in_specs=specs,
        out_specs=pl.BlockSpec((tile, columns), lambda i: (i, 0)),
        cost_estimate=cost,
        name=name,
    )(*[array for pair in pairs for array in pair])


def halves(values):
    place = lax.axis_index("inner")
    size = values.shape[1] // 2
    mine = lax.dynamic_slice_in_dim(values, place * size, size, 1)
    theirs = lax.dynamic_slice_in_dim(values, (1 - place) * size, size, 1)
    return (mine, theirs)


def in_order(mine, theirs, axis):
    first = lax.axis_index("inner") == 0
    return jnp.concatenate([jnp.where(first, mine, theirs), jnp.where(first, theirs, mine)], axis)


def pair_weights(parts):
    cut = [halves(part) for part in parts]
    mine = jnp.concatenate([mine for mine, _ in cut], 1)
    theirs = jnp.concatenate([theirs for _, theirs in cut], 1)
    return (mine, theirs)


def gather_weights(mine, theirs):
    return gather_outer(in_order(mine, theirs, 0))


def pair_rows(values):
    rows = values.shape[0] // 2
    return lax.dynamic_slice_in_dim(values, (1 - lax.axis_index("inner")) * rows, rows, 0)


def total(values):
    for axis in ("narrow", "inner", "outer"):
        bit = 1
        while bit < lax.axis_size(axis):
            values = values + swap(values, (axis, bit))
            bit *= 2
    return values


def places_of(blocks, count):
    half = blocks.shape[1] // 2
    places = []
    for side in (0, 4):
        places += [blocks.at[side], blocks.at[side + 1], blocks.at[side + 2]]
        if count == 8:
            places += [blocks.at[side + 3]]
        else:
            places += [blocks.at[side + 3, pl.ds(0, half)], blocks.at[side + 3, pl.ds(half, half)]]
    return places


def parts_of(block, count):
    first = block % 4 + (block // 4) * (count // 2)
    return range(first, first + (count // 2 - 3 if block % 4 == 3 else 1))


def join_kernel(*refs):
    count = len(refs) - 4
    pieces = refs[:count]
    joined, blocks, arrive, leave = refs[count:]
    places = places_of(blocks, count)
    arrivals = [pltpu.make_async_copy(pieces[i], places[i], arrive.at[i]) for i in range(count)]
    departures = [pltpu.make_async_copy(blocks.at[i], joined.at[i], leave.at[i]) for i in range(8)]
    for copy in arrivals:
        copy.start()
    for block in range(8):
        for index in parts_of(block, count):
            arrivals[index].wait()
        departures[block].start()
    for copy in departures:
        copy.wait()


def join(pieces):
    rows, depth = pieces[0].shape
    anywhere = pl.BlockSpec(memory_space=pltpu.HBM)
    return pl.pallas_call(
        join_kernel,
        out_shape=jax.ShapeDtypeStruct((8, rows, depth), jnp.bfloat16),
        in_specs=[anywhere] * len(pieces),
        out_specs=anywhere,
        scratch_shapes=[
            pltpu.VMEM((8, rows, depth), jnp.bfloat16),
            pltpu.SemaphoreType.DMA((len(pieces),)),
            pltpu.SemaphoreType.DMA((8,)),
        ],
        cost_estimate=LIGHT,
        name="join",
    )(*pieces).reshape(8 * rows, depth)


def rows_kernel(finish, count, extra, results, *refs):
    pieces = refs[:count]
    weights = refs[count : count + extra]
    outputs = refs[count + extra : count + extra + results]
    joined, *beside, blocks, arrive, leave = refs[count + extra + results :]
    step = pl.program_id(0)
    places = places_of(blocks, count)

    def arrival(index):
        return pltpu.make_async_copy(pieces[index], places[index], arrive.at[index])

    def departure(block):
        return pltpu.make_async_copy(blocks.at[block], joined.at[block], leave.at[block])

    def beside_copies():
        if not beside:
            return []
        width = weights[0].shape[1]
        return [
            pltpu.make_async_copy(weight, beside[0].at[:, pl.ds(i * width, width)], leave.at[8 + i])
            for i, weight in enumerate(weights)
        ]

    @pl.when(step == 0)
    def _():
        for index in range(count):
            arrival(index).start()
        for copy in beside_copies():
            copy.start()

    for block in range(8):

        @pl.when(step == block)
        def _(block=block):
            for index in parts_of(block, count):
                arrival(index).wait()
            departure(block).start()

    finish(blocks[step], weights, (), outputs)

    @pl.when(step == 7)
    def _():
        for block in range(8):
            departure(block).wait()
        for copy in beside_copies():
            copy.wait()


def rows_call(name, finish, pieces, weights, widths, kinds, columns=None, place=0):
    rows, depth = pieces[0].shape
    columns = columns or weights[0].shape[1]
    beside = (depth, len(weights) * columns)

    def block(width):
        return pl.BlockSpec((None, rows, width), lambda i: (i, 0, 0))

    anywhere = pl.BlockSpec(memory_space=pltpu.HBM)
    more = len(weights) > 1
    results = pl.pallas_call(
        functools.partial(rows_kernel, finish, len(pieces), len(weights), len(widths)),
        out_shape=tuple(
            jax.ShapeDtypeStruct((8, rows, width), kind) for width, kind in zip(widths, kinds)
        )
        + (jax.ShapeDtypeStruct((8, rows, depth), jnp.bfloat16),)
        + (jax.ShapeDtypeStruct(beside, jnp.bfloat16),) * more,
        grid=(8,),
        in_specs=[anywhere] * len(pieces)
        + [pl.BlockSpec((depth, columns), lambda i: (0, place), pipeline_mode=pl.Buffered(1))]
        * len(weights),
        out_specs=tuple(block(width) for width in widths) + (anywhere,) * (1 + more),
        scratch_shapes=[
            pltpu.VMEM((8, rows, depth), jnp.bfloat16),
            pltpu.SemaphoreType.DMA((len(pieces),)),
            pltpu.SemaphoreType.DMA((8 + len(weights),)),
        ],
        cost_estimate=LIGHT,
        name=name,
    )(*pieces, *weights)
    count = len(widths) + 1
    return [result.reshape(8 * rows, result.shape[-1]) for result in results[:count]] + list(results[count:])


def blocks_kernel(finish, left, weight, *refs):
    finish(left[...], (weight,), refs[:-1], refs[-1:])


def blocks_call(name, finish, left, weight, operands, width, rows):
    depth, columns = weight.shape
    count = left.shape[0] // rows

    def block(size):
        return pl.BlockSpec((rows, size), lambda i: (i, 0))

    return pl.pallas_call(
        functools.partial(blocks_kernel, finish),
        out_shape=jax.ShapeDtypeStruct((left.shape[0], width), jnp.bfloat16),
        grid=(count,),
        in_specs=[block(depth), pl.BlockSpec(weight.shape, lambda i: (0, 0), pipeline_mode=pl.Buffered(1))]
        + [block(operand.shape[1]) for operand in operands],
        out_specs=block(width),
        cost_estimate=LIGHT,
        name=name,
    )(left, weight, *operands)


def product(left, right):
    return jnp.dot(left, right, preferred_element_type=jnp.float32)


def plain_finish(left, weights, operands, outputs):
    outputs[0][...] = product(left, weights[0][...]).astype(outputs[0].dtype)


def tiles_of(size):
    return [slice(start, start + 256) for start in range(0, size, 256)]


def gate_finish(left, weights, operands, outputs):
    both, hidden = outputs
    size = hidden.shape[1]
    for tile in tiles_of(size):
        up_tile = slice(size + tile.start, size + tile.stop)
        gate_val = product(left, weights[0][:, tile])
        up_val = product(left, weights[0][:, up_tile])
        both[:, tile] = gate_val.astype(both.dtype)
        both[:, up_tile] = up_val.astype(both.dtype)
        hidden[:, tile] = (gate_val * jax.nn.sigmoid(gate_val) * up_val).astype(hidden.dtype)


def hidden_finish(left, weights, operands, outputs):
    (both,) = operands
    (grads,) = outputs
    size = both.shape[1] // 2
    for tile in tiles_of(size):
        up_tile = slice(size + tile.start, size + tile.stop)
        hidden_grad = product(left, weights[0][:, tile])
        gate_val = both[:, tile].astype(jnp.float32)
        up_val = both[:, up_tile].astype(jnp.float32)
        sigmoid = jax.nn.sigmoid(gate_val)
        slope = sigmoid * (1.0 + gate_val * (1.0 - sigmoid))
        grads[:, tile] = (hidden_grad * up_val * slope).astype(grads.dtype)
        grads[:, up_tile] = (hidden_grad * (gate_val * sigmoid)).astype(grads.dtype)


def rope_tables(length):
    places = jnp.arange(length, dtype=jnp.float32)
    frequency = THETA ** (-jnp.arange(HD // 2, dtype=jnp.float32) * 2.0 / HD)
    angles = places[:, None] * frequency[None, :]
    cos_table = jnp.cos(angles)
    sin_table = jnp.sin(angles)
    return (
        jnp.concatenate([cos_table, cos_table], 1),
        jnp.concatenate([-sin_table, sin_table], 1),
    )


def unit_of(raw):
    inverse = lax.rsqrt(jnp.mean(raw * raw, -1, keepdims=True) + EPS)
    return (raw * inverse, inverse)


def turn(values, cos_table, sin_table):
    return values * cos_table + pltpu.roll(values, HD // 2, 1) * sin_table


def place_of(meta, block):
    relative = jnp.bitwise_xor(meta[0], block)
    return (jnp.bitwise_and(relative, 1), lax.shift_right_logical(relative, 1))


def load_heads(meta, raw, gains, cos_ref, sin_ref, queries, keys, values, rows, blocks, heads):
    gain_query = gains[0:1, :]
    gain_key = gains[1:2, :]
    for block in range(blocks):
        core, chip = place_of(meta, block)
        span = slice(block * rows, (block + 1) * rows)
        tile = raw[core, chip]
        cos_table = cos_ref[span, :]
        sin_table = sin_ref[span, :]
        for head in range(heads):
            unit, _ = unit_of(tile[:, head * HD : (head + 1) * HD])
            queries[head, span, :] = turn(unit * gain_query, cos_table, sin_table).astype(jnp.bfloat16)
        unit, _ = unit_of(tile[:, heads * HD : (heads + 1) * HD])
        keys[span, :] = turn(unit * gain_key, cos_table, sin_table).astype(jnp.bfloat16)
        values[span, :] = tile[:, (heads + 1) * HD :].astype(jnp.bfloat16)


def weights_of(left, right, start, valid_len, key_axis):
    scores = lax.dot_general(left, right, (((1,), (1,)), ((), ())), preferred_element_type=jnp.float32)
    query_place = start + lax.broadcasted_iota(jnp.int32, scores.shape, 1 - key_axis)
    key_place = lax.broadcasted_iota(jnp.int32, scores.shape, key_axis)
    allowed = (key_place <= query_place) & (key_place < valid_len)
    return jnp.where(allowed, jnp.exp(scores * SCALE), 0.0)


def forward_kernel(rows, blocks, heads, meta, raw, gains, cos_ref, sin_ref, context, queries, keys, values):
    load_heads(meta, raw, gains, cos_ref, sin_ref, queries, keys, values, rows, blocks, heads)
    valid_len = meta[1 + pl.program_id(0)]
    for block in range(blocks):
        core, chip = place_of(meta, block)
        seen = (block + 1) * rows
        for head in range(heads):
            query = queries[head, block * rows : seen, :]
            weights = weights_of(query, keys[:seen, :], block * rows, valid_len, 1)
            inverse = 1.0 / jnp.sum(weights, -1, keepdims=True)
            part = jnp.dot(
                weights.astype(jnp.bfloat16), values[:seen, :], preferred_element_type=jnp.float32
            )
            context[core, chip, :, head * HD : (head + 1) * HD] = (part * inverse).astype(jnp.bfloat16)


def backward_kernel(
    rows, blocks, heads, meta, raw, context_grad, gains, cos_ref, sin_ref,
    raw_grad, gain_grad, queries, keys, values, key_grad, value_grad, query_grad,
):
    load_heads(meta, raw, gains, cos_ref, sin_ref, queries, keys, values, rows, blocks, heads)
    valid_len = meta[1 + pl.program_id(0)]
    key_grad[...] = jnp.zeros_like(key_grad)
    value_grad[...] = jnp.zeros_like(value_grad)
    first = (((0,), (0,)), ((), ()))
    last = (((1,), (1,)), ((), ()))
    for block in range(blocks):
        core, chip = place_of(meta, block)
        seen = (block + 1) * rows
        for head in range(heads):
            query = queries[head, block * rows : seen, :]
            grad = context_grad[core, chip, :, head * HD : (head + 1) * HD]
            weights = weights_of(keys[:seen, :], query, block * rows, valid_len, 0)
            probability = weights * (1.0 / jnp.sum(weights, 0, keepdims=True))
            value_grad[:seen, :] += jnp.dot(
                probability.astype(jnp.bfloat16), grad, preferred_element_type=jnp.float32
            )
            prob_grad = lax.dot_general(values[:seen, :], grad, last, preferred_element_type=jnp.float32)
            inner = jnp.sum(probability * prob_grad, 0, keepdims=True)
            score_grad = (probability * (prob_grad - inner)).astype(jnp.bfloat16)
            query_grad[head, block * rows : seen, :] = SCALE * lax.dot_general(
                score_grad, keys[:seen, :], first, preferred_element_type=jnp.float32
            )
            key_grad[:seen, :] += SCALE * jnp.dot(score_grad, query, preferred_element_type=jnp.float32)
    query_total = jnp.zeros((1, HD), jnp.float32)
    key_total = jnp.zeros((1, HD), jnp.float32)
    for block in range(blocks):
        core, chip = place_of(meta, block)
        span = slice(block * rows, (block + 1) * rows)
        cos_table = cos_ref[span, :]
        sin_table = sin_ref[span, :]

        def back(raw_values, turned, gain):
            unit, inverse = unit_of(raw_values)
            scaled = turn(turned, cos_table, -sin_table)
            total = jnp.sum(scaled * unit, 0, keepdims=True)
            scaled = scaled * gain
            result = inverse * (scaled - unit * jnp.mean(scaled * unit, -1, keepdims=True))
            return (result.astype(jnp.bfloat16), total)

        for head in range(heads):
            columns = slice(head * HD, (head + 1) * HD)
            result, total = back(raw[core, chip, :, columns], query_grad[head, span, :], gains[0:1, :])
            raw_grad[core, chip, :, columns] = result
            query_total += total
        columns = slice(heads * HD, (heads + 1) * HD)
        result, total = back(raw[core, chip, :, columns], key_grad[span, :], gains[1:2, :])
        raw_grad[core, chip, :, columns] = result
        key_total += total
        raw_grad[core, chip, :, (heads + 1) * HD :] = value_grad[span, :].astype(jnp.bfloat16)
    gain_grad[0:1, :] = query_total
    gain_grad[1:2, :] = key_total


def row_blocks(rows, columns):
    return pl.BlockSpec((2, None, 2, rows, columns), lambda s, meta: (0, s, 0, 0, 0))


def whole(shape):
    return pl.BlockSpec(shape, lambda s, meta: (0,) * len(shape))


def split_rows(values, rows):
    return values.reshape(2, 2, 2, rows, values.shape[-1])


def attend_forward(meta, raw, gains, cos_table, sin_table):
    length = cos_table.shape[0]
    rows = raw.shape[0] // 8
    blocks = length // rows
    heads = raw.shape[1] // HD - 2
    result = pl.pallas_call(
        functools.partial(forward_kernel, rows, blocks, heads),
        out_shape=jax.ShapeDtypeStruct((2, 2, 2, rows, heads * HD), jnp.bfloat16),
        grid_spec=pltpu.PrefetchScalarGridSpec(
            num_scalar_prefetch=1,
            grid=(2,),
            in_specs=[
                row_blocks(rows, raw.shape[1]),
                whole((2, HD)),
                whole((length, HD)),
                whole((length, HD)),
            ],
            out_specs=row_blocks(rows, heads * HD),
            scratch_shapes=[
                pltpu.VMEM((heads, length, HD), jnp.bfloat16),
                pltpu.VMEM((length, HD), jnp.bfloat16),
                pltpu.VMEM((length, HD), jnp.bfloat16),
            ],
        ),
        cost_estimate=LIGHT,
        name="attend_forward",
    )(meta, split_rows(raw, rows), gains, cos_table, sin_table)
    return result.reshape(8 * rows, heads * HD)


def attend_backward(meta, raw, context_grad, gains, cos_table, sin_table):
    length = cos_table.shape[0]
    rows = raw.shape[0] // 8
    blocks = length // rows
    width = raw.shape[1]
    heads = width // HD - 2
    raw_grad, gain_grad = pl.pallas_call(
        functools.partial(backward_kernel, rows, blocks, heads),
        out_shape=(
            jax.ShapeDtypeStruct((2, 2, 2, rows, width), jnp.bfloat16),
            jax.ShapeDtypeStruct((2, 2, HD), jnp.float32),
        ),
        grid_spec=pltpu.PrefetchScalarGridSpec(
            num_scalar_prefetch=1,
            grid=(2,),
            in_specs=[
                row_blocks(rows, width),
                row_blocks(rows, heads * HD),
                whole((2, HD)),
                whole((length, HD)),
                whole((length, HD)),
            ],
            out_specs=(
                row_blocks(rows, width),
                pl.BlockSpec((None, 2, HD), lambda s, meta: (s, 0, 0)),
            ),
            scratch_shapes=[
                pltpu.VMEM((heads, length, HD), jnp.bfloat16),
                pltpu.VMEM((length, HD), jnp.bfloat16),
                pltpu.VMEM((length, HD), jnp.bfloat16),
                pltpu.VMEM((length, HD), jnp.float32),
                pltpu.VMEM((length, HD), jnp.float32),
                pltpu.VMEM((heads, length, HD), jnp.float32),
            ],
        ),
        cost_estimate=LIGHT,
        name="attend_backward",
    )(meta, split_rows(raw, rows), split_rows(context_grad, rows), gains, cos_table, sin_table)
    return (raw_grad.reshape(8 * rows, width), jnp.sum(gain_grad, 0))


def norm_back(normed_grad, hat_values, inverse, gain_vector):
    gain_grad = jnp.sum(normed_grad * hat_values, axis=0)
    scaled = normed_grad * gain_vector
    return (
        inverse * (scaled - hat_values * jnp.mean(scaled * hat_values, -1, keepdims=True)),
        gain_grad,
    )


def moments(gradient, moment_one, moment_two):
    new_one = BETA_ONE * moment_one + (1.0 - BETA_ONE) * gradient
    new_two = BETA_TWO * moment_two + (1.0 - BETA_TWO) * gradient * gradient
    return (new_one, new_two)


def update_of(new_one, new_two, master):
    return (
        new_one / (1.0 - BETA_ONE**STEP) / (jnp.sqrt(new_two / (1.0 - BETA_TWO**STEP)) + ADAM_EPS)
        + DECAY * master
    )


def square(values):
    return jnp.sum(jnp.sum(values * values, 1, keepdims=True), 0, keepdims=True)


def step_part(gradient, span, arrays, results):
    one, two, master = (array[span].reshape(gradient.shape) for array in arrays)
    new_one, new_two = moments(gradient, one, two)
    update = update_of(new_one, new_two, master)
    for result, values in zip(results, (new_one, new_two, update)):
        result[span] = values.reshape(result[span].shape)
    return (square(master), square(update))


def put_sums(sums, pairs, first):
    row = lax.broadcasted_iota(jnp.int32, sums.shape, 0)
    tile = jnp.zeros(sums.shape, jnp.float32)
    for index, value in enumerate(pairs):
        tile = jnp.where(row == index, value, tile)
    sums[...] = tile + jnp.where(first, 0.0, sums[...])


def add_pairs(left, right):
    return (left[0] + right[0], left[1] + right[1])


def stacked_step(meta, mine, other, one, two, master, new_one, new_two, update, sums):
    step = pl.program_id(0)
    size = one.shape[2]
    pairs = []
    for side in range(2):
        columns = slice(side * size, (side + 1) * size)
        own = step == meta[0]
        gradient = jnp.where(own, mine[:, columns], other[:, columns]).astype(jnp.float32)
        pairs += step_part(gradient, (side,), (one, two, master), (new_one, new_two, update))
    put_sums(sums, pairs, step == 0)


def turned_step(meta, mine, other, one, two, master, new_one, new_two, update, sums):
    step = pl.program_id(0)
    gradient = jnp.where(step == meta[0], mine[...], other[...]).astype(jnp.float32).T
    pair = step_part(gradient, (slice(None),), (one, two, master), (new_one, new_two, update))
    put_sums(sums, pair, step == 0)


def attn_step(
    meta, mine, other, query_one, query_two, query, keyval_one, keyval_two, keyval,
    output_one, output_two, output, new_query_one, new_query_two, query_update,
    new_keyval_one, new_keyval_two, keyval_update, new_output_one, new_output_two, output_update, sums,
):
    step = pl.program_id(0)
    own = step == meta[0]
    width = query.shape[1]
    key_width = keyval.shape[2]

    def part(first, size):
        columns = slice(first, first + size)
        return jnp.where(own, mine[:, columns], other[:, columns]).astype(jnp.float32)

    whole_span = (slice(None),)
    pairs = []
    pairs += step_part(part(0, width), whole_span, (query_one, query_two, query), (new_query_one, new_query_two, query_update))
    for side in range(2):
        pairs += step_part(
            part(width + side * key_width, key_width), (side,),
            (keyval_one, keyval_two, keyval), (new_keyval_one, new_keyval_two, keyval_update),
        )
    pairs += step_part(
        part(width + 2 * key_width, mine.shape[1] - width - 2 * key_width).T, whole_span,
        (output_one, output_two, output), (new_output_one, new_output_two, output_update),
    )
    put_sums(sums, pairs, step == 0)


def half_block(array, axis):
    shape = tuple(size // 2 if place == axis else size for place, size in enumerate(array.shape))
    return pl.BlockSpec(shape, lambda i, meta: tuple(i if place == axis else 0 for place in range(len(shape))))


def step_call(name, kernel, place, mine, other, arrays, axes):
    own = pl.BlockSpec(other.shape, lambda i, meta: (meta[0], 0))
    fixed = pl.BlockSpec(other.shape, lambda i, meta: (0, 0))
    specs = [half_block(array, axis) for group, axis in zip(arrays, axes) for array in group]
    out_arrays = [(array, axis) for group, axis in zip(arrays, axes) for array in group]
    return pl.pallas_call(
        kernel,
        out_shape=tuple(jax.ShapeDtypeStruct(array.shape, jnp.float32) for array, _ in out_arrays)
        + (jax.ShapeDtypeStruct((8, HD), jnp.float32),),
        grid_spec=pltpu.PrefetchScalarGridSpec(
            num_scalar_prefetch=1,
            grid=(2,),
            in_specs=[own, fixed] + specs,
            out_specs=tuple(half_block(array, axis) for array, axis in out_arrays)
            + (pl.BlockSpec((8, HD), lambda i, meta: (0, 0)),),
        ),
        cost_estimate=LIGHT,
        name=name,
    )(place, mine, other, *[array for group in arrays for array in group])


def ratio_of(weight_square, update_square):
    return jnp.sqrt(weight_square) / jnp.sqrt(update_square)


def apply_kernel(parts, axes, *refs):
    sums = refs[0]
    count = len(parts)
    for place, rows in enumerate(parts):
        update, master = refs[1 + 2 * place : 3 + 2 * place]
        result = refs[1 + 2 * count + place]
        for side, row in enumerate(rows):
            span = (side,) if len(rows) > 1 else (slice(None),)
            trust = ratio_of(sums[row : row + 1, 0:1], sums[row + 1 : row + 2, 0:1])
            result[span] = master[span] - LEARN * trust * update[span]


def apply_call(name, sums, arrays, parts, axes, steps):
    def block(array, axis):
        shape = tuple(size // steps if place == axis else size for place, size in enumerate(array.shape))
        return pl.BlockSpec(shape, lambda i: tuple(i if place == axis else 0 for place in range(len(shape))))

    return pl.pallas_call(
        functools.partial(apply_kernel, parts, axes),
        out_shape=tuple(jax.ShapeDtypeStruct(group[1].shape, jnp.float32) for group in arrays),
        grid=(steps,),
        in_specs=[pl.BlockSpec(sums.shape, lambda i: (0, 0))]
        + [block(array, axis) for group, axis in zip(arrays, axes) for array in group],
        out_specs=tuple(block(group[1], axis) for group, axis in zip(arrays, axes)),
        cost_estimate=LIGHT,
        name=name,
    )(sums, *[array for group in arrays for array in group])


def gains_kernel(rows, sums, first, second, gains, new_first, new_second, new_gains, stats, trust):
    each = (rows - 2) // 2
    new_one, new_two = moments(sums[24 : 24 + rows, :], first[:rows, :], second[:rows, :])
    for row in range(rows):
        new_first[row * HD : (row + 1) * HD] = new_one[row]
        new_second[row * HD : (row + 1) * HD] = new_two[row]
    lane = lax.broadcasted_iota(jnp.int32, (1, HD), 1)
    weight_row = jnp.zeros((1, HD), jnp.float32)
    update_row = jnp.zeros((1, HD), jnp.float32)

    def put(place, weight_square, update_square, weight_row, update_row):
        return (
            jnp.where(lane == place, jnp.sqrt(weight_square), weight_row),
            jnp.where(lane == place, jnp.sqrt(update_square), update_row),
        )

    for place, start, size in ((0, 0, each), (7, each, each), (4, 2 * each, 1), (5, 2 * each + 1, 1)):
        span = slice(start, start + size)
        old = gains[span, :]
        update = update_of(new_one[span, :], new_two[span, :], old)
        weight_square, update_square = (square(old), square(update))
        new_old = old - LEARN * ratio_of(weight_square, update_square) * update
        for row in range(size):
            new_gains[(start + row) * HD : (start + row + 1) * HD] = new_old[row]
        weight_row, update_row = put(place, weight_square, update_square, weight_row, update_row)
    for place, index in ((1, 16), (2, 18), (3, 20), (6, 22), (8, 0), (9, 2), (10, 8)):
        weight_row, update_row = put(
            place, sums[index : index + 1, 0:1], sums[index + 1 : index + 2, 0:1], weight_row, update_row
        )
    stats[0:1, :] = weight_row[:, :11]
    stats[1:2, :] = update_row[:, :11]
    trust[...] = (weight_row / jnp.where(lane < 11, update_row, 1.0))[:, :11]


def root_mean(values):
    return jnp.sqrt(jnp.mean(values * values, -1))


def gather_outer(values):
    return lax.all_gather(values, "outer", axis=0, tiled=True)


def scatter_outer(values):
    return lax.psum_scatter(values, "outer", scatter_dimension=0, tiled=True)


def shards(
    tokens,
    cotangent,
    lengths,
    norm_gains,
    gains_first,
    gains_second,
    query_weight,
    query_first,
    query_second,
    keyval_weight,
    keyval_first,
    keyval_second,
    output_weight,
    output_first,
    output_second,
    gateup_weight,
    gateup_first,
    gateup_second,
    down_weight,
    down_first,
    down_second,
):
    low = jnp.bfloat16
    shard_len = tokens.shape[1]
    narrow_size = lax.axis_size("narrow")
    outer_size = lax.axis_size("outer")
    seq_len = shard_len * narrow_size
    gain_one = norm_gains[:D]
    gain_two = norm_gains[D : 2 * D]
    head_gains = norm_gains[2 * D :].reshape(2, HD)
    cos_table, sin_table = rope_tables(seq_len)

    residual = tokens[0].astype(jnp.float32)
    inv_one = lax.rsqrt(jnp.mean(residual * residual, -1, keepdims=True) + EPS)
    hat_one = residual * inv_one
    normed = (hat_one * gain_one).astype(low)

    query_half = query_weight.shape[1] // 2
    key_half = keyval_weight.shape[2] // 2
    output_half = output_weight.shape[0] // 2
    hidden_size = down_weight.shape[0] // 2
    raw_width = query_half + 2 * key_half
    places = lax.axis_index("narrow") * shard_len + jnp.arange(shard_len, dtype=jnp.int32)
    valid = (places < lengths[0]).astype(jnp.float32)
    grad_out = cotangent[0].astype(jnp.float32) * valid[:, None]
    attn_low = [w.astype(low) for w in (query_weight, keyval_weight[0], keyval_weight[1])]
    mine, theirs = pair_weights(attn_low + [output_weight.astype(low).T])
    full_attn = gather_weights(mine, swap(theirs, PAIR))

    chip, pair = named("norm_one", gather_start, normed)
    gateup_mine, gateup_theirs = pair_weights(
        [gateup_weight[0].astype(low), gateup_weight[1].astype(low), down_weight.astype(low).T]
    )
    meta = jnp.concatenate(
        [lax.axis_index("narrow").astype(jnp.int32)[None], lengths, swap(lengths, PAIR)]
    )
    chip, pair, gateup_theirs, cos_table, sin_table, meta, head_gains = together(
        chip, pair, gateup_theirs, cos_table, sin_table, meta, head_gains
    )
    (cross,) = named("norm_one", gather_cross, chip, pair, False)
    gateup_pair = in_order(gateup_mine, swap(gateup_theirs, PAIR), 0)
    full_attn, grad_low = together(full_attn, grad_out.astype(low))
    cross, gateup_pair = together(cross, gateup_pair)
    full_gateup = gather_outer(gateup_pair[:, : 2 * hidden_size])
    full_down = gather_outer(gateup_pair[:, 2 * hidden_size :])
    grad_chip, grad_pair = named("output_grad", gather_start, grad_low)
    pieces_one = named("norm_one", gather_end, (normed, chip, pair, cross))
    raw, whole_one = rows_call(
        "query_key_value", plain_finish, pieces_one, [full_attn], [raw_width], [jnp.float32], raw_width
    )
    context = attend_forward(meta, raw, head_gains, cos_table, sin_table)
    context, grad_chip, grad_pair = together(context, grad_chip, grad_pair)

    cross, near, far = named(
        "attention_out", partial_rows, context, full_attn, output_half, raw_width // output_half
    )
    moved = named("attention_out", scatter_cross, cross)
    near, far[0], from_pair, from_chip = together(near, far[0], *moved)
    chip, pair = named("attention_out", near_sums, near, far, from_pair, from_chip)
    chip, pair = named("attention_out", scatter_near, chip, pair)
    attn_part = all_sums(near, far, chip, pair)
    middle = residual + attn_part
    inv_two = lax.rsqrt(jnp.mean(middle * middle, -1, keepdims=True) + EPS)
    hat_two = middle * inv_two
    normed = (hat_two * gain_two).astype(low)
    chip, pair = named("norm_two", gather_start, normed)
    cross = named("norm_two", gather_cross, chip, pair, True)
    *cross, grad_chip, grad_pair = together(*cross, grad_chip, grad_pair)
    pieces_two = named("norm_two", gather_end, (normed, chip, pair, *cross))
    grad_cross = named("output_grad", gather_cross, grad_chip, grad_pair, True)
    both, hidden, whole_two = rows_call(
        "gate_up", gate_finish, pieces_two, [full_gateup], [2 * hidden_size, hidden_size], [low, low],
    )
    hidden, *grad_cross = together(hidden, *grad_cross)
    whole_grad = join(
        named("output_grad", gather_end, (grad_low, grad_chip, grad_pair, *grad_cross))
    )
    down_grad = product_first("down_weight_grad", (whole_grad, hidden))
    full_down, down_grad = together(full_down, down_grad)
    down_own = scatter_outer(down_grad)
    pair_grad = blocks_call(
        "hidden_grad", hidden_finish, whole_grad, full_down, [both], 2 * hidden_size, shard_len
    )
    cross, near, far = named("norm_two_grad", partial_rows, pair_grad, full_gateup, 2 * hidden_size)
    moved = named("norm_two_grad", scatter_cross, cross)
    near, far[0], from_pair, from_chip = together(near, far[0], *moved)
    chip, pair = named("norm_two_grad", near_sums, near, far, from_pair, from_chip)
    chip, pair, pair_grad = together(chip, pair, pair_grad)
    chip, pair = named("norm_two_grad", scatter_near, chip, pair)
    gateup_grad = product_first(
        "gateup_weight_grad",
        (whole_two, pair_grad),
        cost=pl.CostEstimate(
            flops=2 * whole_two.size * pair_grad.shape[1], transcendentals=0, bytes_accessed=2 * whole_two.size
        ),
    )
    down_other = pair_rows(down_own)
    chip, pair, down_other, gateup_grad = together(chip, pair, down_other, gateup_grad)
    gateup_own = scatter_outer(gateup_grad)
    normed_two = all_sums(near, far, chip, pair)
    middle_norm, gain_two_grad = norm_back(normed_two, hat_two, inv_two, gain_two)
    middle_grad = grad_out + middle_norm
    middle_low, down_other = together(middle_grad.astype(low), swap(down_other, PAIR))
    chip, pair = named("middle_grad", gather_start, middle_low)
    cross = named("middle_grad", gather_cross, chip, pair, True)
    hidden, middle_low = together(hidden, middle_low)
    mlp_cross, mlp_near, mlp_far = named("mlp_out", partial_rows, hidden, full_down, hidden_size)
    *cross, mlp_cross, mlp_near = together(*cross, mlp_cross, mlp_near)
    pieces_mid = named("middle_grad", gather_end, (middle_low, chip, pair, *cross))
    context_grad, whole_mid = rows_call(
        "context_grad", plain_finish, pieces_mid, [full_attn], [output_half], [low],
        output_half, raw_width // output_half,
    )
    moved = named("mlp_out", scatter_cross, mlp_cross)
    context_grad, *moved = together(context_grad, *moved)
    mlp_chip, mlp_pair = named("mlp_out", near_sums, mlp_near, mlp_far, *moved)
    context_grad, mlp_chip, mlp_pair = together(context_grad, mlp_chip, mlp_pair)
    mlp_chip, mlp_pair = named("mlp_out", scatter_near, mlp_chip, mlp_pair)
    raw_grad, head_gain_grad = attend_backward(meta, raw, context_grad, head_gains, cos_table, sin_table)
    raw_grad, mlp_chip, mlp_pair = together(raw_grad, mlp_chip, mlp_pair)
    mlp_part = all_sums(mlp_near, mlp_far, mlp_chip, mlp_pair)
    attn_grad = product_first("attention_weight_grad", (whole_one, raw_grad), (whole_mid, context))
    attn_own = scatter_outer(attn_grad)
    gateup_other = swap(pair_rows(gateup_own), PAIR)
    place = lax.axis_index("inner").astype(jnp.int32)[None]
    down = (down_first, down_second, down_weight)
    gateup = (gateup_first, gateup_second, gateup_weight)
    cross, near, far, gateup_other = named(
        "norm_one_grad", partial_rows, raw_grad, full_attn, raw_width, 0, (gateup_other,)
    )
    final = middle + mlp_part
    result = final.astype(low)
    rms_values = jnp.stack([root_mean(attn_part), root_mean(mlp_part), root_mean(final)])[:, None, :]
    moved = named("norm_one_grad", scatter_cross, cross)
    near, far[0], from_pair, from_chip = together(near, far[0], *moved)
    chip, pair = named("norm_one_grad", near_sums, near, far, from_pair, from_chip)
    chip, pair = named("norm_one_grad", scatter_near, chip, pair)
    new_down_first, new_down_second, down_update, down_sums = step_call(
        "down_step", turned_step, place, down_own, down_other, [down], [0]
    )
    new_gateup_first, new_gateup_second, gateup_update, gateup_sums = step_call(
        "gateup_step", stacked_step, place, gateup_own, gateup_other, [gateup], [2]
    )
    attn_own, gain_two_grad = together(attn_own, gain_two_grad)
    attn_other = swap(pair_rows(attn_own), PAIR)
    chip, pair, gateup_sums, down_sums, attn_other, result, rms_values = together(
        chip, pair, gateup_sums, down_sums, attn_other, result, rms_values
    )
    normed_one = all_sums(near, far, chip, pair)
    input_norm, gain_one_grad = norm_back(normed_one, hat_one, inv_one, gain_one)
    input_grad = (middle_grad + input_norm).astype(low)

    attn_arrays = [
        (query_first, query_second, query_weight),
        (keyval_first, keyval_second, keyval_weight),
        (output_first, output_second, output_weight),
    ]
    (
        new_query_first, new_query_second, query_update, new_keyval_first, new_keyval_second,
        keyval_update, new_output_first, new_output_second, output_update, attn_sums,
    ) = step_call("attention_step", attn_step, place, attn_own, attn_other, attn_arrays, [1, 2, 0])
    sums = jnp.concatenate(
        [gateup_sums, down_sums, attn_sums]
        + [gain_one_grad.reshape(-1, HD), gain_two_grad.reshape(-1, HD), head_gain_grad],
        0,
    )
    sums = named("all_sums", total, sums)
    matrix_sums = sums[:24]
    gain_rows = norm_gains.size // HD
    new_query, new_keyval, new_output = apply_call(
        "attention",
        matrix_sums,
        [(query_update, query_weight), (keyval_update, keyval_weight), (output_update, output_weight)],
        ((16,), (18, 20), (22,)),
        (0, 1, 0),
        2,
    )
    new_gateup, new_down = apply_call(
        "gateup_down",
        matrix_sums,
        [(gateup_update, gateup_weight), (down_update, down_weight)],
        ((0, 2), (8,)),
        (1, 0),
        4,
    )
    padded = -(-gain_rows // 8) * 8
    gain_shape = jax.ShapeDtypeStruct(norm_gains.shape, jnp.float32)
    new_gains_first, new_gains_second, new_gains, lamb_stats, trust = pl.pallas_call(
        functools.partial(gains_kernel, gain_rows),
        out_shape=(gain_shape, gain_shape, gain_shape)
        + tuple(jax.ShapeDtypeStruct((rows, 11), jnp.float32) for rows in (2, 1)),
        name="gains",
    )(
        sums,
        *[
            jnp.pad(values, (0, (padded - gain_rows) * HD)).reshape(padded, HD)
            for values in (gains_first, gains_second, norm_gains)
        ],
    )
    trust = trust[0]
    return (
        result[None],
        input_grad[None],
        rms_values,
        new_gains,
        new_gains_first,
        new_gains_second,
        new_query,
        new_query_first,
        new_query_second,
        new_keyval,
        new_keyval_first,
        new_keyval_second,
        new_output,
        new_output_first,
        new_output_second,
        new_gateup,
        new_gateup_first,
        new_gateup_second,
        new_down,
        new_down_first,
        new_down_second,
        lamb_stats,
        trust,
    )


def solution(mesh):
    wide_size, narrow_size = mesh.devices.shape
    cube = jax.sharding.Mesh(
        mesh.devices.reshape(wide_size // 2, 2, narrow_size), ("outer", "inner", "narrow")
    )
    wide = ("outer", "inner")
    rows = P(wide, "narrow", None)
    matrix = P(wide, "narrow")
    stacked = P(None, wide, "narrow")
    turned = P("narrow", wide)
    in_specs = (rows, rows, P(wide), P(), P(), P())
    in_specs += (matrix,) * 3 + (stacked,) * 3 + (turned,) * 3 + (stacked,) * 3 + (turned,) * 3
    out_specs = (rows, rows, stacked, P(), P(), P())
    out_specs += (matrix,) * 3 + (stacked,) * 3 + (turned,) * 3 + (stacked,) * 3 + (turned,) * 3
    out_specs += (P(), P())
    return jax.shard_map(shards, mesh=cube, in_specs=in_specs, out_specs=out_specs, check_vma=False)
```
